128 devices in a mesh: gx: 8 (over y, core), gy: 4 (over z), gz: 4 (over x).
Axes of the slice: x: 4, y: 4, z: 4, core: 2. Of those that a mesh axis runs over, the one named last changes fastest.
Arguments:
- right_side: float32 [128, 64, 1024], P('gx', 'gy', 'gz'), may hold values from -8 to 8
- conductance: float32 [3, 128, 64, 1024], P(None, 'gx', 'gy', 'gz'), may hold values from 0.2 to 5
- storage: float32 [128, 64, 1024], P('gx', 'gy', 'gz'), may hold values from 0.05 to 0.8
- dirichlet: int32 [128, 64, 1024], P('gx', 'gy', 'gz'), may hold values 0 or 1
- basis: float32 [16, 128, 64, 1024], P(None, 'gx', 'gy', 'gz'), may hold values from -2 to 2
- coarse_inverse: float32 [2048, 2048], P(('gx', 'gy', 'gz')), may hold values from 0 to 2, as said below
Outputs:
- solution_field: float32 [128, 64, 1024], P('gx', 'gy', 'gz')
- residual: float32 [128, 64, 1024], P('gx', 'gy', 'gz')
The draws below stay inside these ranges and needn't reach their ends.
Inputs may be any that keep to these rules, and one draw needn't show every extreme that they name: `coarse_inverse`: symmetric positive definite.
All inputs are finite; a program needn't handle non-finite values. No bound on the sum of `dirichlet` on one device may be relied on, other than what follows from the above.
Results may differ from the reference program's by a relative error of at most 0.0003.
Values sent between devices are 32-bit elements; how exact they have to be, the bound alone decides.
A program may use at most 128 MiB of HBM per device.

```python
import math
import jax
import jax.numpy as jnp
from jax import lax

CX = 16
CY = 16
CZ = 256
VECS = 16
SWEEPS = 4
ITERS = 2
NX = 128
NY = 64
NZ = 1024
NC = 2048
N_GX = 8
N_GY = 4
N_GZ = 4


def draw_right_side(key, part):
    pos_x = (jnp.arange(NX, dtype=jnp.float32) + 0.5) / NX
    pos_y = (jnp.arange(NY, dtype=jnp.float32) + 0.5) / NY
    pos_z = (jnp.arange(NZ, dtype=jnp.float32) + 0.5) / NZ
    smooth = 1.0 + 0.5 * jnp.sin(2.0 * math.pi * pos_x)[:, None, None] * jnp.cos(math.pi * pos_y)[None, :, None] + 0.3 * jnp.cos(2.0 * math.pi * pos_z)[None, None, :]
    rough = jax.random.truncated_normal(key, -4.0, 4.0, (NX, NY, NZ), jnp.float32)
    return rough + 0.5 * smooth


def draw_basis(key, part):
    local_x = ((jnp.arange(NX) % CX).astype(jnp.float32) + 0.5) / CX
    local_y = ((jnp.arange(NY) % CY).astype(jnp.float32) + 0.5) / CY
    local_z = ((jnp.arange(NZ) % CZ).astype(jnp.float32) + 0.5) / CZ
    order = jnp.arange(VECS)
    first = (order // 8).astype(jnp.float32)
    second = (order // 4 % 2).astype(jnp.float32)
    third = (order % 4).astype(jnp.float32)
    mode = jnp.cos(math.pi * first[:, None, None, None] * local_x[None, :, None, None]) * jnp.cos(math.pi * second[:, None, None, None] * local_y[None, None, :, None]) * jnp.cos(math.pi * third[:, None, None, None] * local_z[None, None, None, :])
    noise = jax.random.uniform(key, (VECS, NX, NY, NZ), jnp.float32, -1.0, 1.0)
    rough = 1.0 + 0.3 * noise
    return mode * rough / math.sqrt(CX * CY * CZ)


def draw_coarse_inverse(key, part):
    key_scale = jax.random.fold_in(key, 11)
    key_diag = jax.random.fold_in(key, 12)
    rows = jnp.arange(NC)
    owner = rows // VECS
    vector = rows % VECS
    sub_x = owner // (N_GY * N_GZ)
    sub_y = owner // N_GZ % N_GY
    sub_z = owner % N_GZ
    reach = 2.0
    scales = jnp.exp(jax.random.uniform(key_scale, (NC,), jnp.float32, math.log(0.3), 0.0))
    gap = jnp.abs(sub_x[:, None] - sub_x[None, :]) + jnp.abs(sub_y[:, None] - sub_y[None, :]) + jnp.abs(sub_z[:, None] - sub_z[None, :])
    spread = jnp.abs(vector[:, None] - vector[None, :])
    kernel = jnp.exp(-gap.astype(jnp.float32) / reach) * jnp.exp(-spread.astype(jnp.float32) / 3.0)
    coupled = 0.06 * scales[:, None] * scales[None, :] * kernel
    diag = 0.5 + jax.random.uniform(key_diag, (NC,), jnp.float32)
    same = rows[:, None] == rows[None, :]
    return coupled + jnp.where(same, diag[:, None], 0.0)


def touch_ends(result, stream_key, low, largest):
    shape = result.shape
    place = [jax.random.randint(jax.random.fold_in(stream_key, axis), (), 0, shape[axis]) for axis in range(len(shape))]
    result = result.at[tuple(place)].set(low)
    longest = shape.index(max(shape))
    place[longest] = (place[longest] + 1) % shape[longest]
    return result.at[tuple(place)].set(largest)


def block_levels(key, dims, cuts, smallest, largest):
    def one(dim, blocks):
        steps = jax.random.uniform(jax.random.fold_in(jax.random.fold_in(key, 6), dim), (blocks,), jnp.float32, smallest / len(cuts), largest / len(cuts))
        return jnp.repeat(jnp.exp(steps), dims[dim] // blocks).reshape((-1,) + (1,) * (len(dims) - dim - 1))

    loudness = one(*cuts[0])
    for cut in cuts[1:]:
        loudness = loudness * one(*cut)
    return loudness


def setup_inputs(seed: int = 0) -> dict:
    key_of = jax.random.split(jax.random.key(seed), 7)
    right_side = draw_right_side(jax.random.fold_in(key_of[6], 71), 0)
    conductance = jnp.clip(jnp.exp(math.log(5.0) - 3.218876 * jax.random.uniform(key_of[1], (3, NX, NY, NZ), jnp.float32) ** block_levels(key_of[1], (3, NX, NY, NZ), ((1, 8), (2, 4), (3, 4)), -0.2, 0.2)), 0.2, 5.0)
    storage = jnp.clip(jnp.exp(math.log(0.8) - 2.7725887 * jax.random.uniform(key_of[2], (NX, NY, NZ), jnp.float32) ** block_levels(key_of[2], (NX, NY, NZ), ((0, 8), (1, 4), (2, 4)), -0.2, 0.2)), 0.05, 0.8)
    dirichlet = touch_ends((jax.random.randint(key_of[3], (NX, NY, NZ), 0, 16) < 1).astype(jnp.int32), jax.random.fold_in(key_of[3], 1), 0, 1)
    basis = draw_basis(jax.random.fold_in(key_of[6], 71), 0)
    coarse_inverse = draw_coarse_inverse(jax.random.fold_in(key_of[6], 71), 0)
    return dict(right_side=right_side, conductance=conductance, storage=storage, dirichlet=dirichlet, basis=basis, coarse_inverse=coarse_inverse)


RELAX = 2.0 / 3.0


def pad_cond(cond):
    return jnp.pad(cond, ((0, 0), (1, 1), (1, 1), (1, 1)))


def stencil(padded_free, padded_cond, field, storage, free):
    middle = padded_free[1:-1, 1:-1, 1:-1]
    total = storage * middle
    total = total + padded_cond[0, 1:-1, 1:-1, 1:-1] * (middle - padded_free[2:, 1:-1, 1:-1]) + padded_cond[0, :-2, 1:-1, 1:-1] * (middle - padded_free[:-2, 1:-1, 1:-1])
    total = total + padded_cond[1, 1:-1, 1:-1, 1:-1] * (middle - padded_free[1:-1, 2:, 1:-1]) + padded_cond[1, 1:-1, :-2, 1:-1] * (middle - padded_free[1:-1, :-2, 1:-1])
    total = total + padded_cond[2, 1:-1, 1:-1, 1:-1] * (middle - padded_free[1:-1, 1:-1, 2:]) + padded_cond[2, 1:-1, 1:-1, :-2] * (middle - padded_free[1:-1, 1:-1, :-2])
    return free * total + (1.0 - free) * field


def diagonal_of(padded_cond, storage, free):
    total = storage + padded_cond[0, 1:-1, 1:-1, 1:-1] + padded_cond[0, :-2, 1:-1, 1:-1]
    total = total + padded_cond[1, 1:-1, 1:-1, 1:-1] + padded_cond[1, 1:-1, :-2, 1:-1]
    total = total + padded_cond[2, 1:-1, 1:-1, 1:-1] + padded_cond[2, 1:-1, 1:-1, :-2]
    return free * total + (1.0 - free)


def jacobi(rhs_box, padded_cond, diagonal, storage_box, free_box):
    guess = jnp.zeros_like(rhs_box)
    for sweep in range(SWEEPS):
        image = stencil(jnp.pad(free_box * guess, 1), padded_cond, guess, storage_box, free_box)
        guess = guess + RELAX * (rhs_box - image) / diagonal
    return guess


def reference(right_side, conductance, storage, dirichlet, basis, coarse_inverse):
    free = 1.0 - dirichlet.astype(jnp.float32)
    cond_pad = pad_cond(conductance)

    def apply(field):
        return stencil(jnp.pad(free * field, 1), cond_pad, field, storage, free)

    cond_two = jnp.pad(conductance, ((0, 0), (2, 2), (2, 2), (2, 2)))
    store_two = jnp.pad(storage, 2)
    free_two = jnp.pad(free, 2)
    count = N_GX * N_GY * N_GZ
    box_shape = (CX + 4, CY + 4, CZ + 4)

    def schwarz(residual):
        rhs_two = jnp.pad(residual, 2)

        def one(index):
            first = (index // (N_GY * N_GZ)) * CX
            second = ((index // N_GZ) % N_GY) * CY
            third = (index % N_GZ) * CZ
            rhs_box = lax.dynamic_slice(rhs_two, (first, second, third), box_shape)
            cond_box = lax.dynamic_slice(cond_two, (jnp.zeros((), jnp.int32), first, second, third), (3,) + box_shape)
            store_box = lax.dynamic_slice(store_two, (first, second, third), box_shape)
            free_box = lax.dynamic_slice(free_two, (first, second, third), box_shape)
            padded = pad_cond(cond_box)
            diagonal = diagonal_of(padded, store_box, free_box)
            return jacobi(rhs_box, padded, diagonal, store_box, free_box)[2:-2, 2:-2, 2:-2]

        blocks = lax.map(one, jnp.arange(count, dtype=jnp.int32))
        return blocks.reshape(N_GX, N_GY, N_GZ, CX, CY, CZ).transpose(0, 3, 1, 4, 2, 5).reshape(NX, NY, NZ)

    basis_six = basis.reshape(VECS, N_GX, CX, N_GY, CY, N_GZ, CZ)

    def coarse(residual):
        res_six = residual.reshape(N_GX, CX, N_GY, CY, N_GZ, CZ)
        parts = jnp.einsum('kaxbycz,axbycz->abck', basis_six, res_six, precision=lax.Precision.HIGHEST).reshape(-1)
        weights = jnp.dot(coarse_inverse, parts, precision=lax.Precision.HIGHEST).reshape(N_GX, N_GY, N_GZ, VECS)
        return jnp.einsum('abck,kaxbycz->axbycz', weights, basis_six, precision=lax.Precision.HIGHEST).reshape(NX, NY, NZ)

    def precondition(residual):
        return schwarz(residual) + coarse(residual)

    solution = jnp.zeros_like(right_side)
    residual = right_side
    precond = precondition(residual)
    norm_now = jnp.sum(residual * precond)
    direction = precond
    for step in range(ITERS):
        image = apply(direction)
        alpha = norm_now / jnp.sum(direction * image)
        solution = solution + alpha * direction
        residual = residual - alpha * image
        if step + 1 < ITERS:
            precond = precondition(residual)
            norm_next = jnp.sum(residual * precond)
            direction = precond + (norm_next / norm_now) * direction
            norm_now = norm_next
    return solution, residual
```

```python
import jax
import jax.numpy as jnp
from jax import lax
from jax.sharding import PartitionSpec as P

SWEEPS = 4
ITERS = 2


RELAX = 2.0 / 3.0


def padded(value, sides, width):
    for axis, dim in sides:
        count, length = (lax.axis_size(axis), value.shape[dim])
        up = [(i, (i + 1) % count) for i in range(count - 1)]
        down = [(j, i) for i, j in up]
        last = lax.slice_in_dim(value, length - width, length, axis=dim)
        leading = lax.slice_in_dim(value, 0, width, axis=dim)
        before = lax.ppermute(last, axis, up)
        after = lax.ppermute(leading, axis, down)
        value = jnp.concatenate([before, value, after], axis=dim)
    return value


def pad_cond(cond):
    return jnp.pad(cond, ((0, 0), (1, 1), (1, 1), (1, 1)))


def stencil(padded_free, padded_cond, field, storage, free):
    middle = padded_free[1:-1, 1:-1, 1:-1]
    total = storage * middle
    total = (
        total
        + padded_cond[0, 1:-1, 1:-1, 1:-1] * (middle - padded_free[2:, 1:-1, 1:-1])
        + padded_cond[0, :-2, 1:-1, 1:-1] * (middle - padded_free[:-2, 1:-1, 1:-1])
    )
    total = (
        total
        + padded_cond[1, 1:-1, 1:-1, 1:-1] * (middle - padded_free[1:-1, 2:, 1:-1])
        + padded_cond[1, 1:-1, :-2, 1:-1] * (middle - padded_free[1:-1, :-2, 1:-1])
    )
    total = (
        total
        + padded_cond[2, 1:-1, 1:-1, 1:-1] * (middle - padded_free[1:-1, 1:-1, 2:])
        + padded_cond[2, 1:-1, 1:-1, :-2] * (middle - padded_free[1:-1, 1:-1, :-2])
    )
    return free * total + (1.0 - free) * field


def diagonal_of(padded_cond, storage, free):
    total = storage + padded_cond[0, 1:-1, 1:-1, 1:-1] + padded_cond[0, :-2, 1:-1, 1:-1]
    total = total + padded_cond[1, 1:-1, 1:-1, 1:-1] + padded_cond[1, 1:-1, :-2, 1:-1]
    total = total + padded_cond[2, 1:-1, 1:-1, 1:-1] + padded_cond[2, 1:-1, 1:-1, :-2]
    return free * total + (1.0 - free)


def jacobi(rhs_box, padded_cond, diagonal, storage_box, free_box):
    guess = jnp.zeros_like(rhs_box)
    for sweep in range(SWEEPS):
        image = stencil(jnp.pad(free_box * guess, 1), padded_cond, guess, storage_box, free_box)
        guess = guess + RELAX * (rhs_box - image) / diagonal
    return guess


def project(basis, field):
    return jnp.dot(
        basis.reshape(basis.shape[0], -1), field.reshape(-1), precision=lax.Precision.HIGHEST
    )


def expand(basis, weights, field):
    return jnp.dot(
        weights, basis.reshape(basis.shape[0], -1), precision=lax.Precision.HIGHEST
    ).reshape(field.shape)


LANES = 128


def residual_rim(field):
    return padded(field, (("gx", 0), ("gy", 1), ("gz", 2)), 2)


def gather_rows(row):
    return lax.all_gather(row, ("gx", "gy", "gz"), axis=0, tiled=True)


def pack(coarse, scalars):
    vecs = coarse.shape[0]
    row = jnp.zeros((LANES,), jnp.float32)
    row = row.at[:vecs].set(coarse)
    if scalars:
        row = row.at[vecs:vecs + len(scalars)].set(jnp.stack(scalars))
    return row[None]


def unpack(rows, vecs, count):
    coarse = rows[:, :vecs].reshape(-1)
    sums = jnp.sum(rows[:, vecs:vecs + count], axis=0)
    return coarse, [sums[i] for i in range(count)]


def shards(right_side, conductance, storage, dirichlet, basis, coarse_inverse):
    vecs = basis.shape[0]
    free = 1.0 - dirichlet.astype(jnp.float32)
    stacked = jnp.concatenate([conductance, storage[None], free[None]], axis=0)
    wide = padded(stacked, (("gx", 1), ("gy", 2), ("gz", 3)), 3)
    cond_face = wide[:3, 2:-2, 2:-2, 2:-2]
    free_face = wide[4, 2:-2, 2:-2, 2:-2]
    cond_box = wide[:3, 1:-1, 1:-1, 1:-1]
    storage_box = wide[3, 1:-1, 1:-1, 1:-1]
    free_box = wide[4, 1:-1, 1:-1, 1:-1]
    box_cond = pad_cond(cond_box)
    box_diag = diagonal_of(box_cond, storage_box, free_box)

    def schwarz(rhs_box):
        return jacobi(rhs_box, box_cond, box_diag, storage_box, free_box)[2:-2, 2:-2, 2:-2]

    def apply(field):
        near = padded(field, (("gx", 0), ("gy", 1), ("gz", 2)), 1)
        return stencil(free_face * near, cond_face, field, storage, free)

    def precondition(residual, coarse_all):
        weights = jnp.dot(coarse_inverse, coarse_all, precision=lax.Precision.HIGHEST)
        return schwarz(residual_rim(residual)) + expand(basis, weights, residual)

    residual0 = right_side
    coarse0 = project(basis, residual0)
    coarse0_all, _ = unpack(gather_rows(pack(coarse0, [])), vecs, 0)
    z0 = precondition(residual0, coarse0_all)
    image0 = apply(z0)
    coarse_img = project(basis, image0)
    rows = gather_rows(pack(coarse_img, [jnp.sum(residual0 * z0), jnp.sum(z0 * image0)]))
    coarse_img_all, (rz0, curve0) = unpack(rows, vecs, 2)
    alpha0 = rz0 / curve0
    solution1 = alpha0 * z0
    residual1 = residual0 - alpha0 * image0
    coarse1_all = coarse0_all - alpha0 * coarse_img_all
    z1 = precondition(residual1, coarse1_all)
    image_z1 = apply(z1)
    local = [
        jnp.sum(residual1 * z1),
        jnp.sum(z1 * image_z1),
        jnp.sum(z1 * image0),
        jnp.sum(z0 * image_z1),
    ]
    _, (rz1, zz, cross_a, cross_b) = unpack(gather_rows(pack(jnp.zeros((0,), jnp.float32), local)), 0, 4)
    beta = rz1 / rz0
    direction1 = z1 + beta * z0
    image1 = image_z1 + beta * image0
    curve1 = zz + beta * (cross_a + cross_b) + beta * beta * curve0
    alpha1 = rz1 / curve1
    solution2 = solution1 + alpha1 * direction1
    residual2 = residual1 - alpha1 * image1
    return (solution2, residual2)


def solution(mesh):
    placed = (
        P("gx", "gy", "gz"),
        P(None, "gx", "gy", "gz"),
        P("gx", "gy", "gz"),
        P("gx", "gy", "gz"),
        P(None, "gx", "gy", "gz"),
        P(("gx", "gy", "gz"), None),
    )
    return jax.shard_map(
        shards,
        mesh=mesh,
        in_specs=placed,
        out_specs=(P("gx", "gy", "gz"), P("gx", "gy", "gz")),
        check_vma=False,
    )
```

```python
import functools

import jax
import jax.numpy as jnp
from jax import lax
from jax.experimental import pallas as pl
from jax.experimental.pallas import tpu as pltpu
from jax.sharding import PartitionSpec as P

MESH_ID = pl.DeviceIdType.MESH

SWEEPS = 4
ITERS = 2


RELAX = 2.0 / 3.0


def padded(value, sides, width):
    for axis, dim in sides:
        count, length = (lax.axis_size(axis), value.shape[dim])
        up = [(i, (i + 1) % count) for i in range(count - 1)]
        down = [(j, i) for i, j in up]
        last = lax.slice_in_dim(value, length - width, length, axis=dim)
        leading = lax.slice_in_dim(value, 0, width, axis=dim)
        before = lax.ppermute(last, axis, up)
        after = lax.ppermute(leading, axis, down)
        value = jnp.concatenate([before, value, after], axis=dim)
    return value


def pad_cond(cond):
    return jnp.pad(cond, ((0, 0), (1, 1), (1, 1), (1, 1)))


def stencil(padded_free, padded_cond, field, storage, free):
    middle = padded_free[1:-1, 1:-1, 1:-1]
    total = storage * middle
    total = (
        total
        + padded_cond[0, 1:-1, 1:-1, 1:-1] * (middle - padded_free[2:, 1:-1, 1:-1])
        + padded_cond[0, :-2, 1:-1, 1:-1] * (middle - padded_free[:-2, 1:-1, 1:-1])
    )
    total = (
        total
        + padded_cond[1, 1:-1, 1:-1, 1:-1] * (middle - padded_free[1:-1, 2:, 1:-1])
        + padded_cond[1, 1:-1, :-2, 1:-1] * (middle - padded_free[1:-1, :-2, 1:-1])
    )
    total = (
        total
        + padded_cond[2, 1:-1, 1:-1, 1:-1] * (middle - padded_free[1:-1, 1:-1, 2:])
        + padded_cond[2, 1:-1, 1:-1, :-2] * (middle - padded_free[1:-1, 1:-1, :-2])
    )
    return free * total + (1.0 - free) * field


def diagonal_of(padded_cond, storage, free):
    total = storage + padded_cond[0, 1:-1, 1:-1, 1:-1] + padded_cond[0, :-2, 1:-1, 1:-1]
    total = total + padded_cond[1, 1:-1, 1:-1, 1:-1] + padded_cond[1, 1:-1, :-2, 1:-1]
    total = total + padded_cond[2, 1:-1, 1:-1, 1:-1] + padded_cond[2, 1:-1, 1:-1, :-2]
    return free * total + (1.0 - free)


def jacobi(rhs_box, padded_cond, diagonal, storage_box, free_box):
    guess = jnp.zeros_like(rhs_box)
    for sweep in range(SWEEPS):
        image = stencil(jnp.pad(free_box * guess, 1), padded_cond, guess, storage_box, free_box)
        guess = guess + RELAX * (rhs_box - image) / diagonal
    return guess


def project(basis, field):
    return jnp.dot(
        basis.reshape(basis.shape[0], -1), field.reshape(-1), precision=lax.Precision.HIGHEST
    )


def expand(basis, weights, field):
    return jnp.dot(
        weights, basis.reshape(basis.shape[0], -1), precision=lax.Precision.HIGHEST
    ).reshape(field.shape)


LANES = 128


def residual_rim(field):
    return padded(field, (("gx", 0), ("gy", 1), ("gz", 2)), 2)


def gather_kernel(sizes, row_ref, out_ref, held, local_sem, send1, recv1, send2, recv2, send3, recv3):
    nx, ny, nz = sizes
    a = lax.axis_index("gx")
    b = lax.axis_index("gy")
    c = lax.axis_index("gz")
    me = (a * ny + b) * nz + c

    def along_z(k):
        return (a, b, lax.rem(c + k, nz))

    def along_y(k):
        return (a, lax.rem(b + k, ny), c)

    def along_x(k):
        return (lax.rem(a + k, nx), b, c)

    peers = [along_z(k) for k in range(1, nz)]
    peers += [along_y(k) for k in range(1, ny)]
    peers += [along_x(k) for k in range(1, nx)]
    barrier = pltpu.get_barrier_semaphore()
    for peer in peers:
        pl.semaphore_signal(barrier, inc=1, device_id=peer, device_id_type=MESH_ID)
    pl.semaphore_wait(barrier, len(peers))

    own = pltpu.make_async_copy(row_ref, held.at[pl.ds(me, 1)], local_sem.at[0])
    own.start()
    sent = []

    def stage(src_of, first_of, count, size, toward, send, recv):
        for k in range(1, size):
            copy = pltpu.make_async_remote_copy(
                src_ref=src_of(0),
                dst_ref=held.at[pl.ds(first_of(0), count)],
                send_sem=send.at[k],
                recv_sem=recv.at[k],
                device_id=toward(k),
                device_id_type=MESH_ID,
            )
            copy.start()
            sent.append(copy)
        for k in range(1, size):
            pltpu.make_async_remote_copy(
                src_ref=src_of(k),
                dst_ref=held.at[pl.ds(first_of(k), count)],
                send_sem=send.at[k],
                recv_sem=recv.at[k],
                device_id=toward(size - k),
                device_id_type=MESH_ID,
            ).wait_recv()

    z_first = lambda k: (a * ny + b) * nz + lax.rem(c + nz - k, nz)
    stage(lambda k: row_ref, z_first, 1, nz, along_z, send1, recv1)
    own.wait()
    y_first = lambda k: (a * ny + lax.rem(b + ny - k, ny)) * nz
    stage(lambda k: held.at[pl.ds(y_first(k), nz)], y_first, nz, ny, along_y, send2, recv2)
    x_first = lambda k: lax.rem(a + nx - k, nx) * ny * nz
    stage(lambda k: held.at[pl.ds(x_first(k), ny * nz)], x_first, ny * nz, nx, along_x, send3, recv3)
    for copy in sent:
        copy.wait_send()
    final = pltpu.make_async_copy(held, out_ref, local_sem.at[1])
    final.start()
    final.wait()


def gather_rows(row):
    sizes = (lax.axis_size("gx"), lax.axis_size("gy"), lax.axis_size("gz"))
    count = sizes[0] * sizes[1] * sizes[2]
    tile = jnp.zeros((1, 8, LANES), jnp.float32).at[0, 0].set(row[0])
    rows = pl.pallas_call(
        functools.partial(gather_kernel, sizes),
        out_shape=jax.ShapeDtypeStruct((count, 8, LANES), jnp.float32),
        in_specs=[pl.BlockSpec(memory_space=pltpu.VMEM)],
        out_specs=pl.BlockSpec(memory_space=pltpu.VMEM),
        scratch_shapes=[
            pltpu.VMEM((count, 8, LANES), jnp.float32),
            pltpu.SemaphoreType.DMA((2,)),
            pltpu.SemaphoreType.DMA((sizes[2],)),
            pltpu.SemaphoreType.DMA((sizes[2],)),
            pltpu.SemaphoreType.DMA((sizes[1],)),
            pltpu.SemaphoreType.DMA((sizes[1],)),
            pltpu.SemaphoreType.DMA((sizes[0],)),
            pltpu.SemaphoreType.DMA((sizes[0],)),
        ],
        compiler_params=pltpu.CompilerParams(collective_id=0, has_side_effects=True),
    )(tile)
    return rows[:, 0, :]


def pack(coarse, scalars):
    vecs = coarse.shape[0]
    row = jnp.zeros((LANES,), jnp.float32)
    row = row.at[:vecs].set(coarse)
    if scalars:
        row = row.at[vecs:vecs + len(scalars)].set(jnp.stack(scalars))
    return row[None]


def unpack(rows, vecs, count):
    coarse = rows[:, :vecs].reshape(-1)
    sums = jnp.sum(rows[:, vecs:vecs + count], axis=0)
    return coarse, [sums[i] for i in range(count)]


def shards(right_side, conductance, storage, dirichlet, basis, coarse_inverse):
    vecs = basis.shape[0]
    free = 1.0 - dirichlet.astype(jnp.float32)
    stacked = jnp.concatenate([conductance, storage[None], free[None]], axis=0)
    wide = padded(stacked, (("gx", 1), ("gy", 2), ("gz", 3)), 3)
    cond_face = wide[:3, 2:-2, 2:-2, 2:-2]
    free_face = wide[4, 2:-2, 2:-2, 2:-2]
    cond_box = wide[:3, 1:-1, 1:-1, 1:-1]
    storage_box = wide[3, 1:-1, 1:-1, 1:-1]
    free_box = wide[4, 1:-1, 1:-1, 1:-1]
    box_cond = pad_cond(cond_box)
    box_diag = diagonal_of(box_cond, storage_box, free_box)

    def schwarz(rhs_box):
        return jacobi(rhs_box, box_cond, box_diag, storage_box, free_box)[2:-2, 2:-2, 2:-2]

    def apply(field):
        near = padded(field, (("gx", 0), ("gy", 1), ("gz", 2)), 1)
        return stencil(free_face * near, cond_face, field, storage, free)

    def precondition(residual, coarse_all):
        weights = jnp.dot(coarse_inverse, coarse_all, precision=lax.Precision.HIGHEST)
        return schwarz(residual_rim(residual)) + expand(basis, weights, residual)

    residual0 = right_side
    coarse0 = project(basis, residual0)
    coarse0_all, _ = unpack(gather_rows(pack(coarse0, [])), vecs, 0)
    z0 = precondition(residual0, coarse0_all)
    image0 = apply(z0)
    coarse_img = project(basis, image0)
    rows = gather_rows(pack(coarse_img, [jnp.sum(residual0 * z0), jnp.sum(z0 * image0)]))
    coarse_img_all, (rz0, curve0) = unpack(rows, vecs, 2)
    alpha0 = rz0 / curve0
    solution1 = alpha0 * z0
    residual1 = residual0 - alpha0 * image0
    coarse1_all = coarse0_all - alpha0 * coarse_img_all
    z1 = precondition(residual1, coarse1_all)
    image_z1 = apply(z1)
    local = [
        jnp.sum(residual1 * z1),
        jnp.sum(z1 * image_z1),
        jnp.sum(z1 * image0),
        jnp.sum(z0 * image_z1),
    ]
    _, (rz1, zz, cross_a, cross_b) = unpack(gather_rows(pack(jnp.zeros((0,), jnp.float32), local)), 0, 4)
    beta = rz1 / rz0
    direction1 = z1 + beta * z0
    image1 = image_z1 + beta * image0
    curve1 = zz + beta * (cross_a + cross_b) + beta * beta * curve0
    alpha1 = rz1 / curve1
    solution2 = solution1 + alpha1 * direction1
    residual2 = residual1 - alpha1 * image1
    return (solution2, residual2)


def solution(mesh):
    placed = (
        P("gx", "gy", "gz"),
        P(None, "gx", "gy", "gz"),
        P("gx", "gy", "gz"),
        P("gx", "gy", "gz"),
        P(None, "gx", "gy", "gz"),
        P(("gx", "gy", "gz"), None),
    )
    return jax.shard_map(
        shards,
        mesh=mesh,
        in_specs=placed,
        out_specs=(P("gx", "gy", "gz"), P("gx", "gy", "gz")),
        check_vma=False,
    )
```

```python
import functools

import jax
import jax.numpy as jnp
from jax import lax
from jax.experimental import pallas as pl
from jax.experimental.pallas import tpu as pltpu
from jax.sharding import PartitionSpec as P

MESH_ID = pl.DeviceIdType.MESH

SWEEPS = 4
ITERS = 2


RELAX = 2.0 / 3.0


def padded(value, sides, width):
    for axis, dim in sides:
        count, length = (lax.axis_size(axis), value.shape[dim])
        up = [(i, (i + 1) % count) for i in range(count - 1)]
        down = [(j, i) for i, j in up]
        last = lax.slice_in_dim(value, length - width, length, axis=dim)
        leading = lax.slice_in_dim(value, 0, width, axis=dim)
        before = lax.ppermute(last, axis, up)
        after = lax.ppermute(leading, axis, down)
        value = jnp.concatenate([before, value, after], axis=dim)
    return value


def pad_cond(cond):
    return jnp.pad(cond, ((0, 0), (1, 1), (1, 1), (1, 1)))


def stencil(padded_free, padded_cond, field, storage, free):
    middle = padded_free[1:-1, 1:-1, 1:-1]
    total = storage * middle
    total = (
        total
        + padded_cond[0, 1:-1, 1:-1, 1:-1] * (middle - padded_free[2:, 1:-1, 1:-1])
        + padded_cond[0, :-2, 1:-1, 1:-1] * (middle - padded_free[:-2, 1:-1, 1:-1])
    )
    total = (
        total
        + padded_cond[1, 1:-1, 1:-1, 1:-1] * (middle - padded_free[1:-1, 2:, 1:-1])
        + padded_cond[1, 1:-1, :-2, 1:-1] * (middle - padded_free[1:-1, :-2, 1:-1])
    )
    total = (
        total
        + padded_cond[2, 1:-1, 1:-1, 1:-1] * (middle - padded_free[1:-1, 1:-1, 2:])
        + padded_cond[2, 1:-1, 1:-1, :-2] * (middle - padded_free[1:-1, 1:-1, :-2])
    )
    return free * total + (1.0 - free) * field


def diagonal_of(padded_cond, storage, free):
    total = storage + padded_cond[0, 1:-1, 1:-1, 1:-1] + padded_cond[0, :-2, 1:-1, 1:-1]
    total = total + padded_cond[1, 1:-1, 1:-1, 1:-1] + padded_cond[1, 1:-1, :-2, 1:-1]
    total = total + padded_cond[2, 1:-1, 1:-1, 1:-1] + padded_cond[2, 1:-1, 1:-1, :-2]
    return free * total + (1.0 - free)


def jacobi(rhs_box, padded_cond, diagonal, storage_box, free_box):
    guess = jnp.zeros_like(rhs_box)
    for sweep in range(SWEEPS):
        image = stencil(jnp.pad(free_box * guess, 1), padded_cond, guess, storage_box, free_box)
        guess = guess + RELAX * (rhs_box - image) / diagonal
    return guess


def project(basis, field):
    return jnp.dot(
        basis.reshape(basis.shape[0], -1), field.reshape(-1), precision=lax.Precision.HIGHEST
    )


def expand(basis, weights, field):
    return jnp.dot(
        weights, basis.reshape(basis.shape[0], -1), precision=lax.Precision.HIGHEST
    ).reshape(field.shape)


LANES = 128


def residual_rim(field):
    return padded(field, (("gx", 0), ("gy", 1), ("gz", 2)), 2)


def gather_kernel(sizes, row_ref, out_ref, held, local_sem, send1, recv1, send2, recv2, send3, recv3):
    nx, ny, nz = sizes
    a = lax.axis_index("gx")
    b = lax.axis_index("gy")
    c = lax.axis_index("gz")
    me = (a * ny + b) * nz + c

    def along_z(k):
        return (a, b, lax.rem(c + k, nz))

    def along_y(k):
        return (a, lax.rem(b + k, ny), c)

    def along_x(k):
        return (lax.rem(a + k, nx), b, c)

    peers = [along_z(k) for k in range(1, nz)]
    peers += [along_y(k) for k in range(1, ny)]
    peers += [along_x(k) for k in range(1, nx)]
    barrier = pltpu.get_barrier_semaphore()
    for peer in peers:
        pl.semaphore_signal(barrier, inc=1, device_id=peer, device_id_type=MESH_ID)
    pl.semaphore_wait(barrier, len(peers))

    own = pltpu.make_async_copy(row_ref, held.at[pl.ds(me, 1)], local_sem.at[0])
    own.start()
    sent = []

    def stage(src_of, first_of, count, size, toward, send, recv):
        for k in range(1, size):
            copy = pltpu.make_async_remote_copy(
                src_ref=src_of(0),
                dst_ref=held.at[pl.ds(first_of(0), count)],
                send_sem=send.at[k],
                recv_sem=recv.at[k],
                device_id=toward(k),
                device_id_type=MESH_ID,
            )
            copy.start()
            sent.append(copy)
        for k in range(1, size):
            pltpu.make_async_remote_copy(
                src_ref=src_of(k),
                dst_ref=held.at[pl.ds(first_of(k), count)],
                send_sem=send.at[k],
                recv_sem=recv.at[k],
                device_id=toward(size - k),
                device_id_type=MESH_ID,
            ).wait_recv()

    z_first = lambda k: (a * ny + b) * nz + lax.rem(c + nz - k, nz)
    stage(lambda k: row_ref, z_first, 1, nz, along_z, send1, recv1)
    own.wait()
    y_first = lambda k: (a * ny + lax.rem(b + ny - k, ny)) * nz
    stage(lambda k: held.at[pl.ds(y_first(k), nz)], y_first, nz, ny, along_y, send2, recv2)
    x_first = lambda k: lax.rem(a + nx - k, nx) * ny * nz
    stage(lambda k: held.at[pl.ds(x_first(k), ny * nz)], x_first, ny * nz, nx, along_x, send3, recv3)
    for copy in sent:
        copy.wait_send()
    final = pltpu.make_async_copy(held, out_ref, local_sem.at[1])
    final.start()
    final.wait()


def gather_rows(row):
    sizes = (lax.axis_size("gx"), lax.axis_size("gy"), lax.axis_size("gz"))
    count = sizes[0] * sizes[1] * sizes[2]
    tile = jnp.zeros((1, 8, LANES), jnp.float32).at[0, 0].set(row[0])
    rows = pl.pallas_call(
        functools.partial(gather_kernel, sizes),
        out_shape=jax.ShapeDtypeStruct((count, 8, LANES), jnp.float32),
        in_specs=[pl.BlockSpec(memory_space=pltpu.VMEM)],
        out_specs=pl.BlockSpec(memory_space=pltpu.VMEM),
        scratch_shapes=[
            pltpu.VMEM((count, 8, LANES), jnp.float32),
            pltpu.SemaphoreType.DMA((2,)),
            pltpu.SemaphoreType.DMA((sizes[2],)),
            pltpu.SemaphoreType.DMA((sizes[2],)),
            pltpu.SemaphoreType.DMA((sizes[1],)),
            pltpu.SemaphoreType.DMA((sizes[1],)),
            pltpu.SemaphoreType.DMA((sizes[0],)),
            pltpu.SemaphoreType.DMA((sizes[0],)),
        ],
        compiler_params=pltpu.CompilerParams(collective_id=0, has_side_effects=True),
    )(tile)
    return rows[:, 0, :]


def pack(coarse, scalars):
    vecs = coarse.shape[0]
    row = jnp.zeros((LANES,), jnp.float32)
    row = row.at[:vecs].set(coarse)
    if scalars:
        row = row.at[vecs:vecs + len(scalars)].set(jnp.stack(scalars))
    return row[None]


def unpack(rows, vecs, count):
    coarse = rows[:, :vecs].reshape(-1)
    sums = jnp.sum(rows[:, vecs:vecs + count], axis=0)
    return coarse, [sums[i] for i in range(count)]


def shards(right_side, conductance, storage, dirichlet, basis, coarse_inverse):
    vecs = basis.shape[0]
    sides = (("gx", 0), ("gy", 1), ("gz", 2))
    free = 1.0 - dirichlet.astype(jnp.float32)
    stacked = jnp.concatenate([conductance, storage[None], free[None], right_side[None]], axis=0)
    wide = padded(stacked, (("gx", 1), ("gy", 2), ("gz", 3)), 3)
    cond_wide = wide[:3]
    free_wide = wide[4]
    storage_wide = wide[3]
    cond_box = wide[:3, 1:-1, 1:-1, 1:-1]
    storage_box = wide[3, 1:-1, 1:-1, 1:-1]
    free_box = wide[4, 1:-1, 1:-1, 1:-1]
    rhs_box0 = wide[5, 1:-1, 1:-1, 1:-1]
    box_cond = pad_cond(cond_box)
    box_diag = diagonal_of(box_cond, storage_box, free_box)
    cond_face = wide[:3, 2:-2, 2:-2, 2:-2]
    free_face = wide[4, 2:-2, 2:-2, 2:-2]

    def schwarz(rhs_box):
        return jacobi(rhs_box, box_cond, box_diag, storage_box, free_box)[2:-2, 2:-2, 2:-2]

    def precondition(rhs_box, residual, coarse_all):
        weights = jnp.dot(coarse_inverse, coarse_all, precision=lax.Precision.HIGHEST)
        return schwarz(rhs_box) + expand(basis, weights, residual)

    residual0 = right_side
    coarse0 = project(basis, residual0)
    coarse0_all, _ = unpack(gather_rows(pack(coarse0, [])), vecs, 0)
    z0 = precondition(rhs_box0, residual0, coarse0_all)
    near0 = padded(z0, sides, 3)
    inner = (slice(1, -1),) * 3
    image0_box = stencil(free_wide * near0, cond_wide, near0[inner], storage_wide[inner], free_wide[inner])
    image0 = image0_box[2:-2, 2:-2, 2:-2]
    coarse_img = project(basis, image0)
    rows = gather_rows(pack(coarse_img, [jnp.sum(residual0 * z0), jnp.sum(z0 * image0)]))
    coarse_img_all, (rz0, curve0) = unpack(rows, vecs, 2)
    alpha0 = rz0 / curve0
    solution1 = alpha0 * z0
    rhs_box1 = rhs_box0 - alpha0 * image0_box
    residual1 = rhs_box1[2:-2, 2:-2, 2:-2]
    coarse1_all = coarse0_all - alpha0 * coarse_img_all
    z1 = precondition(rhs_box1, residual1, coarse1_all)
    near1 = padded(z1, sides, 1)
    image_z1 = stencil(free_face * near1, cond_face, z1, storage, free)
    local = [
        jnp.sum(residual1 * z1),
        jnp.sum(z1 * image_z1),
        jnp.sum(z1 * image0),
        jnp.sum(z0 * image_z1),
    ]
    _, (rz1, zz, cross_a, cross_b) = unpack(gather_rows(pack(jnp.zeros((0,), jnp.float32), local)), 0, 4)
    beta = rz1 / rz0
    direction1 = z1 + beta * z0
    image1 = image_z1 + beta * image0
    curve1 = zz + beta * (cross_a + cross_b) + beta * beta * curve0
    alpha1 = rz1 / curve1
    solution2 = solution1 + alpha1 * direction1
    residual2 = residual1 - alpha1 * image1
    return (solution2, residual2)


def solution(mesh):
    placed = (
        P("gx", "gy", "gz"),
        P(None, "gx", "gy", "gz"),
        P("gx", "gy", "gz"),
        P("gx", "gy", "gz"),
        P(None, "gx", "gy", "gz"),
        P(("gx", "gy", "gz"), None),
    )
    return jax.shard_map(
        shards,
        mesh=mesh,
        in_specs=placed,
        out_specs=(P("gx", "gy", "gz"), P("gx", "gy", "gz")),
        check_vma=False,
    )
```

```python
import functools

import jax
import jax.numpy as jnp
from jax import lax
from jax.experimental import pallas as pl
from jax.experimental.pallas import tpu as pltpu
from jax.sharding import PartitionSpec as P

MESH_ID = pl.DeviceIdType.MESH

SWEEPS = 4
ITERS = 2


RELAX = 2.0 / 3.0


def padded(value, sides, width):
    for axis, dim in sides:
        count, length = (lax.axis_size(axis), value.shape[dim])
        up = [(i, (i + 1) % count) for i in range(count - 1)]
        down = [(j, i) for i, j in up]
        last = lax.slice_in_dim(value, length - width, length, axis=dim)
        leading = lax.slice_in_dim(value, 0, width, axis=dim)
        before = lax.ppermute(last, axis, up)
        after = lax.ppermute(leading, axis, down)
        value = jnp.concatenate([before, value, after], axis=dim)
    return value


def pad_cond(cond):
    return jnp.pad(cond, ((0, 0), (1, 1), (1, 1), (1, 1)))


def stencil(padded_free, padded_cond, field, storage, free):
    middle = padded_free[1:-1, 1:-1, 1:-1]
    total = storage * middle
    total = (
        total
        + padded_cond[0, 1:-1, 1:-1, 1:-1] * (middle - padded_free[2:, 1:-1, 1:-1])
        + padded_cond[0, :-2, 1:-1, 1:-1] * (middle - padded_free[:-2, 1:-1, 1:-1])
    )
    total = (
        total
        + padded_cond[1, 1:-1, 1:-1, 1:-1] * (middle - padded_free[1:-1, 2:, 1:-1])
        + padded_cond[1, 1:-1, :-2, 1:-1] * (middle - padded_free[1:-1, :-2, 1:-1])
    )
    total = (
        total
        + padded_cond[2, 1:-1, 1:-1, 1:-1] * (middle - padded_free[1:-1, 1:-1, 2:])
        + padded_cond[2, 1:-1, 1:-1, :-2] * (middle - padded_free[1:-1, 1:-1, :-2])
    )
    return free * total + (1.0 - free) * field


def diagonal_of(padded_cond, storage, free):
    total = storage + padded_cond[0, 1:-1, 1:-1, 1:-1] + padded_cond[0, :-2, 1:-1, 1:-1]
    total = total + padded_cond[1, 1:-1, 1:-1, 1:-1] + padded_cond[1, 1:-1, :-2, 1:-1]
    total = total + padded_cond[2, 1:-1, 1:-1, 1:-1] + padded_cond[2, 1:-1, 1:-1, :-2]
    return free * total + (1.0 - free)


def jacobi(rhs_box, padded_cond, diagonal, storage_box, free_box):
    guess = jnp.zeros_like(rhs_box)
    for sweep in range(SWEEPS):
        image = stencil(jnp.pad(free_box * guess, 1), padded_cond, guess, storage_box, free_box)
        guess = guess + RELAX * (rhs_box - image) / diagonal
    return guess


def project(basis, field):
    return jnp.dot(
        basis.reshape(basis.shape[0], -1), field.reshape(-1), precision=lax.Precision.HIGHEST
    )


def expand(basis, weights, field):
    return jnp.dot(
        weights, basis.reshape(basis.shape[0], -1), precision=lax.Precision.HIGHEST
    ).reshape(field.shape)


LANES = 128


def residual_rim(field):
    return padded(field, (("gx", 0), ("gy", 1), ("gz", 2)), 2)


def gather_kernel(sizes, row_ref, out_ref, held, local_sem, send1, recv1, send2, recv2, send3, recv3):
    nx, ny, nz = sizes
    a = lax.axis_index("gx")
    b = lax.axis_index("gy")
    c = lax.axis_index("gz")
    me = (a * ny + b) * nz + c

    def along_z(k):
        return (a, b, lax.rem(c + k, nz))

    def along_y(k):
        return (a, lax.rem(b + k, ny), c)

    def along_x(k):
        return (lax.rem(a + k, nx), b, c)

    peers = [along_z(k) for k in range(1, nz)]
    peers += [along_y(k) for k in range(1, ny)]
    peers += [along_x(k) for k in range(1, nx)]
    barrier = pltpu.get_barrier_semaphore()
    for peer in peers:
        pl.semaphore_signal(barrier, inc=1, device_id=peer, device_id_type=MESH_ID)
    pl.semaphore_wait(barrier, len(peers))

    own = pltpu.make_async_copy(row_ref, held.at[pl.ds(me, 1)], local_sem.at[0])
    own.start()
    sent = []

    def stage(src_of, first_of, count, size, toward, send, recv):
        for k in range(1, size):
            copy = pltpu.make_async_remote_copy(
                src_ref=src_of(0),
                dst_ref=held.at[pl.ds(first_of(0), count)],
                send_sem=send.at[k],
                recv_sem=recv.at[k],
                device_id=toward(k),
                device_id_type=MESH_ID,
            )
            copy.start()
            sent.append(copy)
        for k in range(1, size):
            pltpu.make_async_remote_copy(
                src_ref=src_of(k),
                dst_ref=held.at[pl.ds(first_of(k), count)],
                send_sem=send.at[k],
                recv_sem=recv.at[k],
                device_id=toward(size - k),
                device_id_type=MESH_ID,
            ).wait_recv()

    z_first = lambda k: (a * ny + b) * nz + lax.rem(c + nz - k, nz)
    stage(lambda k: row_ref, z_first, 1, nz, along_z, send1, recv1)
    own.wait()
    y_first = lambda k: (a * ny + lax.rem(b + ny - k, ny)) * nz
    stage(lambda k: held.at[pl.ds(y_first(k), nz)], y_first, nz, ny, along_y, send2, recv2)
    x_first = lambda k: lax.rem(a + nx - k, nx) * ny * nz
    stage(lambda k: held.at[pl.ds(x_first(k), ny * nz)], x_first, ny * nz, nx, along_x, send3, recv3)
    for copy in sent:
        copy.wait_send()
    final = pltpu.make_async_copy(held, out_ref, local_sem.at[1])
    final.start()
    final.wait()


def gather_rows(row):
    sizes = (lax.axis_size("gx"), lax.axis_size("gy"), lax.axis_size("gz"))
    count = sizes[0] * sizes[1] * sizes[2]
    tile = row[:, None, :]
    rows = pl.pallas_call(
        functools.partial(gather_kernel, sizes),
        out_shape=jax.ShapeDtypeStruct((count, 1, LANES), jnp.float32),
        in_specs=[pl.BlockSpec(memory_space=pltpu.VMEM)],
        out_specs=pl.BlockSpec(memory_space=pltpu.VMEM),
        scratch_shapes=[
            pltpu.VMEM((count, 1, LANES), jnp.float32),
            pltpu.SemaphoreType.DMA((2,)),
            pltpu.SemaphoreType.DMA((sizes[2],)),
            pltpu.SemaphoreType.DMA((sizes[2],)),
            pltpu.SemaphoreType.DMA((sizes[1],)),
            pltpu.SemaphoreType.DMA((sizes[1],)),
            pltpu.SemaphoreType.DMA((sizes[0],)),
            pltpu.SemaphoreType.DMA((sizes[0],)),
        ],
        compiler_params=pltpu.CompilerParams(collective_id=0, has_side_effects=True),
    )(tile)
    return rows[:, 0, :]


def pack(coarse, scalars):
    vecs = coarse.shape[0]
    row = jnp.zeros((LANES,), jnp.float32)
    row = row.at[:vecs].set(coarse)
    if scalars:
        row = row.at[vecs:vecs + len(scalars)].set(jnp.stack(scalars))
    return row[None]


def unpack(rows, vecs, count):
    coarse = rows[:, :vecs].reshape(-1)
    sums = jnp.sum(rows[:, vecs:vecs + count], axis=0)
    return coarse, [sums[i] for i in range(count)]


def shards(right_side, conductance, storage, dirichlet, basis, coarse_inverse):
    vecs = basis.shape[0]
    sides = (("gx", 0), ("gy", 1), ("gz", 2))
    free = 1.0 - dirichlet.astype(jnp.float32)
    stacked = jnp.concatenate([conductance, storage[None], free[None], right_side[None]], axis=0)
    wide = padded(stacked, (("gx", 1), ("gy", 2), ("gz", 3)), 3)
    cond_wide = wide[:3]
    free_wide = wide[4]
    storage_wide = wide[3]
    cond_box = wide[:3, 1:-1, 1:-1, 1:-1]
    storage_box = wide[3, 1:-1, 1:-1, 1:-1]
    free_box = wide[4, 1:-1, 1:-1, 1:-1]
    rhs_box0 = wide[5, 1:-1, 1:-1, 1:-1]
    box_cond = pad_cond(cond_box)
    box_diag = diagonal_of(box_cond, storage_box, free_box)
    cond_face = wide[:3, 2:-2, 2:-2, 2:-2]
    free_face = wide[4, 2:-2, 2:-2, 2:-2]

    def schwarz(rhs_box):
        return jacobi(rhs_box, box_cond, box_diag, storage_box, free_box)[2:-2, 2:-2, 2:-2]

    def precondition(rhs_box, residual, coarse_all):
        weights = jnp.dot(coarse_inverse, coarse_all, precision=lax.Precision.HIGHEST)
        return schwarz(rhs_box) + expand(basis, weights, residual)

    residual0 = right_side
    coarse0 = project(basis, residual0)
    coarse0_all, _ = unpack(gather_rows(pack(coarse0, [])), vecs, 0)
    z0 = precondition(rhs_box0, residual0, coarse0_all)
    near0 = padded(z0, sides, 3)
    inner = (slice(1, -1),) * 3
    image0_box = stencil(free_wide * near0, cond_wide, near0[inner], storage_wide[inner], free_wide[inner])
    image0 = image0_box[2:-2, 2:-2, 2:-2]
    coarse_img = project(basis, image0)
    rows = gather_rows(pack(coarse_img, [jnp.sum(residual0 * z0), jnp.sum(z0 * image0)]))
    coarse_img_all, (rz0, curve0) = unpack(rows, vecs, 2)
    alpha0 = rz0 / curve0
    solution1 = alpha0 * z0
    rhs_box1 = rhs_box0 - alpha0 * image0_box
    residual1 = rhs_box1[2:-2, 2:-2, 2:-2]
    coarse1_all = coarse0_all - alpha0 * coarse_img_all
    z1 = precondition(rhs_box1, residual1, coarse1_all)
    near1 = padded(z1, sides, 1)
    image_z1 = stencil(free_face * near1, cond_face, z1, storage, free)
    local = [
        jnp.sum(residual1 * z1),
        jnp.sum(z1 * image_z1),
        jnp.sum(z1 * image0),
        jnp.sum(z0 * image_z1),
    ]
    _, (rz1, zz, cross_a, cross_b) = unpack(gather_rows(pack(jnp.zeros((0,), jnp.float32), local)), 0, 4)
    beta = rz1 / rz0
    direction1 = z1 + beta * z0
    image1 = image_z1 + beta * image0
    curve1 = zz + beta * (cross_a + cross_b) + beta * beta * curve0
    alpha1 = rz1 / curve1
    solution2 = solution1 + alpha1 * direction1
    residual2 = residual1 - alpha1 * image1
    return (solution2, residual2)


def solution(mesh):
    placed = (
        P("gx", "gy", "gz"),
        P(None, "gx", "gy", "gz"),
        P("gx", "gy", "gz"),
        P("gx", "gy", "gz"),
        P(None, "gx", "gy", "gz"),
        P(("gx", "gy", "gz"), None),
    )
    return jax.shard_map(
        shards,
        mesh=mesh,
        in_specs=placed,
        out_specs=(P("gx", "gy", "gz"), P("gx", "gy", "gz")),
        check_vma=False,
    )
```

```python
import functools

import jax
import jax.numpy as jnp
from jax import lax
from jax.experimental import pallas as pl
from jax.experimental.pallas import tpu as pltpu
from jax.sharding import PartitionSpec as P

MESH_ID = pl.DeviceIdType.MESH

SWEEPS = 4
ITERS = 2


RELAX = 2.0 / 3.0


def padded(value, sides, width):
    for axis, dim in sides:
        count, length = (lax.axis_size(axis), value.shape[dim])
        up = [(i, (i + 1) % count) for i in range(count - 1)]
        down = [(j, i) for i, j in up]
        last = lax.slice_in_dim(value, length - width, length, axis=dim)
        leading = lax.slice_in_dim(value, 0, width, axis=dim)
        before = lax.ppermute(last, axis, up)
        after = lax.ppermute(leading, axis, down)
        value = jnp.concatenate([before, value, after], axis=dim)
    return value


def pad_cond(cond):
    return jnp.pad(cond, ((0, 0), (1, 1), (1, 1), (1, 1)))


def stencil(padded_free, padded_cond, field, storage, free):
    middle = padded_free[1:-1, 1:-1, 1:-1]
    total = storage * middle
    total = (
        total
        + padded_cond[0, 1:-1, 1:-1, 1:-1] * (middle - padded_free[2:, 1:-1, 1:-1])
        + padded_cond[0, :-2, 1:-1, 1:-1] * (middle - padded_free[:-2, 1:-1, 1:-1])
    )
    total = (
        total
        + padded_cond[1, 1:-1, 1:-1, 1:-1] * (middle - padded_free[1:-1, 2:, 1:-1])
        + padded_cond[1, 1:-1, :-2, 1:-1] * (middle - padded_free[1:-1, :-2, 1:-1])
    )
    total = (
        total
        + padded_cond[2, 1:-1, 1:-1, 1:-1] * (middle - padded_free[1:-1, 1:-1, 2:])
        + padded_cond[2, 1:-1, 1:-1, :-2] * (middle - padded_free[1:-1, 1:-1, :-2])
    )
    return free * total + (1.0 - free) * field


def diagonal_of(padded_cond, storage, free):
    total = storage + padded_cond[0, 1:-1, 1:-1, 1:-1] + padded_cond[0, :-2, 1:-1, 1:-1]
    total = total + padded_cond[1, 1:-1, 1:-1, 1:-1] + padded_cond[1, 1:-1, :-2, 1:-1]
    total = total + padded_cond[2, 1:-1, 1:-1, 1:-1] + padded_cond[2, 1:-1, 1:-1, :-2]
    return free * total + (1.0 - free)


def jacobi(rhs_box, padded_cond, diagonal, storage_box, free_box):
    guess = jnp.zeros_like(rhs_box)
    for sweep in range(SWEEPS):
        image = stencil(jnp.pad(free_box * guess, 1), padded_cond, guess, storage_box, free_box)
        guess = guess + RELAX * (rhs_box - image) / diagonal
    return guess


def project(basis, field):
    return jnp.sum(basis * field[None], axis=(1, 2, 3))


def expand(basis, weights, field):
    return jnp.sum(weights[:, None, None, None] * basis, axis=0)


LANES = 128


def residual_rim(field):
    return padded(field, (("gx", 0), ("gy", 1), ("gz", 2)), 2)


def gather_kernel(sizes, row_ref, out_ref, held, local_sem, send1, recv1, send2, recv2, send3, recv3):
    nx, ny, nz = sizes
    a = lax.axis_index("gx")
    b = lax.axis_index("gy")
    c = lax.axis_index("gz")
    me = (a * ny + b) * nz + c

    def along_z(k):
        return (a, b, lax.rem(c + k, nz))

    def along_y(k):
        return (a, lax.rem(b + k, ny), c)

    def along_x(k):
        return (lax.rem(a + k, nx), b, c)

    peers = [along_z(k) for k in range(1, nz)]
    peers += [along_y(k) for k in range(1, ny)]
    peers += [along_x(k) for k in range(1, nx)]
    barrier = pltpu.get_barrier_semaphore()
    for peer in peers:
        pl.semaphore_signal(barrier, inc=1, device_id=peer, device_id_type=MESH_ID)
    pl.semaphore_wait(barrier, len(peers))

    own = pltpu.make_async_copy(row_ref, held.at[pl.ds(me, 1)], local_sem.at[0])
    own.start()
    sent = []

    def stage(src_of, first_of, count, size, toward, send, recv):
        for k in range(1, size):
            copy = pltpu.make_async_remote_copy(
                src_ref=src_of(0),
                dst_ref=held.at[pl.ds(first_of(0), count)],
                send_sem=send.at[k],
                recv_sem=recv.at[k],
                device_id=toward(k),
                device_id_type=MESH_ID,
            )
            copy.start()
            sent.append(copy)
        for k in range(1, size):
            pltpu.make_async_remote_copy(
                src_ref=src_of(k),
                dst_ref=held.at[pl.ds(first_of(k), count)],
                send_sem=send.at[k],
                recv_sem=recv.at[k],
                device_id=toward(size - k),
                device_id_type=MESH_ID,
            ).wait_recv()

    z_first = lambda k: (a * ny + b) * nz + lax.rem(c + nz - k, nz)
    stage(lambda k: row_ref, z_first, 1, nz, along_z, send1, recv1)
    own.wait()
    y_first = lambda k: (a * ny + lax.rem(b + ny - k, ny)) * nz
    stage(lambda k: held.at[pl.ds(y_first(k), nz)], y_first, nz, ny, along_y, send2, recv2)
    x_first = lambda k: lax.rem(a + nx - k, nx) * ny * nz
    stage(lambda k: held.at[pl.ds(x_first(k), ny * nz)], x_first, ny * nz, nx, along_x, send3, recv3)
    for copy in sent:
        copy.wait_send()
    final = pltpu.make_async_copy(held, out_ref, local_sem.at[1])
    final.start()
    final.wait()


def gather_rows(row):
    sizes = (lax.axis_size("gx"), lax.axis_size("gy"), lax.axis_size("gz"))
    count = sizes[0] * sizes[1] * sizes[2]
    tile = row[:, None, :]
    rows = pl.pallas_call(
        functools.partial(gather_kernel, sizes),
        out_shape=jax.ShapeDtypeStruct((count, 1, LANES), jnp.float32),
        in_specs=[pl.BlockSpec(memory_space=pltpu.VMEM)],
        out_specs=pl.BlockSpec(memory_space=pltpu.VMEM),
        scratch_shapes=[
            pltpu.VMEM((count, 1, LANES), jnp.float32),
            pltpu.SemaphoreType.DMA((2,)),
            pltpu.SemaphoreType.DMA((sizes[2],)),
            pltpu.SemaphoreType.DMA((sizes[2],)),
            pltpu.SemaphoreType.DMA((sizes[1],)),
            pltpu.SemaphoreType.DMA((sizes[1],)),
            pltpu.SemaphoreType.DMA((sizes[0],)),
            pltpu.SemaphoreType.DMA((sizes[0],)),
        ],
        compiler_params=pltpu.CompilerParams(collective_id=0, has_side_effects=True),
    )(tile)
    return rows[:, 0, :]


def pack(coarse, scalars):
    vecs = coarse.shape[0]
    row = jnp.zeros((LANES,), jnp.float32)
    row = row.at[:vecs].set(coarse)
    if scalars:
        row = row.at[vecs:vecs + len(scalars)].set(jnp.stack(scalars))
    return row[None]


def unpack(rows, vecs, count):
    coarse = rows[:, :vecs].reshape(-1)
    sums = jnp.sum(rows[:, vecs:vecs + count], axis=0)
    return coarse, [sums[i] for i in range(count)]


def shards(right_side, conductance, storage, dirichlet, basis, coarse_inverse):
    vecs = basis.shape[0]
    sides = (("gx", 0), ("gy", 1), ("gz", 2))
    free = 1.0 - dirichlet.astype(jnp.float32)
    stacked = jnp.concatenate([conductance, storage[None], free[None], right_side[None]], axis=0)
    wide = padded(stacked, (("gx", 1), ("gy", 2), ("gz", 3)), 3)
    cond_wide = wide[:3]
    free_wide = wide[4]
    storage_wide = wide[3]
    cond_box = wide[:3, 1:-1, 1:-1, 1:-1]
    storage_box = wide[3, 1:-1, 1:-1, 1:-1]
    free_box = wide[4, 1:-1, 1:-1, 1:-1]
    rhs_box0 = wide[5, 1:-1, 1:-1, 1:-1]
    box_cond = pad_cond(cond_box)
    box_diag = diagonal_of(box_cond, storage_box, free_box)
    cond_face = wide[:3, 2:-2, 2:-2, 2:-2]
    free_face = wide[4, 2:-2, 2:-2, 2:-2]

    def schwarz(rhs_box):
        return jacobi(rhs_box, box_cond, box_diag, storage_box, free_box)[2:-2, 2:-2, 2:-2]

    def precondition(rhs_box, residual, coarse_all):
        weights = jnp.dot(coarse_inverse, coarse_all, precision=lax.Precision.HIGHEST)
        return schwarz(rhs_box) + expand(basis, weights, residual)

    residual0 = right_side
    coarse0 = project(basis, residual0)
    coarse0_all, _ = unpack(gather_rows(pack(coarse0, [])), vecs, 0)
    z0 = precondition(rhs_box0, residual0, coarse0_all)
    near0 = padded(z0, sides, 3)
    inner = (slice(1, -1),) * 3
    image0_box = stencil(free_wide * near0, cond_wide, near0[inner], storage_wide[inner], free_wide[inner])
    image0 = image0_box[2:-2, 2:-2, 2:-2]
    coarse_img = project(basis, image0)
    rows = gather_rows(pack(coarse_img, [jnp.sum(residual0 * z0), jnp.sum(z0 * image0)]))
    coarse_img_all, (rz0, curve0) = unpack(rows, vecs, 2)
    alpha0 = rz0 / curve0
    solution1 = alpha0 * z0
    rhs_box1 = rhs_box0 - alpha0 * image0_box
    residual1 = rhs_box1[2:-2, 2:-2, 2:-2]
    coarse1_all = coarse0_all - alpha0 * coarse_img_all
    z1 = precondition(rhs_box1, residual1, coarse1_all)
    near1 = padded(z1, sides, 1)
    image_z1 = stencil(free_face * near1, cond_face, z1, storage, free)
    local = [
        jnp.sum(residual1 * z1),
        jnp.sum(z1 * image_z1),
        jnp.sum(z1 * image0),
        jnp.sum(z0 * image_z1),
    ]
    _, (rz1, zz, cross_a, cross_b) = unpack(gather_rows(pack(jnp.zeros((0,), jnp.float32), local)), 0, 4)
    beta = rz1 / rz0
    direction1 = z1 + beta * z0
    image1 = image_z1 + beta * image0
    curve1 = zz + beta * (cross_a + cross_b) + beta * beta * curve0
    alpha1 = rz1 / curve1
    solution2 = solution1 + alpha1 * direction1
    residual2 = residual1 - alpha1 * image1
    return (solution2, residual2)


def solution(mesh):
    placed = (
        P("gx", "gy", "gz"),
        P(None, "gx", "gy", "gz"),
        P("gx", "gy", "gz"),
        P("gx", "gy", "gz"),
        P(None, "gx", "gy", "gz"),
        P(("gx", "gy", "gz"), None),
    )
    return jax.shard_map(
        shards,
        mesh=mesh,
        in_specs=placed,
        out_specs=(P("gx", "gy", "gz"), P("gx", "gy", "gz")),
        check_vma=False,
    )
```

```python
import functools

import jax
import jax.numpy as jnp
from jax import lax
from jax.experimental import pallas as pl
from jax.experimental.pallas import tpu as pltpu
from jax.sharding import PartitionSpec as P

MESH_ID = pl.DeviceIdType.MESH

SWEEPS = 4
ITERS = 2


RELAX = 2.0 / 3.0


def padded(value, sides, width):
    for axis, dim in sides:
        count, length = (lax.axis_size(axis), value.shape[dim])
        up = [(i, (i + 1) % count) for i in range(count - 1)]
        down = [(j, i) for i, j in up]
        last = lax.slice_in_dim(value, length - width, length, axis=dim)
        leading = lax.slice_in_dim(value, 0, width, axis=dim)
        before = lax.ppermute(last, axis, up)
        after = lax.ppermute(leading, axis, down)
        value = jnp.concatenate([before, value, after], axis=dim)
    return value


def pad_cond(cond):
    return jnp.pad(cond, ((0, 0), (1, 1), (1, 1), (1, 1)))


def stencil(padded_free, padded_cond, field, storage, free):
    middle = padded_free[1:-1, 1:-1, 1:-1]
    total = storage * middle
    total = (
        total
        + padded_cond[0, 1:-1, 1:-1, 1:-1] * (middle - padded_free[2:, 1:-1, 1:-1])
        + padded_cond[0, :-2, 1:-1, 1:-1] * (middle - padded_free[:-2, 1:-1, 1:-1])
    )
    total = (
        total
        + padded_cond[1, 1:-1, 1:-1, 1:-1] * (middle - padded_free[1:-1, 2:, 1:-1])
        + padded_cond[1, 1:-1, :-2, 1:-1] * (middle - padded_free[1:-1, :-2, 1:-1])
    )
    total = (
        total
        + padded_cond[2, 1:-1, 1:-1, 1:-1] * (middle - padded_free[1:-1, 1:-1, 2:])
        + padded_cond[2, 1:-1, 1:-1, :-2] * (middle - padded_free[1:-1, 1:-1, :-2])
    )
    return free * total + (1.0 - free) * field


def diagonal_of(padded_cond, storage, free):
    total = storage + padded_cond[0, 1:-1, 1:-1, 1:-1] + padded_cond[0, :-2, 1:-1, 1:-1]
    total = total + padded_cond[1, 1:-1, 1:-1, 1:-1] + padded_cond[1, 1:-1, :-2, 1:-1]
    total = total + padded_cond[2, 1:-1, 1:-1, 1:-1] + padded_cond[2, 1:-1, 1:-1, :-2]
    return free * total + (1.0 - free)


def jacobi(rhs_box, padded_cond, diagonal, storage_box, free_box):
    guess = jnp.zeros_like(rhs_box)
    for sweep in range(SWEEPS):
        image = stencil(jnp.pad(free_box * guess, 1), padded_cond, guess, storage_box, free_box)
        guess = guess + RELAX * (rhs_box - image) / diagonal
    return guess


def project(basis, field):
    return jnp.sum(basis * field[None], axis=(1, 2, 3))


def expand(basis, weights, field):
    return jnp.sum(weights[:, None, None, None] * basis, axis=0)


LANES = 128


def residual_rim(field):
    return padded(field, (("gx", 0), ("gy", 1), ("gz", 2)), 2)


def gather_kernel(sizes, row_ref, out_ref, held, local_sem, send1, recv1, send2, recv2, send3, recv3):
    nx, ny, nz = sizes
    a = lax.axis_index("gx")
    b = lax.axis_index("gy")
    c = lax.axis_index("gz")
    me = (a * ny + b) * nz + c

    def along_z(k):
        return (a, b, lax.rem(c + k, nz))

    def along_y(k):
        return (a, lax.rem(b + k, ny), c)

    def along_x(k):
        return (lax.rem(a + k, nx), b, c)

    peers = [along_z(k) for k in range(1, nz)]
    peers += [along_y(k) for k in range(1, ny)]
    peers += [along_x(k) for k in range(1, nx)]
    barrier = pltpu.get_barrier_semaphore()
    for peer in peers:
        pl.semaphore_signal(barrier, inc=1, device_id=peer, device_id_type=MESH_ID)
    pl.semaphore_wait(barrier, len(peers))

    own = pltpu.make_async_copy(row_ref, held.at[pl.ds(me, 1)], local_sem.at[0])
    own.start()
    sent = []

    def stage(src_of, first_of, count, size, toward, send, recv):
        for k in range(1, size):
            copy = pltpu.make_async_remote_copy(
                src_ref=src_of(0),
                dst_ref=held.at[pl.ds(first_of(0), count)],
                send_sem=send.at[k],
                recv_sem=recv.at[k],
                device_id=toward(k),
                device_id_type=MESH_ID,
            )
            copy.start()
            sent.append(copy)
        for k in range(1, size):
            pltpu.make_async_remote_copy(
                src_ref=src_of(k),
                dst_ref=held.at[pl.ds(first_of(k), count)],
                send_sem=send.at[k],
                recv_sem=recv.at[k],
                device_id=toward(size - k),
                device_id_type=MESH_ID,
            ).wait_recv()

    z_first = lambda k: (a * ny + b) * nz + lax.rem(c + nz - k, nz)
    stage(lambda k: row_ref, z_first, 1, nz, along_z, send1, recv1)
    own.wait()
    y_first = lambda k: (a * ny + lax.rem(b + ny - k, ny)) * nz
    stage(lambda k: held.at[pl.ds(y_first(k), nz)], y_first, nz, ny, along_y, send2, recv2)
    x_first = lambda k: lax.rem(a + nx - k, nx) * ny * nz
    stage(lambda k: held.at[pl.ds(x_first(k), ny * nz)], x_first, ny * nz, nx, along_x, send3, recv3)
    for copy in sent:
        copy.wait_send()
    final = pltpu.make_async_copy(held, out_ref, local_sem.at[1])
    final.start()
    final.wait()


def gather_rows(row):
    sizes = (lax.axis_size("gx"), lax.axis_size("gy"), lax.axis_size("gz"))
    count = sizes[0] * sizes[1] * sizes[2]
    tile = row[:, None, :]
    rows = pl.pallas_call(
        functools.partial(gather_kernel, sizes),
        out_shape=jax.ShapeDtypeStruct((count, 1, LANES), jnp.float32),
        in_specs=[pl.BlockSpec(memory_space=pltpu.VMEM)],
        out_specs=pl.BlockSpec(memory_space=pltpu.VMEM),
        scratch_shapes=[
            pltpu.VMEM((count, 1, LANES), jnp.float32),
            pltpu.SemaphoreType.DMA((2,)),
            pltpu.SemaphoreType.DMA((sizes[2],)),
            pltpu.SemaphoreType.DMA((sizes[2],)),
            pltpu.SemaphoreType.DMA((sizes[1],)),
            pltpu.SemaphoreType.DMA((sizes[1],)),
            pltpu.SemaphoreType.DMA((sizes[0],)),
            pltpu.SemaphoreType.DMA((sizes[0],)),
        ],
        compiler_params=pltpu.CompilerParams(collective_id=0, has_side_effects=True),
    )(tile)
    return rows[:, 0, :]


DIRS = [(i, j, k) for i in (-1, 0, 1) for j in (-1, 0, 1) for k in (-1, 0, 1) if (i, j, k) != (0, 0, 0)]


def halo_kernel(sizes, count, *refs):
    ins, outs, held = refs[:count], refs[count:2 * count], refs[2 * count:3 * count]
    send_sem, recv_sem, local_sem = refs[3 * count:]
    here = [lax.axis_index(name) for name in ("gx", "gy", "gz")]

    def toward(d):
        return tuple(lax.rem(i + s + n, n) for i, s, n in zip(here, d, sizes))

    barrier = pltpu.get_barrier_semaphore()
    for d in DIRS:
        pl.semaphore_signal(barrier, inc=1, device_id=toward(d), device_id_type=MESH_ID)
    pl.semaphore_wait(barrier, len(DIRS))
    flip = [DIRS.index(tuple(-s for s in d)) for d in DIRS]
    sent = []
    for i, d in enumerate(DIRS):
        copy = pltpu.make_async_remote_copy(
            src_ref=ins[i],
            dst_ref=held[flip[i]],
            send_sem=send_sem.at[i],
            recv_sem=recv_sem.at[flip[i]],
            device_id=toward(d),
            device_id_type=MESH_ID,
        )
        copy.start()
        sent.append(copy)
    for j, d in enumerate(DIRS):
        pltpu.make_async_remote_copy(
            src_ref=ins[flip[j]],
            dst_ref=held[j],
            send_sem=send_sem.at[flip[j]],
            recv_sem=recv_sem.at[j],
            device_id=toward(d),
            device_id_type=MESH_ID,
        ).wait_recv()
    for copy in sent:
        copy.wait_send()
    local = []
    for j in range(count):
        copy = pltpu.make_async_copy(held[j], outs[j], local_sem.at[j])
        copy.start()
        local.append(copy)
    for copy in local:
        copy.wait()


def flat_rows(piece):
    size = piece.size
    rows = -(-size // 1024) * 8
    return jnp.pad(piece.reshape(-1), (0, rows * LANES - size)).reshape(rows, LANES)


def exchange(value, dims, width, cid):
    sizes = tuple(lax.axis_size(name) for name in ("gx", "gy", "gz"))
    here = [lax.axis_index(name) for name in ("gx", "gy", "gz")]
    pieces = []
    for d in DIRS:
        index = [slice(None)] * value.ndim
        for dim, s in zip(dims, d):
            length = value.shape[dim]
            if s == 1:
                index[dim] = slice(length - width, length)
            elif s == -1:
                index[dim] = slice(0, width)
        pieces.append(value[tuple(index)])
    flats = [flat_rows(p) for p in pieces]
    count = len(flats)
    shapes = [jax.ShapeDtypeStruct(f.shape, f.dtype) for f in flats]
    spec = pl.BlockSpec(memory_space=pltpu.VMEM)
    got = pl.pallas_call(
        functools.partial(halo_kernel, sizes, count),
        out_shape=shapes,
        in_specs=[spec] * count,
        out_specs=[spec] * count,
        scratch_shapes=[pltpu.VMEM(f.shape, f.dtype) for f in flats]
        + [pltpu.SemaphoreType.DMA((count,))] * 3,
        compiler_params=pltpu.CompilerParams(collective_id=cid, has_side_effects=True),
    )(*flats)
    blocks = {}
    for j, d in enumerate(DIRS):
        shape = pieces[j].shape
        piece = got[j].reshape(-1)[: pieces[j].size].reshape(shape)
        valid = True
        for i, s, n in zip(here, d, sizes):
            if s:
                valid = jnp.logical_and(valid, jnp.logical_and(i + s >= 0, i + s < n))
        blocks[d] = jnp.where(valid, piece, 0.0)
    blocks[(0, 0, 0)] = value
    planes = []
    for dx in (-1, 0, 1):
        lines = []
        for dy in (-1, 0, 1):
            lines.append(jnp.concatenate([blocks[(dx, dy, dz)] for dz in (-1, 0, 1)], axis=dims[2]))
        planes.append(jnp.concatenate(lines, axis=dims[1]))
    return jnp.concatenate(planes, axis=dims[0])


def pack(coarse, scalars):
    vecs = coarse.shape[0]
    row = jnp.zeros((LANES,), jnp.float32)
    row = row.at[:vecs].set(coarse)
    if scalars:
        row = row.at[vecs:vecs + len(scalars)].set(jnp.stack(scalars))
    return row[None]


def unpack(rows, vecs, count):
    coarse = rows[:, :vecs].reshape(-1)
    sums = jnp.sum(rows[:, vecs:vecs + count], axis=0)
    return coarse, [sums[i] for i in range(count)]


def shards(right_side, conductance, storage, dirichlet, basis, coarse_inverse):
    vecs = basis.shape[0]
    sides = (("gx", 0), ("gy", 1), ("gz", 2))
    free = 1.0 - dirichlet.astype(jnp.float32)
    stacked = jnp.concatenate([conductance, storage[None], free[None], right_side[None]], axis=0)
    wide = exchange(stacked, (1, 2, 3), 3, 1)
    cond_wide = wide[:3]
    free_wide = wide[4]
    storage_wide = wide[3]
    cond_box = wide[:3, 1:-1, 1:-1, 1:-1]
    storage_box = wide[3, 1:-1, 1:-1, 1:-1]
    free_box = wide[4, 1:-1, 1:-1, 1:-1]
    rhs_box0 = wide[5, 1:-1, 1:-1, 1:-1]
    box_cond = pad_cond(cond_box)
    box_diag = diagonal_of(box_cond, storage_box, free_box)
    cond_face = wide[:3, 2:-2, 2:-2, 2:-2]
    free_face = wide[4, 2:-2, 2:-2, 2:-2]

    def schwarz(rhs_box):
        return jacobi(rhs_box, box_cond, box_diag, storage_box, free_box)[2:-2, 2:-2, 2:-2]

    def precondition(rhs_box, residual, coarse_all):
        weights = jnp.dot(coarse_inverse, coarse_all, precision=lax.Precision.HIGHEST)
        return schwarz(rhs_box) + expand(basis, weights, residual)

    residual0 = right_side
    coarse0 = project(basis, residual0)
    coarse0_all, _ = unpack(gather_rows(pack(coarse0, [])), vecs, 0)
    z0 = precondition(rhs_box0, residual0, coarse0_all)
    near0 = exchange(z0, (0, 1, 2), 3, 2)
    inner = (slice(1, -1),) * 3
    image0_box = stencil(free_wide * near0, cond_wide, near0[inner], storage_wide[inner], free_wide[inner])
    image0 = image0_box[2:-2, 2:-2, 2:-2]
    coarse_img = project(basis, image0)
    rows = gather_rows(pack(coarse_img, [jnp.sum(residual0 * z0), jnp.sum(z0 * image0)]))
    coarse_img_all, (rz0, curve0) = unpack(rows, vecs, 2)
    alpha0 = rz0 / curve0
    solution1 = alpha0 * z0
    rhs_box1 = rhs_box0 - alpha0 * image0_box
    residual1 = rhs_box1[2:-2, 2:-2, 2:-2]
    coarse1_all = coarse0_all - alpha0 * coarse_img_all
    z1 = precondition(rhs_box1, residual1, coarse1_all)
    near1 = exchange(z1, (0, 1, 2), 1, 3)
    image_z1 = stencil(free_face * near1, cond_face, z1, storage, free)
    local = [
        jnp.sum(residual1 * z1),
        jnp.sum(z1 * image_z1),
        jnp.sum(z1 * image0),
        jnp.sum(z0 * image_z1),
    ]
    _, (rz1, zz, cross_a, cross_b) = unpack(gather_rows(pack(jnp.zeros((0,), jnp.float32), local)), 0, 4)
    beta = rz1 / rz0
    direction1 = z1 + beta * z0
    image1 = image_z1 + beta * image0
    curve1 = zz + beta * (cross_a + cross_b) + beta * beta * curve0
    alpha1 = rz1 / curve1
    solution2 = solution1 + alpha1 * direction1
    residual2 = residual1 - alpha1 * image1
    return (solution2, residual2)


def solution(mesh):
    placed = (
        P("gx", "gy", "gz"),
        P(None, "gx", "gy", "gz"),
        P("gx", "gy", "gz"),
        P("gx", "gy", "gz"),
        P(None, "gx", "gy", "gz"),
        P(("gx", "gy", "gz"), None),
    )
    return jax.shard_map(
        shards,
        mesh=mesh,
        in_specs=placed,
        out_specs=(P("gx", "gy", "gz"), P("gx", "gy", "gz")),
        check_vma=False,
    )
```

```python
import functools

import jax
import jax.numpy as jnp
from jax import lax
from jax.experimental import pallas as pl
from jax.experimental.pallas import tpu as pltpu
from jax.sharding import PartitionSpec as P

MESH_ID = pl.DeviceIdType.MESH

SWEEPS = 4
ITERS = 2


RELAX = 2.0 / 3.0


def padded(value, sides, width):
    for axis, dim in sides:
        count, length = (lax.axis_size(axis), value.shape[dim])
        up = [(i, (i + 1) % count) for i in range(count - 1)]
        down = [(j, i) for i, j in up]
        last = lax.slice_in_dim(value, length - width, length, axis=dim)
        leading = lax.slice_in_dim(value, 0, width, axis=dim)
        before = lax.ppermute(last, axis, up)
        after = lax.ppermute(leading, axis, down)
        value = jnp.concatenate([before, value, after], axis=dim)
    return value


def pad_cond(cond):
    return jnp.pad(cond, ((0, 0), (1, 1), (1, 1), (1, 1)))


def stencil(padded_free, padded_cond, field, storage, free):
    middle = padded_free[1:-1, 1:-1, 1:-1]
    total = storage * middle
    total = (
        total
        + padded_cond[0, 1:-1, 1:-1, 1:-1] * (middle - padded_free[2:, 1:-1, 1:-1])
        + padded_cond[0, :-2, 1:-1, 1:-1] * (middle - padded_free[:-2, 1:-1, 1:-1])
    )
    total = (
        total
        + padded_cond[1, 1:-1, 1:-1, 1:-1] * (middle - padded_free[1:-1, 2:, 1:-1])
        + padded_cond[1, 1:-1, :-2, 1:-1] * (middle - padded_free[1:-1, :-2, 1:-1])
    )
    total = (
        total
        + padded_cond[2, 1:-1, 1:-1, 1:-1] * (middle - padded_free[1:-1, 1:-1, 2:])
        + padded_cond[2, 1:-1, 1:-1, :-2] * (middle - padded_free[1:-1, 1:-1, :-2])
    )
    return free * total + (1.0 - free) * field


def diagonal_of(padded_cond, storage, free):
    total = storage + padded_cond[0, 1:-1, 1:-1, 1:-1] + padded_cond[0, :-2, 1:-1, 1:-1]
    total = total + padded_cond[1, 1:-1, 1:-1, 1:-1] + padded_cond[1, 1:-1, :-2, 1:-1]
    total = total + padded_cond[2, 1:-1, 1:-1, 1:-1] + padded_cond[2, 1:-1, 1:-1, :-2]
    return free * total + (1.0 - free)


def jacobi(rhs_box, padded_cond, diagonal, storage_box, free_box):
    guess = jnp.zeros_like(rhs_box)
    for sweep in range(SWEEPS):
        image = stencil(jnp.pad(free_box * guess, 1), padded_cond, guess, storage_box, free_box)
        guess = guess + RELAX * (rhs_box - image) / diagonal
    return guess


def project(basis, field):
    return jnp.sum(basis * field[None], axis=(1, 2, 3))


def expand(basis, weights, field):
    return jnp.sum(weights[:, None, None, None] * basis, axis=0)


LANES = 128


def residual_rim(field):
    return padded(field, (("gx", 0), ("gy", 1), ("gz", 2)), 2)


def gather_kernel(sizes, row_ref, out_ref, held, local_sem, send1, recv1, send2, recv2):
    nx, ny, nz = sizes
    plane = ny * nz
    a = lax.axis_index("gx")
    b = lax.axis_index("gy")
    c = lax.axis_index("gz")
    me = (a * ny + b) * nz + c

    def in_plane(k):
        return (a, lax.rem(b + k // nz, ny), lax.rem(c + k % nz, nz))

    def along_x(k):
        return (lax.rem(a + k, nx), b, c)

    peers = [in_plane(k) for k in range(1, plane)] + [along_x(k) for k in range(1, nx)]
    barrier = pltpu.get_barrier_semaphore()
    for peer in peers:
        pl.semaphore_signal(barrier, inc=1, device_id=peer, device_id_type=MESH_ID)
    pl.semaphore_wait(barrier, len(peers))

    own = pltpu.make_async_copy(row_ref, held.at[pl.ds(me, 1)], local_sem.at[0])
    own.start()
    sent = []

    def stage(src_of, first_of, count, size, toward, send, recv):
        for k in range(1, size):
            copy = pltpu.make_async_remote_copy(
                src_ref=src_of(0),
                dst_ref=held.at[pl.ds(first_of(0), count)],
                send_sem=send.at[k],
                recv_sem=recv.at[k],
                device_id=toward(k),
                device_id_type=MESH_ID,
            )
            copy.start()
            sent.append(copy)
        for k in range(1, size):
            pltpu.make_async_remote_copy(
                src_ref=src_of(k),
                dst_ref=held.at[pl.ds(first_of(k), count)],
                send_sem=send.at[k],
                recv_sem=recv.at[k],
                device_id=toward(size - k),
                device_id_type=MESH_ID,
            ).wait_recv()

    def p_first(k):
        return (a * ny + lax.rem(b + ny - k // nz, ny)) * nz + lax.rem(c + nz - k % nz, nz)

    stage(lambda k: row_ref, p_first, 1, plane, in_plane, send1, recv1)
    own.wait()
    x_first = lambda k: lax.rem(a + nx - k, nx) * plane
    stage(lambda k: held.at[pl.ds(x_first(k), plane)], x_first, plane, nx, along_x, send2, recv2)
    for copy in sent:
        copy.wait_send()
    final = pltpu.make_async_copy(held, out_ref, local_sem.at[1])
    final.start()
    final.wait()


def gather_rows(row):
    sizes = (lax.axis_size("gx"), lax.axis_size("gy"), lax.axis_size("gz"))
    count = sizes[0] * sizes[1] * sizes[2]
    tile = row[:, None, :]
    rows = pl.pallas_call(
        functools.partial(gather_kernel, sizes),
        out_shape=jax.ShapeDtypeStruct((count, 1, LANES), jnp.float32),
        in_specs=[pl.BlockSpec(memory_space=pltpu.VMEM)],
        out_specs=pl.BlockSpec(memory_space=pltpu.VMEM),
        scratch_shapes=[
            pltpu.VMEM((count, 1, LANES), jnp.float32),
            pltpu.SemaphoreType.DMA((2,)),
            pltpu.SemaphoreType.DMA((sizes[1] * sizes[2],)),
            pltpu.SemaphoreType.DMA((sizes[1] * sizes[2],)),
            pltpu.SemaphoreType.DMA((sizes[0],)),
            pltpu.SemaphoreType.DMA((sizes[0],)),
        ],
        compiler_params=pltpu.CompilerParams(collective_id=0, has_side_effects=True),
    )(tile)
    return rows[:, 0, :]


def pack(coarse, scalars):
    vecs = coarse.shape[0]
    row = jnp.zeros((LANES,), jnp.float32)
    row = row.at[:vecs].set(coarse)
    if scalars:
        row = row.at[vecs:vecs + len(scalars)].set(jnp.stack(scalars))
    return row[None]


def unpack(rows, vecs, count):
    coarse = rows[:, :vecs].reshape(-1)
    sums = jnp.sum(rows[:, vecs:vecs + count], axis=0)
    return coarse, [sums[i] for i in range(count)]


def shards(right_side, conductance, storage, dirichlet, basis, coarse_inverse):
    vecs = basis.shape[0]
    sides = (("gx", 0), ("gy", 1), ("gz", 2))
    free = 1.0 - dirichlet.astype(jnp.float32)
    stacked = jnp.concatenate([conductance, storage[None], free[None], right_side[None]], axis=0)
    wide = padded(stacked, (("gx", 1), ("gy", 2), ("gz", 3)), 3)
    cond_wide = wide[:3]
    free_wide = wide[4]
    storage_wide = wide[3]
    cond_box = wide[:3, 1:-1, 1:-1, 1:-1]
    storage_box = wide[3, 1:-1, 1:-1, 1:-1]
    free_box = wide[4, 1:-1, 1:-1, 1:-1]
    rhs_box0 = wide[5, 1:-1, 1:-1, 1:-1]
    box_cond = pad_cond(cond_box)
    box_diag = diagonal_of(box_cond, storage_box, free_box)
    cond_face = wide[:3, 2:-2, 2:-2, 2:-2]
    free_face = wide[4, 2:-2, 2:-2, 2:-2]

    def schwarz(rhs_box):
        return jacobi(rhs_box, box_cond, box_diag, storage_box, free_box)[2:-2, 2:-2, 2:-2]

    def precondition(rhs_box, residual, coarse_all):
        weights = jnp.dot(coarse_inverse, coarse_all, precision=lax.Precision.HIGHEST)
        return schwarz(rhs_box) + expand(basis, weights, residual)

    residual0 = right_side
    coarse0 = project(basis, residual0)
    coarse0_all, _ = unpack(gather_rows(pack(coarse0, [])), vecs, 0)
    z0 = precondition(rhs_box0, residual0, coarse0_all)
    near0 = padded(z0, sides, 3)
    inner = (slice(1, -1),) * 3
    image0_box = stencil(free_wide * near0, cond_wide, near0[inner], storage_wide[inner], free_wide[inner])
    image0 = image0_box[2:-2, 2:-2, 2:-2]
    coarse_img = project(basis, image0)
    rows = gather_rows(pack(coarse_img, [jnp.sum(residual0 * z0), jnp.sum(z0 * image0)]))
    coarse_img_all, (rz0, curve0) = unpack(rows, vecs, 2)
    alpha0 = rz0 / curve0
    solution1 = alpha0 * z0
    rhs_box1 = rhs_box0 - alpha0 * image0_box
    residual1 = rhs_box1[2:-2, 2:-2, 2:-2]
    coarse1_all = coarse0_all - alpha0 * coarse_img_all
    z1 = precondition(rhs_box1, residual1, coarse1_all)
    near1 = padded(z1, sides, 1)
    image_z1 = stencil(free_face * near1, cond_face, z1, storage, free)
    local = [
        jnp.sum(residual1 * z1),
        jnp.sum(z1 * image_z1),
        jnp.sum(z1 * image0),
        jnp.sum(z0 * image_z1),
    ]
    _, (rz1, zz, cross_a, cross_b) = unpack(gather_rows(pack(jnp.zeros((0,), jnp.float32), local)), 0, 4)
    beta = rz1 / rz0
    direction1 = z1 + beta * z0
    image1 = image_z1 + beta * image0
    curve1 = zz + beta * (cross_a + cross_b) + beta * beta * curve0
    alpha1 = rz1 / curve1
    solution2 = solution1 + alpha1 * direction1
    residual2 = residual1 - alpha1 * image1
    return (solution2, residual2)


def solution(mesh):
    placed = (
        P("gx", "gy", "gz"),
        P(None, "gx", "gy", "gz"),
        P("gx", "gy", "gz"),
        P("gx", "gy", "gz"),
        P(None, "gx", "gy", "gz"),
        P(("gx", "gy", "gz"), None),
    )
    return jax.shard_map(
        shards,
        mesh=mesh,
        in_specs=placed,
        out_specs=(P("gx", "gy", "gz"), P("gx", "gy", "gz")),
        check_vma=False,
    )
```

```python
import functools

import jax
import jax.numpy as jnp
from jax import lax
from jax.experimental import pallas as pl
from jax.experimental.pallas import tpu as pltpu
from jax.sharding import PartitionSpec as P

MESH_ID = pl.DeviceIdType.MESH

SWEEPS = 4
ITERS = 2


RELAX = 2.0 / 3.0


def padded(value, sides, width):
    for axis, dim in sides:
        count, length = (lax.axis_size(axis), value.shape[dim])
        up = [(i, (i + 1) % count) for i in range(count - 1)]
        down = [(j, i) for i, j in up]
        last = lax.slice_in_dim(value, length - width, length, axis=dim)
        leading = lax.slice_in_dim(value, 0, width, axis=dim)
        before = lax.ppermute(last, axis, up)
        after = lax.ppermute(leading, axis, down)
        value = jnp.concatenate([before, value, after], axis=dim)
    return value


def pad_cond(cond):
    return jnp.pad(cond, ((0, 0), (1, 1), (1, 1), (1, 1)))


def stencil(padded_free, padded_cond, field, storage, free):
    middle = padded_free[1:-1, 1:-1, 1:-1]
    total = storage * middle
    total = (
        total
        + padded_cond[0, 1:-1, 1:-1, 1:-1] * (middle - padded_free[2:, 1:-1, 1:-1])
        + padded_cond[0, :-2, 1:-1, 1:-1] * (middle - padded_free[:-2, 1:-1, 1:-1])
    )
    total = (
        total
        + padded_cond[1, 1:-1, 1:-1, 1:-1] * (middle - padded_free[1:-1, 2:, 1:-1])
        + padded_cond[1, 1:-1, :-2, 1:-1] * (middle - padded_free[1:-1, :-2, 1:-1])
    )
    total = (
        total
        + padded_cond[2, 1:-1, 1:-1, 1:-1] * (middle - padded_free[1:-1, 1:-1, 2:])
        + padded_cond[2, 1:-1, 1:-1, :-2] * (middle - padded_free[1:-1, 1:-1, :-2])
    )
    return free * total + (1.0 - free) * field


def diagonal_of(padded_cond, storage, free):
    total = storage + padded_cond[0, 1:-1, 1:-1, 1:-1] + padded_cond[0, :-2, 1:-1, 1:-1]
    total = total + padded_cond[1, 1:-1, 1:-1, 1:-1] + padded_cond[1, 1:-1, :-2, 1:-1]
    total = total + padded_cond[2, 1:-1, 1:-1, 1:-1] + padded_cond[2, 1:-1, 1:-1, :-2]
    return free * total + (1.0 - free)


def jacobi(rhs_box, padded_cond, diagonal, storage_box, free_box):
    guess = jnp.zeros_like(rhs_box)
    for sweep in range(SWEEPS):
        image = stencil(jnp.pad(free_box * guess, 1), padded_cond, guess, storage_box, free_box)
        guess = guess + RELAX * (rhs_box - image) / diagonal
    return guess


def project(basis, field):
    return jnp.sum(basis * field[None], axis=(1, 2, 3))


def expand(basis, weights, field):
    return jnp.sum(weights[:, None, None, None] * basis, axis=0)


LANES = 128


def faces(field):
    result = jnp.pad(field, 1)
    for dim, axis in enumerate(("gx", "gy", "gz")):
        count, length = (lax.axis_size(axis), field.shape[dim])
        up = [(i, i + 1) for i in range(count - 1)]
        down = [(j, i) for i, j in up]
        before = lax.ppermute(lax.slice_in_dim(field, length - 1, length, axis=dim), axis, up)
        after = lax.ppermute(lax.slice_in_dim(field, 0, 1, axis=dim), axis, down)
        lead = [1, 1, 1]
        lead[dim] = 0
        result = lax.dynamic_update_slice(result, before, tuple(lead))
        lead[dim] = length + 1
        result = lax.dynamic_update_slice(result, after, tuple(lead))
    return result


def residual_rim(field):
    return padded(field, (("gx", 0), ("gy", 1), ("gz", 2)), 2)


def gather_kernel(sizes, row_ref, out_ref, held, local_sem, send1, recv1, send2, recv2):
    nx, ny, nz = sizes
    plane = ny * nz
    a = lax.axis_index("gx")
    b = lax.axis_index("gy")
    c = lax.axis_index("gz")
    me = (a * ny + b) * nz + c

    def in_plane(k):
        return (a, lax.rem(b + k // nz, ny), lax.rem(c + k % nz, nz))

    def along_x(k):
        return (lax.rem(a + k, nx), b, c)

    peers = [in_plane(k) for k in range(1, plane)] + [along_x(k) for k in range(1, nx)]
    barrier = pltpu.get_barrier_semaphore()
    for peer in peers:
        pl.semaphore_signal(barrier, inc=1, device_id=peer, device_id_type=MESH_ID)
    pl.semaphore_wait(barrier, len(peers))

    own = pltpu.make_async_copy(row_ref, held.at[pl.ds(me, 1)], local_sem.at[0])
    own.start()
    sent = []

    def stage(src_of, first_of, count, size, toward, send, recv):
        for k in range(1, size):
            copy = pltpu.make_async_remote_copy(
                src_ref=src_of(0),
                dst_ref=held.at[pl.ds(first_of(0), count)],
                send_sem=send.at[k],
                recv_sem=recv.at[k],
                device_id=toward(k),
                device_id_type=MESH_ID,
            )
            copy.start()
            sent.append(copy)
        for k in range(1, size):
            pltpu.make_async_remote_copy(
                src_ref=src_of(k),
                dst_ref=held.at[pl.ds(first_of(k), count)],
                send_sem=send.at[k],
                recv_sem=recv.at[k],
                device_id=toward(size - k),
                device_id_type=MESH_ID,
            ).wait_recv()

    def p_first(k):
        return (a * ny + lax.rem(b + ny - k // nz, ny)) * nz + lax.rem(c + nz - k % nz, nz)

    stage(lambda k: row_ref, p_first, 1, plane, in_plane, send1, recv1)
    own.wait()
    x_first = lambda k: lax.rem(a + nx - k, nx) * plane
    stage(lambda k: held.at[pl.ds(x_first(k), plane)], x_first, plane, nx, along_x, send2, recv2)
    for copy in sent:
        copy.wait_send()
    final = pltpu.make_async_copy(held, out_ref, local_sem.at[1])
    final.start()
    final.wait()


def gather_rows(row):
    sizes = (lax.axis_size("gx"), lax.axis_size("gy"), lax.axis_size("gz"))
    count = sizes[0] * sizes[1] * sizes[2]
    tile = row[:, None, :]
    rows = pl.pallas_call(
        functools.partial(gather_kernel, sizes),
        out_shape=jax.ShapeDtypeStruct((count, 1, LANES), jnp.float32),
        in_specs=[pl.BlockSpec(memory_space=pltpu.VMEM)],
        out_specs=pl.BlockSpec(memory_space=pltpu.VMEM),
        scratch_shapes=[
            pltpu.VMEM((count, 1, LANES), jnp.float32),
            pltpu.SemaphoreType.DMA((2,)),
            pltpu.SemaphoreType.DMA((sizes[1] * sizes[2],)),
            pltpu.SemaphoreType.DMA((sizes[1] * sizes[2],)),
            pltpu.SemaphoreType.DMA((sizes[0],)),
            pltpu.SemaphoreType.DMA((sizes[0],)),
        ],
        compiler_params=pltpu.CompilerParams(collective_id=0, has_side_effects=True),
    )(tile)
    return rows[:, 0, :]


def pack(coarse, scalars):
    vecs = coarse.shape[0]
    row = jnp.zeros((LANES,), jnp.float32)
    row = row.at[:vecs].set(coarse)
    if scalars:
        row = row.at[vecs:vecs + len(scalars)].set(jnp.stack(scalars))
    return row[None]


def unpack(rows, vecs, count):
    coarse = rows[:, :vecs].reshape(-1)
    sums = jnp.sum(rows[:, vecs:vecs + count], axis=0)
    return coarse, [sums[i] for i in range(count)]


def shards(right_side, conductance, storage, dirichlet, basis, coarse_inverse):
    vecs = basis.shape[0]
    sides = (("gx", 0), ("gy", 1), ("gz", 2))
    free = 1.0 - dirichlet.astype(jnp.float32)
    stacked = jnp.concatenate([conductance, storage[None], free[None], right_side[None]], axis=0)
    wide = padded(stacked, (("gx", 1), ("gy", 2), ("gz", 3)), 3)
    cond_wide = wide[:3]
    free_wide = wide[4]
    storage_wide = wide[3]
    cond_box = wide[:3, 1:-1, 1:-1, 1:-1]
    storage_box = wide[3, 1:-1, 1:-1, 1:-1]
    free_box = wide[4, 1:-1, 1:-1, 1:-1]
    rhs_box0 = wide[5, 1:-1, 1:-1, 1:-1]
    box_cond = pad_cond(cond_box)
    box_diag = diagonal_of(box_cond, storage_box, free_box)
    cond_face = wide[:3, 2:-2, 2:-2, 2:-2]
    free_face = wide[4, 2:-2, 2:-2, 2:-2]

    def schwarz(rhs_box):
        return jacobi(rhs_box, box_cond, box_diag, storage_box, free_box)[2:-2, 2:-2, 2:-2]

    def precondition(rhs_box, residual, coarse_all):
        weights = jnp.dot(coarse_inverse, coarse_all, precision=lax.Precision.HIGHEST)
        return schwarz(rhs_box) + expand(basis, weights, residual)

    residual0 = right_side
    coarse0 = project(basis, residual0)
    coarse0_all, _ = unpack(gather_rows(pack(coarse0, [])), vecs, 0)
    z0 = precondition(rhs_box0, residual0, coarse0_all)
    near0 = padded(z0, sides, 3)
    inner = (slice(1, -1),) * 3
    image0_box = stencil(free_wide * near0, cond_wide, near0[inner], storage_wide[inner], free_wide[inner])
    image0 = image0_box[2:-2, 2:-2, 2:-2]
    coarse_img = project(basis, image0)
    rows = gather_rows(pack(coarse_img, [jnp.sum(residual0 * z0), jnp.sum(z0 * image0)]))
    coarse_img_all, (rz0, curve0) = unpack(rows, vecs, 2)
    alpha0 = rz0 / curve0
    solution1 = alpha0 * z0
    rhs_box1 = rhs_box0 - alpha0 * image0_box
    residual1 = rhs_box1[2:-2, 2:-2, 2:-2]
    coarse1_all = coarse0_all - alpha0 * coarse_img_all
    z1 = precondition(rhs_box1, residual1, coarse1_all)
    near1 = faces(z1)
    image_z1 = stencil(free_face * near1, cond_face, z1, storage, free)
    local = [
        jnp.sum(residual1 * z1),
        jnp.sum(z1 * image_z1),
        jnp.sum(z1 * image0),
        jnp.sum(z0 * image_z1),
    ]
    _, (rz1, zz, cross_a, cross_b) = unpack(gather_rows(pack(jnp.zeros((0,), jnp.float32), local)), 0, 4)
    beta = rz1 / rz0
    direction1 = z1 + beta * z0
    image1 = image_z1 + beta * image0
    curve1 = zz + beta * (cross_a + cross_b) + beta * beta * curve0
    alpha1 = rz1 / curve1
    solution2 = solution1 + alpha1 * direction1
    residual2 = residual1 - alpha1 * image1
    return (solution2, residual2)


def solution(mesh):
    placed = (
        P("gx", "gy", "gz"),
        P(None, "gx", "gy", "gz"),
        P("gx", "gy", "gz"),
        P("gx", "gy", "gz"),
        P(None, "gx", "gy", "gz"),
        P(("gx", "gy", "gz"), None),
    )
    return jax.shard_map(
        shards,
        mesh=mesh,
        in_specs=placed,
        out_specs=(P("gx", "gy", "gz"), P("gx", "gy", "gz")),
        check_vma=False,
    )
```

```python
import functools

import jax
import jax.numpy as jnp
from jax import lax
from jax.experimental import pallas as pl
from jax.experimental.pallas import tpu as pltpu
from jax.sharding import PartitionSpec as P

MESH_ID = pl.DeviceIdType.MESH

SWEEPS = 4
ITERS = 2


RELAX = 2.0 / 3.0


def padded(value, sides, width):
    for axis, dim in sides:
        count, length = (lax.axis_size(axis), value.shape[dim])
        up = [(i, (i + 1) % count) for i in range(count - 1)]
        down = [(j, i) for i, j in up]
        last = lax.slice_in_dim(value, length - width, length, axis=dim)
        leading = lax.slice_in_dim(value, 0, width, axis=dim)
        before = lax.ppermute(last, axis, up)
        after = lax.ppermute(leading, axis, down)
        value = jnp.concatenate([before, value, after], axis=dim)
    return value


def pad_cond(cond):
    return jnp.pad(cond, ((0, 0), (1, 1), (1, 1), (1, 1)))


def stencil(padded_free, padded_cond, field, storage, free):
    middle = padded_free[1:-1, 1:-1, 1:-1]
    total = storage * middle
    total = (
        total
        + padded_cond[0, 1:-1, 1:-1, 1:-1] * (middle - padded_free[2:, 1:-1, 1:-1])
        + padded_cond[0, :-2, 1:-1, 1:-1] * (middle - padded_free[:-2, 1:-1, 1:-1])
    )
    total = (
        total
        + padded_cond[1, 1:-1, 1:-1, 1:-1] * (middle - padded_free[1:-1, 2:, 1:-1])
        + padded_cond[1, 1:-1, :-2, 1:-1] * (middle - padded_free[1:-1, :-2, 1:-1])
    )
    total = (
        total
        + padded_cond[2, 1:-1, 1:-1, 1:-1] * (middle - padded_free[1:-1, 1:-1, 2:])
        + padded_cond[2, 1:-1, 1:-1, :-2] * (middle - padded_free[1:-1, 1:-1, :-2])
    )
    return free * total + (1.0 - free) * field


def diagonal_of(padded_cond, storage, free):
    total = storage + padded_cond[0, 1:-1, 1:-1, 1:-1] + padded_cond[0, :-2, 1:-1, 1:-1]
    total = total + padded_cond[1, 1:-1, 1:-1, 1:-1] + padded_cond[1, 1:-1, :-2, 1:-1]
    total = total + padded_cond[2, 1:-1, 1:-1, 1:-1] + padded_cond[2, 1:-1, 1:-1, :-2]
    return free * total + (1.0 - free)


def jacobi(rhs_box, padded_cond, diagonal, storage_box, free_box):
    guess = jnp.zeros_like(rhs_box)
    for sweep in range(SWEEPS):
        image = stencil(jnp.pad(free_box * guess, 1), padded_cond, guess, storage_box, free_box)
        guess = guess + RELAX * (rhs_box - image) / diagonal
    return guess


def project(basis, field):
    return jnp.sum(basis * field[None], axis=(1, 2, 3))


def expand(basis, weights, field):
    return jnp.sum(weights[:, None, None, None] * basis, axis=0)


LANES = 128


def faces(field):
    pieces = []
    for dim, axis in enumerate(("gx", "gy", "gz")):
        count, length = (lax.axis_size(axis), field.shape[dim])
        up = [(i, i + 1) for i in range(count - 1)]
        down = [(j, i) for i, j in up]
        before = lax.ppermute(lax.slice_in_dim(field, length - 1, length, axis=dim), axis, up)
        after = lax.ppermute(lax.slice_in_dim(field, 0, 1, axis=dim), axis, down)
        pieces.append((before, after))
    result = field
    for dim in range(3):
        before, after = pieces[dim]
        widths = [(1, 1) if d < dim else (0, 0) for d in range(3)]
        result = jnp.concatenate([jnp.pad(before, widths), result, jnp.pad(after, widths)], axis=dim)
    return result


def residual_rim(field):
    return padded(field, (("gx", 0), ("gy", 1), ("gz", 2)), 2)


def gather_kernel(sizes, row_ref, out_ref, held, local_sem, send1, recv1, send2, recv2):
    nx, ny, nz = sizes
    plane = ny * nz
    a = lax.axis_index("gx")
    b = lax.axis_index("gy")
    c = lax.axis_index("gz")
    me = (a * ny + b) * nz + c

    def in_plane(k):
        return (a, lax.rem(b + k // nz, ny), lax.rem(c + k % nz, nz))

    def along_x(k):
        return (lax.rem(a + k, nx), b, c)

    peers = [in_plane(k) for k in range(1, plane)] + [along_x(k) for k in range(1, nx)]
    barrier = pltpu.get_barrier_semaphore()
    for peer in peers:
        pl.semaphore_signal(barrier, inc=1, device_id=peer, device_id_type=MESH_ID)
    pl.semaphore_wait(barrier, len(peers))

    own = pltpu.make_async_copy(row_ref, held.at[pl.ds(me, 1)], local_sem.at[0])
    own.start()
    sent = []

    def stage(src_of, first_of, count, size, toward, send, recv):
        for k in range(1, size):
            copy = pltpu.make_async_remote_copy(
                src_ref=src_of(0),
                dst_ref=held.at[pl.ds(first_of(0), count)],
                send_sem=send.at[k],
                recv_sem=recv.at[k],
                device_id=toward(k),
                device_id_type=MESH_ID,
            )
            copy.start()
            sent.append(copy)
        for k in range(1, size):
            pltpu.make_async_remote_copy(
                src_ref=src_of(k),
                dst_ref=held.at[pl.ds(first_of(k), count)],
                send_sem=send.at[k],
                recv_sem=recv.at[k],
                device_id=toward(size - k),
                device_id_type=MESH_ID,
            ).wait_recv()

    def p_first(k):
        return (a * ny + lax.rem(b + ny - k // nz, ny)) * nz + lax.rem(c + nz - k % nz, nz)

    stage(lambda k: row_ref, p_first, 1, plane, in_plane, send1, recv1)
    own.wait()
    x_first = lambda k: lax.rem(a + nx - k, nx) * plane
    stage(lambda k: held.at[pl.ds(x_first(k), plane)], x_first, plane, nx, along_x, send2, recv2)
    for copy in sent:
        copy.wait_send()
    final = pltpu.make_async_copy(held, out_ref, local_sem.at[1])
    final.start()
    final.wait()


def gather_rows(row):
    sizes = (lax.axis_size("gx"), lax.axis_size("gy"), lax.axis_size("gz"))
    count = sizes[0] * sizes[1] * sizes[2]
    tile = row[:, None, :]
    rows = pl.pallas_call(
        functools.partial(gather_kernel, sizes),
        out_shape=jax.ShapeDtypeStruct((count, 1, LANES), jnp.float32),
        in_specs=[pl.BlockSpec(memory_space=pltpu.VMEM)],
        out_specs=pl.BlockSpec(memory_space=pltpu.VMEM),
        scratch_shapes=[
            pltpu.VMEM((count, 1, LANES), jnp.float32),
            pltpu.SemaphoreType.DMA((2,)),
            pltpu.SemaphoreType.DMA((sizes[1] * sizes[2],)),
            pltpu.SemaphoreType.DMA((sizes[1] * sizes[2],)),
            pltpu.SemaphoreType.DMA((sizes[0],)),
            pltpu.SemaphoreType.DMA((sizes[0],)),
        ],
        compiler_params=pltpu.CompilerParams(collective_id=0, has_side_effects=True),
    )(tile)
    return rows[:, 0, :]


def pack(coarse, scalars):
    vecs = coarse.shape[0]
    row = jnp.zeros((LANES,), jnp.float32)
    row = row.at[:vecs].set(coarse)
    if scalars:
        row = row.at[vecs:vecs + len(scalars)].set(jnp.stack(scalars))
    return row[None]


def unpack(rows, vecs, count):
    coarse = rows[:, :vecs].reshape(-1)
    sums = jnp.sum(rows[:, vecs:vecs + count], axis=0)
    return coarse, [sums[i] for i in range(count)]


def shards(right_side, conductance, storage, dirichlet, basis, coarse_inverse):
    vecs = basis.shape[0]
    sides = (("gx", 0), ("gy", 1), ("gz", 2))
    free = 1.0 - dirichlet.astype(jnp.float32)
    stacked = jnp.concatenate([conductance, storage[None], free[None], right_side[None]], axis=0)
    wide = padded(stacked, (("gx", 1), ("gy", 2), ("gz", 3)), 3)
    cond_wide = wide[:3]
    free_wide = wide[4]
    storage_wide = wide[3]
    cond_box = wide[:3, 1:-1, 1:-1, 1:-1]
    storage_box = wide[3, 1:-1, 1:-1, 1:-1]
    free_box = wide[4, 1:-1, 1:-1, 1:-1]
    rhs_box0 = wide[5, 1:-1, 1:-1, 1:-1]
    box_cond = pad_cond(cond_box)
    box_diag = diagonal_of(box_cond, storage_box, free_box)
    cond_face = wide[:3, 2:-2, 2:-2, 2:-2]
    free_face = wide[4, 2:-2, 2:-2, 2:-2]

    def schwarz(rhs_box):
        return jacobi(rhs_box, box_cond, box_diag, storage_box, free_box)[2:-2, 2:-2, 2:-2]

    def precondition(rhs_box, residual, coarse_all):
        weights = jnp.dot(coarse_inverse, coarse_all, precision=lax.Precision.HIGHEST)
        return schwarz(rhs_box) + expand(basis, weights, residual)

    residual0 = right_side
    coarse0 = project(basis, residual0)
    coarse0_all, _ = unpack(gather_rows(pack(coarse0, [])), vecs, 0)
    z0 = precondition(rhs_box0, residual0, coarse0_all)
    near0 = padded(z0, sides, 3)
    inner = (slice(1, -1),) * 3
    image0_box = stencil(free_wide * near0, cond_wide, near0[inner], storage_wide[inner], free_wide[inner])
    image0 = image0_box[2:-2, 2:-2, 2:-2]
    coarse_img = project(basis, image0)
    rows = gather_rows(pack(coarse_img, [jnp.sum(residual0 * z0), jnp.sum(z0 * image0)]))
    coarse_img_all, (rz0, curve0) = unpack(rows, vecs, 2)
    alpha0 = rz0 / curve0
    solution1 = alpha0 * z0
    rhs_box1 = rhs_box0 - alpha0 * image0_box
    residual1 = rhs_box1[2:-2, 2:-2, 2:-2]
    coarse1_all = coarse0_all - alpha0 * coarse_img_all
    z1 = precondition(rhs_box1, residual1, coarse1_all)
    near1 = faces(z1)
    image_z1 = stencil(free_face * near1, cond_face, z1, storage, free)
    local = [
        jnp.sum(residual1 * z1),
        jnp.sum(z1 * image_z1),
        jnp.sum(z1 * image0),
        jnp.sum(z0 * image_z1),
    ]
    _, (rz1, zz, cross_a, cross_b) = unpack(gather_rows(pack(jnp.zeros((0,), jnp.float32), local)), 0, 4)
    beta = rz1 / rz0
    direction1 = z1 + beta * z0
    image1 = image_z1 + beta * image0
    curve1 = zz + beta * (cross_a + cross_b) + beta * beta * curve0
    alpha1 = rz1 / curve1
    solution2 = solution1 + alpha1 * direction1
    residual2 = residual1 - alpha1 * image1
    return (solution2, residual2)


def solution(mesh):
    placed = (
        P("gx", "gy", "gz"),
        P(None, "gx", "gy", "gz"),
        P("gx", "gy", "gz"),
        P("gx", "gy", "gz"),
        P(None, "gx", "gy", "gz"),
        P(("gx", "gy", "gz"), None),
    )
    return jax.shard_map(
        shards,
        mesh=mesh,
        in_specs=placed,
        out_specs=(P("gx", "gy", "gz"), P("gx", "gy", "gz")),
        check_vma=False,
    )
```

```python
import functools

import jax
import jax.numpy as jnp
from jax import lax
from jax.experimental import pallas as pl
from jax.experimental.pallas import tpu as pltpu
from jax.sharding import PartitionSpec as P

MESH_ID = pl.DeviceIdType.MESH

SWEEPS = 4
ITERS = 2


RELAX = 2.0 / 3.0


def padded(value, sides, width):
    for axis, dim in sides:
        count, length = (lax.axis_size(axis), value.shape[dim])
        up = [(i, (i + 1) % count) for i in range(count - 1)]
        down = [(j, i) for i, j in up]
        last = lax.slice_in_dim(value, length - width, length, axis=dim)
        leading = lax.slice_in_dim(value, 0, width, axis=dim)
        before = lax.ppermute(last, axis, up)
        after = lax.ppermute(leading, axis, down)
        value = jnp.concatenate([before, value, after], axis=dim)
    return value


def pad_cond(cond):
    return jnp.pad(cond, ((0, 0), (1, 1), (1, 1), (1, 1)))


def stencil(padded_free, padded_cond, field, storage, free):
    middle = padded_free[1:-1, 1:-1, 1:-1]
    total = storage * middle
    total = (
        total
        + padded_cond[0, 1:-1, 1:-1, 1:-1] * (middle - padded_free[2:, 1:-1, 1:-1])
        + padded_cond[0, :-2, 1:-1, 1:-1] * (middle - padded_free[:-2, 1:-1, 1:-1])
    )
    total = (
        total
        + padded_cond[1, 1:-1, 1:-1, 1:-1] * (middle - padded_free[1:-1, 2:, 1:-1])
        + padded_cond[1, 1:-1, :-2, 1:-1] * (middle - padded_free[1:-1, :-2, 1:-1])
    )
    total = (
        total
        + padded_cond[2, 1:-1, 1:-1, 1:-1] * (middle - padded_free[1:-1, 1:-1, 2:])
        + padded_cond[2, 1:-1, 1:-1, :-2] * (middle - padded_free[1:-1, 1:-1, :-2])
    )
    return free * total + (1.0 - free) * field


def diagonal_of(padded_cond, storage, free):
    total = storage + padded_cond[0, 1:-1, 1:-1, 1:-1] + padded_cond[0, :-2, 1:-1, 1:-1]
    total = total + padded_cond[1, 1:-1, 1:-1, 1:-1] + padded_cond[1, 1:-1, :-2, 1:-1]
    total = total + padded_cond[2, 1:-1, 1:-1, 1:-1] + padded_cond[2, 1:-1, 1:-1, :-2]
    return free * total + (1.0 - free)


def jacobi(rhs_box, padded_cond, diagonal, storage_box, free_box):
    guess = jnp.zeros_like(rhs_box)
    for sweep in range(SWEEPS):
        image = stencil(jnp.pad(free_box * guess, 1), padded_cond, guess, storage_box, free_box)
        guess = guess + RELAX * (rhs_box - image) / diagonal
    return guess


def project(basis, field):
    return jnp.sum(basis * field[None], axis=(1, 2, 3))


def expand(basis, weights, field):
    return jnp.sum(weights[:, None, None, None] * basis, axis=0)


LANES = 128


def faces(field):
    pieces = []
    for dim, axis in enumerate(("gx", "gy", "gz")):
        count, length = (lax.axis_size(axis), field.shape[dim])
        up = [(i, i + 1) for i in range(count - 1)]
        down = [(j, i) for i, j in up]
        before = lax.ppermute(lax.slice_in_dim(field, length - 1, length, axis=dim), axis, up)
        after = lax.ppermute(lax.slice_in_dim(field, 0, 1, axis=dim), axis, down)
        pieces.append((before, after))
    result = field
    for dim in range(3):
        before, after = pieces[dim]
        widths = [(1, 1) if d < dim else (0, 0) for d in range(3)]
        result = jnp.concatenate([jnp.pad(before, widths), result, jnp.pad(after, widths)], axis=dim)
    return result


def residual_rim(field):
    return padded(field, (("gx", 0), ("gy", 1), ("gz", 2)), 2)


def gather_kernel(sizes, row_ref, out_ref, held, local_sem, send1, recv1, send2, recv2):
    nx, ny, nz = sizes
    plane = ny * nz
    a = lax.axis_index("gx")
    b = lax.axis_index("gy")
    c = lax.axis_index("gz")
    me = (a * ny + b) * nz + c

    def in_plane(k):
        return (a, lax.rem(b + k // nz, ny), lax.rem(c + k % nz, nz))

    def along_x(k):
        return (lax.rem(a + k, nx), b, c)

    peers = [in_plane(k) for k in range(1, plane)] + [along_x(k) for k in range(1, nx)]
    barrier = pltpu.get_barrier_semaphore()
    for peer in peers:
        pl.semaphore_signal(barrier, inc=1, device_id=peer, device_id_type=MESH_ID)
    pl.semaphore_wait(barrier, len(peers))

    own = pltpu.make_async_copy(row_ref, held.at[pl.ds(me, 1)], local_sem.at[0])
    own.start()
    sent = []

    def stage(src_of, first_of, count, size, toward, send, recv):
        for k in range(1, size):
            copy = pltpu.make_async_remote_copy(
                src_ref=src_of(0),
                dst_ref=held.at[pl.ds(first_of(0), count)],
                send_sem=send.at[k],
                recv_sem=recv.at[k],
                device_id=toward(k),
                device_id_type=MESH_ID,
            )
            copy.start()
            sent.append(copy)
        for k in range(1, size):
            pltpu.make_async_remote_copy(
                src_ref=src_of(k),
                dst_ref=held.at[pl.ds(first_of(k), count)],
                send_sem=send.at[k],
                recv_sem=recv.at[k],
                device_id=toward(size - k),
                device_id_type=MESH_ID,
            ).wait_recv()

    def p_first(k):
        return (a * ny + lax.rem(b + ny - k // nz, ny)) * nz + lax.rem(c + nz - k % nz, nz)

    stage(lambda k: row_ref, p_first, 1, plane, in_plane, send1, recv1)
    own.wait()
    x_first = lambda k: lax.rem(a + nx - k, nx) * plane
    stage(lambda k: held.at[pl.ds(x_first(k), plane)], x_first, plane, nx, along_x, send2, recv2)
    for copy in sent:
        copy.wait_send()
    final = pltpu.make_async_copy(held, out_ref, local_sem.at[1])
    final.start()
    final.wait()


def gather_rows(row):
    sizes = (lax.axis_size("gx"), lax.axis_size("gy"), lax.axis_size("gz"))
    count = sizes[0] * sizes[1] * sizes[2]
    tile = row[:, None, :]
    rows = pl.pallas_call(
        functools.partial(gather_kernel, sizes),
        out_shape=jax.ShapeDtypeStruct((count, 1, LANES), jnp.float32),
        in_specs=[pl.BlockSpec(memory_space=pltpu.VMEM)],
        out_specs=pl.BlockSpec(memory_space=pltpu.VMEM),
        scratch_shapes=[
            pltpu.VMEM((count, 1, LANES), jnp.float32),
            pltpu.SemaphoreType.DMA((2,)),
            pltpu.SemaphoreType.DMA((sizes[1] * sizes[2],)),
            pltpu.SemaphoreType.DMA((sizes[1] * sizes[2],)),
            pltpu.SemaphoreType.DMA((sizes[0],)),
            pltpu.SemaphoreType.DMA((sizes[0],)),
        ],
        compiler_params=pltpu.CompilerParams(collective_id=0, has_side_effects=True),
    )(tile)
    return rows[:, 0, :]


def pack(coarse, scalars):
    vecs = coarse.shape[0]
    row = jnp.zeros((LANES,), jnp.float32)
    row = row.at[:vecs].set(coarse)
    if scalars:
        row = row.at[vecs:vecs + len(scalars)].set(jnp.stack(scalars))
    return row[None]


def unpack(rows, vecs, count):
    coarse = rows[:, :vecs].reshape(-1)
    sums = jnp.sum(rows[:, vecs:vecs + count], axis=0)
    return coarse, [sums[i] for i in range(count)]


def shards(right_side, conductance, storage, dirichlet, basis, coarse_inverse):
    vecs = basis.shape[0]
    sides = (("gx", 0), ("gy", 1), ("gz", 2))
    free = 1.0 - dirichlet.astype(jnp.float32)
    stacked = jnp.concatenate([conductance, storage[None], free[None], right_side[None]], axis=0)
    wide = padded(stacked, (("gz", 3), ("gx", 1), ("gy", 2)), 3)
    cond_wide = wide[:3]
    free_wide = wide[4]
    storage_wide = wide[3]
    cond_box = wide[:3, 1:-1, 1:-1, 1:-1]
    storage_box = wide[3, 1:-1, 1:-1, 1:-1]
    free_box = wide[4, 1:-1, 1:-1, 1:-1]
    rhs_box0 = wide[5, 1:-1, 1:-1, 1:-1]
    box_cond = pad_cond(cond_box)
    box_diag = diagonal_of(box_cond, storage_box, free_box)
    cond_face = wide[:3, 2:-2, 2:-2, 2:-2]
    free_face = wide[4, 2:-2, 2:-2, 2:-2]

    def schwarz(rhs_box):
        return jacobi(rhs_box, box_cond, box_diag, storage_box, free_box)[2:-2, 2:-2, 2:-2]

    def precondition(rhs_box, residual, coarse_all):
        weights = jnp.dot(coarse_inverse, coarse_all, precision=lax.Precision.HIGHEST)
        return schwarz(rhs_box) + expand(basis, weights, residual)

    residual0 = right_side
    coarse0 = project(basis, residual0)
    coarse0_all, _ = unpack(gather_rows(pack(coarse0, [])), vecs, 0)
    z0 = precondition(rhs_box0, residual0, coarse0_all)
    near0 = padded(z0, (("gz", 2), ("gx", 0), ("gy", 1)), 3)
    inner = (slice(1, -1),) * 3
    image0_box = stencil(free_wide * near0, cond_wide, near0[inner], storage_wide[inner], free_wide[inner])
    image0 = image0_box[2:-2, 2:-2, 2:-2]
    coarse_img = project(basis, image0)
    rows = gather_rows(pack(coarse_img, [jnp.sum(residual0 * z0), jnp.sum(z0 * image0)]))
    coarse_img_all, (rz0, curve0) = unpack(rows, vecs, 2)
    alpha0 = rz0 / curve0
    solution1 = alpha0 * z0
    rhs_box1 = rhs_box0 - alpha0 * image0_box
    residual1 = rhs_box1[2:-2, 2:-2, 2:-2]
    coarse1_all = coarse0_all - alpha0 * coarse_img_all
    z1 = precondition(rhs_box1, residual1, coarse1_all)
    near1 = faces(z1)
    image_z1 = stencil(free_face * near1, cond_face, z1, storage, free)
    local = [
        jnp.sum(residual1 * z1),
        jnp.sum(z1 * image_z1),
        jnp.sum(z1 * image0),
        jnp.sum(z0 * image_z1),
    ]
    _, (rz1, zz, cross_a, cross_b) = unpack(gather_rows(pack(jnp.zeros((0,), jnp.float32), local)), 0, 4)
    beta = rz1 / rz0
    direction1 = z1 + beta * z0
    image1 = image_z1 + beta * image0
    curve1 = zz + beta * (cross_a + cross_b) + beta * beta * curve0
    alpha1 = rz1 / curve1
    solution2 = solution1 + alpha1 * direction1
    residual2 = residual1 - alpha1 * image1
    return (solution2, residual2)


def solution(mesh):
    placed = (
        P("gx", "gy", "gz"),
        P(None, "gx", "gy", "gz"),
        P("gx", "gy", "gz"),
        P("gx", "gy", "gz"),
        P(None, "gx", "gy", "gz"),
        P(("gx", "gy", "gz"), None),
    )
    return jax.shard_map(
        shards,
        mesh=mesh,
        in_specs=placed,
        out_specs=(P("gx", "gy", "gz"), P("gx", "gy", "gz")),
        check_vma=False,
    )
```

```python
import functools

import jax
import jax.numpy as jnp
from jax import lax
from jax.experimental import pallas as pl
from jax.experimental.pallas import tpu as pltpu
from jax.sharding import PartitionSpec as P

MESH_ID = pl.DeviceIdType.MESH

SWEEPS = 4
ITERS = 2


RELAX = 2.0 / 3.0


def padded(value, sides, width):
    for axis, dim in sides:
        count, length = (lax.axis_size(axis), value.shape[dim])
        up = [(i, (i + 1) % count) for i in range(count - 1)]
        down = [(j, i) for i, j in up]
        last = lax.slice_in_dim(value, length - width, length, axis=dim)
        leading = lax.slice_in_dim(value, 0, width, axis=dim)
        before = lax.ppermute(last, axis, up)
        after = lax.ppermute(leading, axis, down)
        value = jnp.concatenate([before, value, after], axis=dim)
    return value


def pad_cond(cond):
    return jnp.pad(cond, ((0, 0), (1, 1), (1, 1), (1, 1)))


def stencil(padded_free, padded_cond, field, storage, free):
    middle = padded_free[1:-1, 1:-1, 1:-1]
    total = storage * middle
    total = (
        total
        + padded_cond[0, 1:-1, 1:-1, 1:-1] * (middle - padded_free[2:, 1:-1, 1:-1])
        + padded_cond[0, :-2, 1:-1, 1:-1] * (middle - padded_free[:-2, 1:-1, 1:-1])
    )
    total = (
        total
        + padded_cond[1, 1:-1, 1:-1, 1:-1] * (middle - padded_free[1:-1, 2:, 1:-1])
        + padded_cond[1, 1:-1, :-2, 1:-1] * (middle - padded_free[1:-1, :-2, 1:-1])
    )
    total = (
        total
        + padded_cond[2, 1:-1, 1:-1, 1:-1] * (middle - padded_free[1:-1, 1:-1, 2:])
        + padded_cond[2, 1:-1, 1:-1, :-2] * (middle - padded_free[1:-1, 1:-1, :-2])
    )
    return free * total + (1.0 - free) * field


def diagonal_of(padded_cond, storage, free):
    total = storage + padded_cond[0, 1:-1, 1:-1, 1:-1] + padded_cond[0, :-2, 1:-1, 1:-1]
    total = total + padded_cond[1, 1:-1, 1:-1, 1:-1] + padded_cond[1, 1:-1, :-2, 1:-1]
    total = total + padded_cond[2, 1:-1, 1:-1, 1:-1] + padded_cond[2, 1:-1, 1:-1, :-2]
    return free * total + (1.0 - free)


def jacobi(rhs_box, padded_cond, diagonal, storage_box, free_box):
    guess = jnp.zeros_like(rhs_box)
    for sweep in range(SWEEPS):
        image = stencil(jnp.pad(free_box * guess, 1), padded_cond, guess, storage_box, free_box)
        guess = guess + RELAX * (rhs_box - image) / diagonal
    return guess


def project(basis, field):
    return jnp.sum(basis * field[None], axis=(1, 2, 3))


def expand(basis, weights, field):
    return jnp.sum(weights[:, None, None, None] * basis, axis=0)


LANES = 128


def face_kernel(sizes, ins_outs_held, *refs):
    count = 6
    ins, outs, held = refs[:count], refs[count:2 * count], refs[2 * count:3 * count]
    send_sem, recv_sem, local_sem = refs[3 * count:]
    here = [lax.axis_index(name) for name in ("gx", "gy", "gz")]

    def toward(dim, step):
        return tuple(lax.rem(i + step + n, n) if d == dim else i for d, (i, n) in enumerate(zip(here, sizes)))

    barrier = pltpu.get_barrier_semaphore()
    for dim in range(3):
        for step in (-1, 1):
            pl.semaphore_signal(barrier, inc=1, device_id=toward(dim, step), device_id_type=MESH_ID)
    pl.semaphore_wait(barrier, count)
    sent = []
    for dim in range(3):
        for side, step in ((0, -1), (1, 1)):
            i = 2 * dim + side
            j = 2 * dim + 1 - side
            copy = pltpu.make_async_remote_copy(
                src_ref=ins[i],
                dst_ref=held[j],
                send_sem=send_sem.at[i],
                recv_sem=recv_sem.at[j],
                device_id=toward(dim, step),
                device_id_type=MESH_ID,
            )
            copy.start()
            sent.append(copy)
    for dim in range(3):
        for side, step in ((0, -1), (1, 1)):
            j = 2 * dim + side
            i = 2 * dim + 1 - side
            pltpu.make_async_remote_copy(
                src_ref=ins[i],
                dst_ref=held[j],
                send_sem=send_sem.at[i],
                recv_sem=recv_sem.at[j],
                device_id=toward(dim, step),
                device_id_type=MESH_ID,
            ).wait_recv()
    for copy in sent:
        copy.wait_send()
    local = []
    for j in range(count):
        copy = pltpu.make_async_copy(held[j], outs[j], local_sem.at[j])
        copy.start()
        local.append(copy)
    for copy in local:
        copy.wait()


def faces(field):
    names = ("gx", "gy", "gz")
    sizes = tuple(lax.axis_size(name) for name in names)
    here = [lax.axis_index(name) for name in names]
    slabs = []
    for dim in range(3):
        length = field.shape[dim]
        slabs.append(lax.slice_in_dim(field, 0, 1, axis=dim))
        slabs.append(lax.slice_in_dim(field, length - 1, length, axis=dim))
    spec = pl.BlockSpec(memory_space=pltpu.VMEM)
    got = pl.pallas_call(
        functools.partial(face_kernel, sizes, None),
        out_shape=[jax.ShapeDtypeStruct(s.shape, s.dtype) for s in slabs],
        in_specs=[spec] * 6,
        out_specs=[spec] * 6,
        scratch_shapes=[pltpu.VMEM(s.shape, s.dtype) for s in slabs] + [pltpu.SemaphoreType.DMA((6,))] * 3,
        compiler_params=pltpu.CompilerParams(collective_id=1, has_side_effects=True),
    )(*slabs)
    result = field
    for dim in range(3):
        below = jnp.where(here[dim] > 0, got[2 * dim], 0.0)
        above = jnp.where(here[dim] < sizes[dim] - 1, got[2 * dim + 1], 0.0)
        widths = [(1, 1) if d < dim else (0, 0) for d in range(3)]
        below = jnp.pad(below, widths)
        above = jnp.pad(above, widths)
        result = jnp.concatenate([below, result, above], axis=dim)
    return result


def residual_rim(field):
    return padded(field, (("gx", 0), ("gy", 1), ("gz", 2)), 2)


def gather_kernel(sizes, row_ref, out_ref, held, local_sem, send1, recv1, send2, recv2):
    nx, ny, nz = sizes
    plane = ny * nz
    a = lax.axis_index("gx")
    b = lax.axis_index("gy")
    c = lax.axis_index("gz")
    me = (a * ny + b) * nz + c

    def in_plane(k):
        return (a, lax.rem(b + k // nz, ny), lax.rem(c + k % nz, nz))

    def along_x(k):
        return (lax.rem(a + k, nx), b, c)

    peers = [in_plane(k) for k in range(1, plane)] + [along_x(k) for k in range(1, nx)]
    barrier = pltpu.get_barrier_semaphore()
    for peer in peers:
        pl.semaphore_signal(barrier, inc=1, device_id=peer, device_id_type=MESH_ID)
    pl.semaphore_wait(barrier, len(peers))

    own = pltpu.make_async_copy(row_ref, held.at[pl.ds(me, 1)], local_sem.at[0])
    own.start()
    sent = []

    def stage(src_of, first_of, count, size, toward, send, recv):
        for k in range(1, size):
            copy = pltpu.make_async_remote_copy(
                src_ref=src_of(0),
                dst_ref=held.at[pl.ds(first_of(0), count)],
                send_sem=send.at[k],
                recv_sem=recv.at[k],
                device_id=toward(k),
                device_id_type=MESH_ID,
            )
            copy.start()
            sent.append(copy)
        for k in range(1, size):
            pltpu.make_async_remote_copy(
                src_ref=src_of(k),
                dst_ref=held.at[pl.ds(first_of(k), count)],
                send_sem=send.at[k],
                recv_sem=recv.at[k],
                device_id=toward(size - k),
                device_id_type=MESH_ID,
            ).wait_recv()

    def p_first(k):
        return (a * ny + lax.rem(b + ny - k // nz, ny)) * nz + lax.rem(c + nz - k % nz, nz)

    stage(lambda k: row_ref, p_first, 1, plane, in_plane, send1, recv1)
    own.wait()
    x_first = lambda k: lax.rem(a + nx - k, nx) * plane
    stage(lambda k: held.at[pl.ds(x_first(k), plane)], x_first, plane, nx, along_x, send2, recv2)
    for copy in sent:
        copy.wait_send()
    final = pltpu.make_async_copy(held, out_ref, local_sem.at[1])
    final.start()
    final.wait()


def gather_rows(row):
    sizes = (lax.axis_size("gx"), lax.axis_size("gy"), lax.axis_size("gz"))
    count = sizes[0] * sizes[1] * sizes[2]
    tile = row[:, None, :]
    rows = pl.pallas_call(
        functools.partial(gather_kernel, sizes),
        out_shape=jax.ShapeDtypeStruct((count, 1, LANES), jnp.float32),
        in_specs=[pl.BlockSpec(memory_space=pltpu.VMEM)],
        out_specs=pl.BlockSpec(memory_space=pltpu.VMEM),
        scratch_shapes=[
            pltpu.VMEM((count, 1, LANES), jnp.float32),
            pltpu.SemaphoreType.DMA((2,)),
            pltpu.SemaphoreType.DMA((sizes[1] * sizes[2],)),
            pltpu.SemaphoreType.DMA((sizes[1] * sizes[2],)),
            pltpu.SemaphoreType.DMA((sizes[0],)),
            pltpu.SemaphoreType.DMA((sizes[0],)),
        ],
        compiler_params=pltpu.CompilerParams(collective_id=0, has_side_effects=True),
    )(tile)
    return rows[:, 0, :]


def pack(coarse, scalars):
    vecs = coarse.shape[0]
    row = jnp.zeros((LANES,), jnp.float32)
    row = row.at[:vecs].set(coarse)
    if scalars:
        row = row.at[vecs:vecs + len(scalars)].set(jnp.stack(scalars))
    return row[None]


def unpack(rows, vecs, count):
    coarse = rows[:, :vecs].reshape(-1)
    sums = jnp.sum(rows[:, vecs:vecs + count], axis=0)
    return coarse, [sums[i] for i in range(count)]


def shards(right_side, conductance, storage, dirichlet, basis, coarse_inverse):
    vecs = basis.shape[0]
    sides = (("gx", 0), ("gy", 1), ("gz", 2))
    free = 1.0 - dirichlet.astype(jnp.float32)
    stacked = jnp.concatenate([conductance, storage[None], free[None], right_side[None]], axis=0)
    wide = padded(stacked, (("gz", 3), ("gx", 1), ("gy", 2)), 3)
    cond_wide = wide[:3]
    free_wide = wide[4]
    storage_wide = wide[3]
    cond_box = wide[:3, 1:-1, 1:-1, 1:-1]
    storage_box = wide[3, 1:-1, 1:-1, 1:-1]
    free_box = wide[4, 1:-1, 1:-1, 1:-1]
    rhs_box0 = wide[5, 1:-1, 1:-1, 1:-1]
    box_cond = pad_cond(cond_box)
    box_diag = diagonal_of(box_cond, storage_box, free_box)
    cond_face = wide[:3, 2:-2, 2:-2, 2:-2]
    free_face = wide[4, 2:-2, 2:-2, 2:-2]

    def schwarz(rhs_box):
        return jacobi(rhs_box, box_cond, box_diag, storage_box, free_box)[2:-2, 2:-2, 2:-2]

    def precondition(rhs_box, residual, coarse_all):
        weights = jnp.dot(coarse_inverse, coarse_all, precision=lax.Precision.HIGHEST)
        return schwarz(rhs_box) + expand(basis, weights, residual)

    residual0 = right_side
    coarse0 = project(basis, residual0)
    coarse0_all, _ = unpack(gather_rows(pack(coarse0, [])), vecs, 0)
    z0 = precondition(rhs_box0, residual0, coarse0_all)
    near0 = padded(z0, (("gz", 2), ("gx", 0), ("gy", 1)), 3)
    inner = (slice(1, -1),) * 3
    image0_box = stencil(free_wide * near0, cond_wide, near0[inner], storage_wide[inner], free_wide[inner])
    image0 = image0_box[2:-2, 2:-2, 2:-2]
    coarse_img = project(basis, image0)
    rows = gather_rows(pack(coarse_img, [jnp.sum(residual0 * z0), jnp.sum(z0 * image0)]))
    coarse_img_all, (rz0, curve0) = unpack(rows, vecs, 2)
    alpha0 = rz0 / curve0
    solution1 = alpha0 * z0
    rhs_box1 = rhs_box0 - alpha0 * image0_box
    residual1 = rhs_box1[2:-2, 2:-2, 2:-2]
    coarse1_all = coarse0_all - alpha0 * coarse_img_all
    z1 = precondition(rhs_box1, residual1, coarse1_all)
    near1 = faces(z1)
    image_z1 = stencil(free_face * near1, cond_face, z1, storage, free)
    local = [
        jnp.sum(residual1 * z1),
        jnp.sum(z1 * image_z1),
        jnp.sum(z1 * image0),
        jnp.sum(z0 * image_z1),
    ]
    _, (rz1, zz, cross_a, cross_b) = unpack(gather_rows(pack(jnp.zeros((0,), jnp.float32), local)), 0, 4)
    beta = rz1 / rz0
    direction1 = z1 + beta * z0
    image1 = image_z1 + beta * image0
    curve1 = zz + beta * (cross_a + cross_b) + beta * beta * curve0
    alpha1 = rz1 / curve1
    solution2 = solution1 + alpha1 * direction1
    residual2 = residual1 - alpha1 * image1
    return (solution2, residual2)


def solution(mesh):
    placed = (
        P("gx", "gy", "gz"),
        P(None, "gx", "gy", "gz"),
        P("gx", "gy", "gz"),
        P("gx", "gy", "gz"),
        P(None, "gx", "gy", "gz"),
        P(("gx", "gy", "gz"), None),
    )
    return jax.shard_map(
        shards,
        mesh=mesh,
        in_specs=placed,
        out_specs=(P("gx", "gy", "gz"), P("gx", "gy", "gz")),
        check_vma=False,
    )
```

```python
import functools

import jax
import jax.numpy as jnp
from jax import lax
from jax.experimental import pallas as pl
from jax.experimental.pallas import tpu as pltpu
from jax.sharding import PartitionSpec as P

MESH_ID = pl.DeviceIdType.MESH

SWEEPS = 4
ITERS = 2


RELAX = 2.0 / 3.0


def padded(value, sides, width):
    for axis, dim in sides:
        count, length = (lax.axis_size(axis), value.shape[dim])
        up = [(i, (i + 1) % count) for i in range(count - 1)]
        down = [(j, i) for i, j in up]
        last = lax.slice_in_dim(value, length - width, length, axis=dim)
        leading = lax.slice_in_dim(value, 0, width, axis=dim)
        before = lax.ppermute(last, axis, up)
        after = lax.ppermute(leading, axis, down)
        value = jnp.concatenate([before, value, after], axis=dim)
    return value


def pad_cond(cond):
    return jnp.pad(cond, ((0, 0), (1, 1), (1, 1), (1, 1)))


def stencil(padded_free, padded_cond, field, storage, free):
    middle = padded_free[1:-1, 1:-1, 1:-1]
    total = storage * middle
    total = (
        total
        + padded_cond[0, 1:-1, 1:-1, 1:-1] * (middle - padded_free[2:, 1:-1, 1:-1])
        + padded_cond[0, :-2, 1:-1, 1:-1] * (middle - padded_free[:-2, 1:-1, 1:-1])
    )
    total = (
        total
        + padded_cond[1, 1:-1, 1:-1, 1:-1] * (middle - padded_free[1:-1, 2:, 1:-1])
        + padded_cond[1, 1:-1, :-2, 1:-1] * (middle - padded_free[1:-1, :-2, 1:-1])
    )
    total = (
        total
        + padded_cond[2, 1:-1, 1:-1, 1:-1] * (middle - padded_free[1:-1, 1:-1, 2:])
        + padded_cond[2, 1:-1, 1:-1, :-2] * (middle - padded_free[1:-1, 1:-1, :-2])
    )
    return free * total + (1.0 - free) * field


def diagonal_of(padded_cond, storage, free):
    total = storage + padded_cond[0, 1:-1, 1:-1, 1:-1] + padded_cond[0, :-2, 1:-1, 1:-1]
    total = total + padded_cond[1, 1:-1, 1:-1, 1:-1] + padded_cond[1, 1:-1, :-2, 1:-1]
    total = total + padded_cond[2, 1:-1, 1:-1, 1:-1] + padded_cond[2, 1:-1, 1:-1, :-2]
    return free * total + (1.0 - free)


def jacobi(rhs_box, padded_cond, diagonal, storage_box, free_box):
    guess = jnp.zeros_like(rhs_box)
    for sweep in range(SWEEPS):
        image = stencil(jnp.pad(free_box * guess, 1), padded_cond, guess, storage_box, free_box)
        guess = guess + RELAX * (rhs_box - image) / diagonal
    return guess


def project(basis, field):
    return jnp.sum(basis * field[None], axis=(1, 2, 3))


def expand(basis, weights, field):
    return jnp.sum(weights[:, None, None, None] * basis, axis=0)


LANES = 128


def faces(field):
    pieces = []
    for dim, axis in enumerate(("gx", "gy", "gz")):
        count, length = (lax.axis_size(axis), field.shape[dim])
        up = [(i, i + 1) for i in range(count - 1)]
        down = [(j, i) for i, j in up]
        before = lax.ppermute(lax.slice_in_dim(field, length - 1, length, axis=dim), axis, up)
        after = lax.ppermute(lax.slice_in_dim(field, 0, 1, axis=dim), axis, down)
        pieces.append((before, after))
    result = field
    for dim in range(3):
        before, after = pieces[dim]
        widths = [(1, 1) if d < dim else (0, 0) for d in range(3)]
        result = jnp.concatenate([jnp.pad(before, widths), result, jnp.pad(after, widths)], axis=dim)
    return result


def residual_rim(field):
    return padded(field, (("gx", 0), ("gy", 1), ("gz", 2)), 2)


def gather_kernel(sizes, row_ref, out_ref, held, local_sem, send1, recv1, send2, recv2):
    nx, ny, nz = sizes
    plane = ny * nz
    a = lax.axis_index("gx")
    b = lax.axis_index("gy")
    c = lax.axis_index("gz")
    me = (a * ny + b) * nz + c

    def in_plane(k):
        return (a, lax.rem(b + k // nz, ny), lax.rem(c + k % nz, nz))

    def along_x(k):
        return (lax.rem(a + k, nx), b, c)

    peers = [in_plane(k) for k in range(1, plane)] + [along_x(k) for k in range(1, nx)]
    barrier = pltpu.get_barrier_semaphore()
    for peer in peers:
        pl.semaphore_signal(barrier, inc=1, device_id=peer, device_id_type=MESH_ID)
    pl.semaphore_wait(barrier, len(peers))

    own = pltpu.make_async_copy(row_ref, held.at[pl.ds(me, 1)], local_sem.at[0])
    own.start()
    sent = []

    def stage(src_of, first_of, count, size, toward, send, recv):
        for k in range(1, size):
            copy = pltpu.make_async_remote_copy(
                src_ref=src_of(0),
                dst_ref=held.at[pl.ds(first_of(0), count)],
                send_sem=send.at[k],
                recv_sem=recv.at[k],
                device_id=toward(k),
                device_id_type=MESH_ID,
            )
            copy.start()
            sent.append(copy)
        for k in range(1, size):
            pltpu.make_async_remote_copy(
                src_ref=src_of(k),
                dst_ref=held.at[pl.ds(first_of(k), count)],
                send_sem=send.at[k],
                recv_sem=recv.at[k],
                device_id=toward(size - k),
                device_id_type=MESH_ID,
            ).wait_recv()

    def p_first(k):
        return (a * ny + lax.rem(b + ny - k // nz, ny)) * nz + lax.rem(c + nz - k % nz, nz)

    stage(lambda k: row_ref, p_first, 1, plane, in_plane, send1, recv1)
    own.wait()
    x_first = lambda k: lax.rem(a + nx - k, nx) * plane
    stage(lambda k: held.at[pl.ds(x_first(k), plane)], x_first, plane, nx, along_x, send2, recv2)
    for copy in sent:
        copy.wait_send()
    final = pltpu.make_async_copy(held, out_ref, local_sem.at[1])
    final.start()
    final.wait()


def gather_rows(row):
    sizes = (lax.axis_size("gx"), lax.axis_size("gy"), lax.axis_size("gz"))
    count = sizes[0] * sizes[1] * sizes[2]
    tile = row[:, None, :]
    rows = pl.pallas_call(
        functools.partial(gather_kernel, sizes),
        out_shape=jax.ShapeDtypeStruct((count, 1, LANES), jnp.float32),
        in_specs=[pl.BlockSpec(memory_space=pltpu.VMEM)],
        out_specs=pl.BlockSpec(memory_space=pltpu.VMEM),
        scratch_shapes=[
            pltpu.VMEM((count, 1, LANES), jnp.float32),
            pltpu.SemaphoreType.DMA((2,)),
            pltpu.SemaphoreType.DMA((sizes[1] * sizes[2],)),
            pltpu.SemaphoreType.DMA((sizes[1] * sizes[2],)),
            pltpu.SemaphoreType.DMA((sizes[0],)),
            pltpu.SemaphoreType.DMA((sizes[0],)),
        ],
        compiler_params=pltpu.CompilerParams(collective_id=0, has_side_effects=True),
    )(tile)
    return rows[:, 0, :]


def pack(coarse, scalars):
    vecs = coarse.shape[0]
    row = jnp.zeros((LANES,), jnp.float32)
    row = row.at[:vecs].set(coarse)
    if scalars:
        row = row.at[vecs:vecs + len(scalars)].set(jnp.stack(scalars))
    return row[None]


def unpack(rows, vecs, count):
    coarse = rows[:, :vecs].reshape(-1)
    sums = jnp.sum(rows[:, vecs:vecs + count], axis=0)
    return coarse, [sums[i] for i in range(count)]


def shards(right_side, conductance, storage, dirichlet, basis, coarse_inverse):
    vecs = basis.shape[0]
    sides = (("gx", 0), ("gy", 1), ("gz", 2))
    free = 1.0 - dirichlet.astype(jnp.float32)
    stacked = jnp.concatenate([conductance, storage[None], free[None], right_side[None]], axis=0)
    residual0 = right_side
    coarse0 = project(basis, residual0)
    rows0 = gather_rows(pack(coarse0, []))
    rows0, stacked = lax.optimization_barrier((rows0, stacked))
    coarse0_all, _ = unpack(rows0, vecs, 0)
    wide = padded(stacked, (("gz", 3), ("gx", 1), ("gy", 2)), 3)
    cond_wide = wide[:3]
    free_wide = wide[4]
    storage_wide = wide[3]
    cond_box = wide[:3, 1:-1, 1:-1, 1:-1]
    storage_box = wide[3, 1:-1, 1:-1, 1:-1]
    free_box = wide[4, 1:-1, 1:-1, 1:-1]
    rhs_box0 = wide[5, 1:-1, 1:-1, 1:-1]
    box_cond = pad_cond(cond_box)
    box_diag = diagonal_of(box_cond, storage_box, free_box)
    cond_face = wide[:3, 2:-2, 2:-2, 2:-2]
    free_face = wide[4, 2:-2, 2:-2, 2:-2]

    def schwarz(rhs_box):
        return jacobi(rhs_box, box_cond, box_diag, storage_box, free_box)[2:-2, 2:-2, 2:-2]

    def precondition(rhs_box, residual, coarse_all):
        weights = jnp.dot(coarse_inverse, coarse_all, precision=lax.Precision.HIGHEST)
        return schwarz(rhs_box) + expand(basis, weights, residual)

    z0 = precondition(rhs_box0, residual0, coarse0_all)
    near0 = padded(z0, (("gz", 2), ("gx", 0), ("gy", 1)), 3)
    inner = (slice(1, -1),) * 3
    image0_box = stencil(free_wide * near0, cond_wide, near0[inner], storage_wide[inner], free_wide[inner])
    image0 = image0_box[2:-2, 2:-2, 2:-2]
    coarse_img = project(basis, image0)
    rows = gather_rows(pack(coarse_img, [jnp.sum(residual0 * z0), jnp.sum(z0 * image0)]))
    coarse_img_all, (rz0, curve0) = unpack(rows, vecs, 2)
    alpha0 = rz0 / curve0
    solution1 = alpha0 * z0
    rhs_box1 = rhs_box0 - alpha0 * image0_box
    residual1 = rhs_box1[2:-2, 2:-2, 2:-2]
    coarse1_all = coarse0_all - alpha0 * coarse_img_all
    z1 = precondition(rhs_box1, residual1, coarse1_all)
    near1 = faces(z1)
    image_z1 = stencil(free_face * near1, cond_face, z1, storage, free)
    local = [
        jnp.sum(residual1 * z1),
        jnp.sum(z1 * image_z1),
        jnp.sum(z1 * image0),
        jnp.sum(z0 * image_z1),
    ]
    _, (rz1, zz, cross_a, cross_b) = unpack(gather_rows(pack(jnp.zeros((0,), jnp.float32), local)), 0, 4)
    beta = rz1 / rz0
    direction1 = z1 + beta * z0
    image1 = image_z1 + beta * image0
    curve1 = zz + beta * (cross_a + cross_b) + beta * beta * curve0
    alpha1 = rz1 / curve1
    solution2 = solution1 + alpha1 * direction1
    residual2 = residual1 - alpha1 * image1
    return (solution2, residual2)


def solution(mesh):
    placed = (
        P("gx", "gy", "gz"),
        P(None, "gx", "gy", "gz"),
        P("gx", "gy", "gz"),
        P("gx", "gy", "gz"),
        P(None, "gx", "gy", "gz"),
        P(("gx", "gy", "gz"), None),
    )
    return jax.shard_map(
        shards,
        mesh=mesh,
        in_specs=placed,
        out_specs=(P("gx", "gy", "gz"), P("gx", "gy", "gz")),
        check_vma=False,
    )
```

```python
import functools

import jax
import jax.numpy as jnp
from jax import lax
from jax.experimental import pallas as pl
from jax.experimental.pallas import tpu as pltpu
from jax.sharding import PartitionSpec as P

MESH_ID = pl.DeviceIdType.MESH

SWEEPS = 4
ITERS = 2


RELAX = 2.0 / 3.0


def padded(value, sides, width):
    for axis, dim in sides:
        count, length = (lax.axis_size(axis), value.shape[dim])
        up = [(i, (i + 1) % count) for i in range(count - 1)]
        down = [(j, i) for i, j in up]
        last = lax.slice_in_dim(value, length - width, length, axis=dim)
        leading = lax.slice_in_dim(value, 0, width, axis=dim)
        before = lax.ppermute(last, axis, up)
        after = lax.ppermute(leading, axis, down)
        value = jnp.concatenate([before, value, after], axis=dim)
    return value


def pad_cond(cond):
    return jnp.pad(cond, ((0, 0), (1, 1), (1, 1), (1, 1)))


def stencil(padded_free, padded_cond, field, storage, free):
    middle = padded_free[1:-1, 1:-1, 1:-1]
    total = storage * middle
    total = (
        total
        + padded_cond[0, 1:-1, 1:-1, 1:-1] * (middle - padded_free[2:, 1:-1, 1:-1])
        + padded_cond[0, :-2, 1:-1, 1:-1] * (middle - padded_free[:-2, 1:-1, 1:-1])
    )
    total = (
        total
        + padded_cond[1, 1:-1, 1:-1, 1:-1] * (middle - padded_free[1:-1, 2:, 1:-1])
        + padded_cond[1, 1:-1, :-2, 1:-1] * (middle - padded_free[1:-1, :-2, 1:-1])
    )
    total = (
        total
        + padded_cond[2, 1:-1, 1:-1, 1:-1] * (middle - padded_free[1:-1, 1:-1, 2:])
        + padded_cond[2, 1:-1, 1:-1, :-2] * (middle - padded_free[1:-1, 1:-1, :-2])
    )
    return free * total + (1.0 - free) * field


def diagonal_of(padded_cond, storage, free):
    total = storage + padded_cond[0, 1:-1, 1:-1, 1:-1] + padded_cond[0, :-2, 1:-1, 1:-1]
    total = total + padded_cond[1, 1:-1, 1:-1, 1:-1] + padded_cond[1, 1:-1, :-2, 1:-1]
    total = total + padded_cond[2, 1:-1, 1:-1, 1:-1] + padded_cond[2, 1:-1, 1:-1, :-2]
    return free * total + (1.0 - free)


def jacobi(rhs_box, padded_cond, diagonal, storage_box, free_box):
    trims = [max(0, 2 - (SWEEPS - 1 - s)) for s in range(SWEEPS)]

    def cut(value, t):
        return value[t:value.shape[0] - t, t:value.shape[1] - t, t:value.shape[2] - t]

    guess = RELAX * cut(rhs_box, trims[0]) / cut(diagonal, trims[0])
    for sweep in range(1, SWEEPS):
        t, before = trims[sweep], trims[sweep - 1]
        if t == before:
            near = jnp.pad(cut(free_box, t) * guess, 1)
            field = guess
        else:
            near = cut(free_box, before) * guess
            field = cut(guess, t - before)
        cond = padded_cond[:, t:padded_cond.shape[1] - t, t:padded_cond.shape[2] - t, t:padded_cond.shape[3] - t]
        image = stencil(near, cond, field, cut(storage_box, t), cut(free_box, t))
        guess = field + RELAX * (cut(rhs_box, t) - image) / cut(diagonal, t)
    return cut(guess, 2 - trims[-1])


def project(basis, field):
    return jnp.sum(basis * field[None], axis=(1, 2, 3))


def expand(basis, weights, field):
    return jnp.sum(weights[:, None, None, None] * basis, axis=0)


LANES = 128


def faces(field):
    pieces = []
    for dim, axis in enumerate(("gx", "gy", "gz")):
        count, length = (lax.axis_size(axis), field.shape[dim])
        up = [(i, i + 1) for i in range(count - 1)]
        down = [(j, i) for i, j in up]
        before = lax.ppermute(lax.slice_in_dim(field, length - 1, length, axis=dim), axis, up)
        after = lax.ppermute(lax.slice_in_dim(field, 0, 1, axis=dim), axis, down)
        pieces.append((before, after))
    result = field
    for dim in range(3):
        before, after = pieces[dim]
        widths = [(1, 1) if d < dim else (0, 0) for d in range(3)]
        result = jnp.concatenate([jnp.pad(before, widths), result, jnp.pad(after, widths)], axis=dim)
    return result


def residual_rim(field):
    return padded(field, (("gx", 0), ("gy", 1), ("gz", 2)), 2)


def gather_kernel(sizes, row_ref, out_ref, held, local_sem, send1, recv1, send2, recv2):
    nx, ny, nz = sizes
    plane = ny * nz
    a = lax.axis_index("gx")
    b = lax.axis_index("gy")
    c = lax.axis_index("gz")
    me = (a * ny + b) * nz + c

    def in_plane(k):
        return (a, lax.rem(b + k // nz, ny), lax.rem(c + k % nz, nz))

    def along_x(k):
        return (lax.rem(a + k, nx), b, c)

    peers = [in_plane(k) for k in range(1, plane)] + [along_x(k) for k in range(1, nx)]
    barrier = pltpu.get_barrier_semaphore()
    for peer in peers:
        pl.semaphore_signal(barrier, inc=1, device_id=peer, device_id_type=MESH_ID)
    pl.semaphore_wait(barrier, len(peers))

    own = pltpu.make_async_copy(row_ref, held.at[pl.ds(me, 1)], local_sem.at[0])
    own.start()
    sent = []

    def stage(src_of, first_of, count, size, toward, send, recv):
        for k in range(1, size):
            copy = pltpu.make_async_remote_copy(
                src_ref=src_of(0),
                dst_ref=held.at[pl.ds(first_of(0), count)],
                send_sem=send.at[k],
                recv_sem=recv.at[k],
                device_id=toward(k),
                device_id_type=MESH_ID,
            )
            copy.start()
            sent.append(copy)
        for k in range(1, size):
            pltpu.make_async_remote_copy(
                src_ref=src_of(k),
                dst_ref=held.at[pl.ds(first_of(k), count)],
                send_sem=send.at[k],
                recv_sem=recv.at[k],
                device_id=toward(size - k),
                device_id_type=MESH_ID,
            ).wait_recv()

    def p_first(k):
        return (a * ny + lax.rem(b + ny - k // nz, ny)) * nz + lax.rem(c + nz - k % nz, nz)

    stage(lambda k: row_ref, p_first, 1, plane, in_plane, send1, recv1)
    own.wait()
    x_first = lambda k: lax.rem(a + nx - k, nx) * plane
    stage(lambda k: held.at[pl.ds(x_first(k), plane)], x_first, plane, nx, along_x, send2, recv2)
    for copy in sent:
        copy.wait_send()
    final = pltpu.make_async_copy(held, out_ref, local_sem.at[1])
    final.start()
    final.wait()


def gather_rows(row):
    sizes = (lax.axis_size("gx"), lax.axis_size("gy"), lax.axis_size("gz"))
    count = sizes[0] * sizes[1] * sizes[2]
    tile = row[:, None, :]
    rows = pl.pallas_call(
        functools.partial(gather_kernel, sizes),
        out_shape=jax.ShapeDtypeStruct((count, 1, LANES), jnp.float32),
        in_specs=[pl.BlockSpec(memory_space=pltpu.VMEM)],
        out_specs=pl.BlockSpec(memory_space=pltpu.VMEM),
        scratch_shapes=[
            pltpu.VMEM((count, 1, LANES), jnp.float32),
            pltpu.SemaphoreType.DMA((2,)),
            pltpu.SemaphoreType.DMA((sizes[1] * sizes[2],)),
            pltpu.SemaphoreType.DMA((sizes[1] * sizes[2],)),
            pltpu.SemaphoreType.DMA((sizes[0],)),
            pltpu.SemaphoreType.DMA((sizes[0],)),
        ],
        compiler_params=pltpu.CompilerParams(collective_id=0, has_side_effects=True),
    )(tile)
    return rows[:, 0, :]


def pack(coarse, scalars):
    vecs = coarse.shape[0]
    row = jnp.zeros((LANES,), jnp.float32)
    row = row.at[:vecs].set(coarse)
    if scalars:
        row = row.at[vecs:vecs + len(scalars)].set(jnp.stack(scalars))
    return row[None]


def unpack(rows, vecs, count):
    coarse = rows[:, :vecs].reshape(-1)
    sums = jnp.sum(rows[:, vecs:vecs + count], axis=0)
    return coarse, [sums[i] for i in range(count)]


def shards(right_side, conductance, storage, dirichlet, basis, coarse_inverse):
    vecs = basis.shape[0]
    sides = (("gx", 0), ("gy", 1), ("gz", 2))
    free = 1.0 - dirichlet.astype(jnp.float32)
    stacked = jnp.concatenate([conductance, storage[None], free[None], right_side[None]], axis=0)
    wide = padded(stacked, (("gz", 3), ("gx", 1), ("gy", 2)), 3)
    cond_wide = wide[:3]
    free_wide = wide[4]
    storage_wide = wide[3]
    cond_box = wide[:3, 1:-1, 1:-1, 1:-1]
    storage_box = wide[3, 1:-1, 1:-1, 1:-1]
    free_box = wide[4, 1:-1, 1:-1, 1:-1]
    rhs_box0 = wide[5, 1:-1, 1:-1, 1:-1]
    box_cond = pad_cond(cond_box)
    box_diag = diagonal_of(box_cond, storage_box, free_box)
    cond_face = wide[:3, 2:-2, 2:-2, 2:-2]
    free_face = wide[4, 2:-2, 2:-2, 2:-2]

    def schwarz(rhs_box):
        return jacobi(rhs_box, box_cond, box_diag, storage_box, free_box)

    def precondition(rhs_box, residual, coarse_all):
        weights = jnp.dot(coarse_inverse, coarse_all, precision=lax.Precision.HIGHEST)
        return schwarz(rhs_box) + expand(basis, weights, residual)

    residual0 = right_side
    coarse0 = project(basis, residual0)
    coarse0_all, _ = unpack(gather_rows(pack(coarse0, [])), vecs, 0)
    z0 = precondition(rhs_box0, residual0, coarse0_all)
    near0 = padded(z0, (("gz", 2), ("gx", 0), ("gy", 1)), 3)
    inner = (slice(1, -1),) * 3
    image0_box = stencil(free_wide * near0, cond_wide, near0[inner], storage_wide[inner], free_wide[inner])
    image0 = image0_box[2:-2, 2:-2, 2:-2]
    coarse_img = project(basis, image0)
    rows = gather_rows(pack(coarse_img, [jnp.sum(residual0 * z0), jnp.sum(z0 * image0)]))
    coarse_img_all, (rz0, curve0) = unpack(rows, vecs, 2)
    alpha0 = rz0 / curve0
    solution1 = alpha0 * z0
    rhs_box1 = rhs_box0 - alpha0 * image0_box
    residual1 = rhs_box1[2:-2, 2:-2, 2:-2]
    coarse1_all = coarse0_all - alpha0 * coarse_img_all
    z1 = precondition(rhs_box1, residual1, coarse1_all)
    near1 = faces(z1)
    image_z1 = stencil(free_face * near1, cond_face, z1, storage, free)
    local = [
        jnp.sum(residual1 * z1),
        jnp.sum(z1 * image_z1),
        jnp.sum(z1 * image0),
        jnp.sum(z0 * image_z1),
    ]
    _, (rz1, zz, cross_a, cross_b) = unpack(gather_rows(pack(jnp.zeros((0,), jnp.float32), local)), 0, 4)
    beta = rz1 / rz0
    direction1 = z1 + beta * z0
    image1 = image_z1 + beta * image0
    curve1 = zz + beta * (cross_a + cross_b) + beta * beta * curve0
    alpha1 = rz1 / curve1
    solution2 = solution1 + alpha1 * direction1
    residual2 = residual1 - alpha1 * image1
    return (solution2, residual2)


def solution(mesh):
    placed = (
        P("gx", "gy", "gz"),
        P(None, "gx", "gy", "gz"),
        P("gx", "gy", "gz"),
        P("gx", "gy", "gz"),
        P(None, "gx", "gy", "gz"),
        P(("gx", "gy", "gz"), None),
    )
    return jax.shard_map(
        shards,
        mesh=mesh,
        in_specs=placed,
        out_specs=(P("gx", "gy", "gz"), P("gx", "gy", "gz")),
        check_vma=False,
    )
```

```python
import functools

import jax
import jax.numpy as jnp
from jax import lax
from jax.experimental import pallas as pl
from jax.experimental.pallas import tpu as pltpu
from jax.sharding import PartitionSpec as P

MESH_ID = pl.DeviceIdType.MESH

SWEEPS = 4
ITERS = 2


RELAX = 2.0 / 3.0


def padded(value, sides, width):
    for axis, dim in sides:
        count, length = (lax.axis_size(axis), value.shape[dim])
        up = [(i, (i + 1) % count) for i in range(count - 1)]
        down = [(j, i) for i, j in up]
        last = lax.slice_in_dim(value, length - width, length, axis=dim)
        leading = lax.slice_in_dim(value, 0, width, axis=dim)
        before = lax.ppermute(last, axis, up)
        after = lax.ppermute(leading, axis, down)
        value = jnp.concatenate([before, value, after], axis=dim)
    return value


def pad_cond(cond):
    return jnp.pad(cond, ((0, 0), (1, 1), (1, 1), (1, 1)))


def stencil(padded_free, padded_cond, field, storage, free):
    middle = padded_free[1:-1, 1:-1, 1:-1]
    total = storage * middle
    total = (
        total
        + padded_cond[0, 1:-1, 1:-1, 1:-1] * (middle - padded_free[2:, 1:-1, 1:-1])
        + padded_cond[0, :-2, 1:-1, 1:-1] * (middle - padded_free[:-2, 1:-1, 1:-1])
    )
    total = (
        total
        + padded_cond[1, 1:-1, 1:-1, 1:-1] * (middle - padded_free[1:-1, 2:, 1:-1])
        + padded_cond[1, 1:-1, :-2, 1:-1] * (middle - padded_free[1:-1, :-2, 1:-1])
    )
    total = (
        total
        + padded_cond[2, 1:-1, 1:-1, 1:-1] * (middle - padded_free[1:-1, 1:-1, 2:])
        + padded_cond[2, 1:-1, 1:-1, :-2] * (middle - padded_free[1:-1, 1:-1, :-2])
    )
    return free * total + (1.0 - free) * field


def diagonal_of(padded_cond, storage, free):
    total = storage + padded_cond[0, 1:-1, 1:-1, 1:-1] + padded_cond[0, :-2, 1:-1, 1:-1]
    total = total + padded_cond[1, 1:-1, 1:-1, 1:-1] + padded_cond[1, 1:-1, :-2, 1:-1]
    total = total + padded_cond[2, 1:-1, 1:-1, 1:-1] + padded_cond[2, 1:-1, 1:-1, :-2]
    return free * total + (1.0 - free)


def jacobi(rhs_box, padded_cond, diagonal, storage_box, free_box):
    guess = RELAX * rhs_box / diagonal
    for sweep in range(1, SWEEPS):
        image = stencil(jnp.pad(free_box * guess, 1), padded_cond, guess, storage_box, free_box)
        guess = guess + RELAX * (rhs_box - image) / diagonal
    return guess


def project(basis, field):
    return jnp.sum(basis * field[None], axis=(1, 2, 3))


def expand(basis, weights, field):
    return jnp.sum(weights[:, None, None, None] * basis, axis=0)


LANES = 128


def faces(field):
    pieces = []
    for dim, axis in enumerate(("gx", "gy", "gz")):
        count, length = (lax.axis_size(axis), field.shape[dim])
        up = [(i, i + 1) for i in range(count - 1)]
        down = [(j, i) for i, j in up]
        before = lax.ppermute(lax.slice_in_dim(field, length - 1, length, axis=dim), axis, up)
        after = lax.ppermute(lax.slice_in_dim(field, 0, 1, axis=dim), axis, down)
        pieces.append((before, after))
    result = field
    for dim in range(3):
        before, after = pieces[dim]
        widths = [(1, 1) if d < dim else (0, 0) for d in range(3)]
        result = jnp.concatenate([jnp.pad(before, widths), result, jnp.pad(after, widths)], axis=dim)
    return result


def residual_rim(field):
    return padded(field, (("gx", 0), ("gy", 1), ("gz", 2)), 2)


def gather_kernel(sizes, row_ref, out_ref, held, local_sem, send1, recv1, send2, recv2):
    nx, ny, nz = sizes
    plane = ny * nz
    a = lax.axis_index("gx")
    b = lax.axis_index("gy")
    c = lax.axis_index("gz")
    me = (a * ny + b) * nz + c

    def in_plane(k):
        return (a, lax.rem(b + k // nz, ny), lax.rem(c + k % nz, nz))

    def along_x(k):
        return (lax.rem(a + k, nx), b, c)

    peers = [in_plane(k) for k in range(1, plane)] + [along_x(k) for k in range(1, nx)]
    barrier = pltpu.get_barrier_semaphore()
    for peer in peers:
        pl.semaphore_signal(barrier, inc=1, device_id=peer, device_id_type=MESH_ID)
    pl.semaphore_wait(barrier, len(peers))

    own = pltpu.make_async_copy(row_ref, held.at[pl.ds(me, 1)], local_sem.at[0])
    own.start()
    sent = []

    def stage(src_of, first_of, count, size, toward, send, recv):
        for k in range(1, size):
            copy = pltpu.make_async_remote_copy(
                src_ref=src_of(0),
                dst_ref=held.at[pl.ds(first_of(0), count)],
                send_sem=send.at[k],
                recv_sem=recv.at[k],
                device_id=toward(k),
                device_id_type=MESH_ID,
            )
            copy.start()
            sent.append(copy)
        for k in range(1, size):
            pltpu.make_async_remote_copy(
                src_ref=src_of(k),
                dst_ref=held.at[pl.ds(first_of(k), count)],
                send_sem=send.at[k],
                recv_sem=recv.at[k],
                device_id=toward(size - k),
                device_id_type=MESH_ID,
            ).wait_recv()

    def p_first(k):
        return (a * ny + lax.rem(b + ny - k // nz, ny)) * nz + lax.rem(c + nz - k % nz, nz)

    stage(lambda k: row_ref, p_first, 1, plane, in_plane, send1, recv1)
    own.wait()
    x_first = lambda k: lax.rem(a + nx - k, nx) * plane
    stage(lambda k: held.at[pl.ds(x_first(k), plane)], x_first, plane, nx, along_x, send2, recv2)
    for copy in sent:
        copy.wait_send()
    final = pltpu.make_async_copy(held, out_ref, local_sem.at[1])
    final.start()
    final.wait()


def gather_rows(row):
    sizes = (lax.axis_size("gx"), lax.axis_size("gy"), lax.axis_size("gz"))
    count = sizes[0] * sizes[1] * sizes[2]
    tile = row[:, None, :]
    rows = pl.pallas_call(
        functools.partial(gather_kernel, sizes),
        out_shape=jax.ShapeDtypeStruct((count, 1, LANES), jnp.float32),
        in_specs=[pl.BlockSpec(memory_space=pltpu.VMEM)],
        out_specs=pl.BlockSpec(memory_space=pltpu.VMEM),
        scratch_shapes=[
            pltpu.VMEM((count, 1, LANES), jnp.float32),
            pltpu.SemaphoreType.DMA((2,)),
            pltpu.SemaphoreType.DMA((sizes[1] * sizes[2],)),
            pltpu.SemaphoreType.DMA((sizes[1] * sizes[2],)),
            pltpu.SemaphoreType.DMA((sizes[0],)),
            pltpu.SemaphoreType.DMA((sizes[0],)),
        ],
        compiler_params=pltpu.CompilerParams(collective_id=0, has_side_effects=True),
    )(tile)
    return rows[:, 0, :]


def pack(coarse, scalars):
    vecs = coarse.shape[0]
    row = jnp.zeros((LANES,), jnp.float32)
    row = row.at[:vecs].set(coarse)
    if scalars:
        row = row.at[vecs:vecs + len(scalars)].set(jnp.stack(scalars))
    return row[None]


def unpack(rows, vecs, count):
    coarse = rows[:, :vecs].reshape(-1)
    sums = jnp.sum(rows[:, vecs:vecs + count], axis=0)
    return coarse, [sums[i] for i in range(count)]


def shards(right_side, conductance, storage, dirichlet, basis, coarse_inverse):
    vecs = basis.shape[0]
    sides = (("gx", 0), ("gy", 1), ("gz", 2))
    free = 1.0 - dirichlet.astype(jnp.float32)
    stacked = jnp.concatenate([conductance, storage[None], free[None], right_side[None]], axis=0)
    wide = padded(stacked, (("gz", 3), ("gx", 1), ("gy", 2)), 3)
    cond_wide = wide[:3]
    free_wide = wide[4]
    storage_wide = wide[3]
    cond_box = wide[:3, 1:-1, 1:-1, 1:-1]
    storage_box = wide[3, 1:-1, 1:-1, 1:-1]
    free_box = wide[4, 1:-1, 1:-1, 1:-1]
    rhs_box0 = wide[5, 1:-1, 1:-1, 1:-1]
    box_cond = pad_cond(cond_box)
    box_diag = diagonal_of(box_cond, storage_box, free_box)
    cond_face = wide[:3, 2:-2, 2:-2, 2:-2]
    free_face = wide[4, 2:-2, 2:-2, 2:-2]

    def schwarz(rhs_box):
        return jacobi(rhs_box, box_cond, box_diag, storage_box, free_box)[2:-2, 2:-2, 2:-2]

    def precondition(rhs_box, residual, coarse_all):
        weights = jnp.dot(coarse_inverse, coarse_all, precision=lax.Precision.HIGHEST)
        return schwarz(rhs_box) + expand(basis, weights, residual)

    residual0 = right_side
    coarse0 = project(basis, residual0)
    coarse0_all, _ = unpack(gather_rows(pack(coarse0, [])), vecs, 0)
    z0 = precondition(rhs_box0, residual0, coarse0_all)
    near0 = padded(z0, (("gz", 2), ("gx", 0), ("gy", 1)), 3)
    inner = (slice(1, -1),) * 3
    image0_box = stencil(free_wide * near0, cond_wide, near0[inner], storage_wide[inner], free_wide[inner])
    image0 = image0_box[2:-2, 2:-2, 2:-2]
    coarse_img = project(basis, image0)
    rows = gather_rows(pack(coarse_img, [jnp.sum(residual0 * z0), jnp.sum(z0 * image0)]))
    coarse_img_all, (rz0, curve0) = unpack(rows, vecs, 2)
    alpha0 = rz0 / curve0
    solution1 = alpha0 * z0
    rhs_box1 = rhs_box0 - alpha0 * image0_box
    residual1 = rhs_box1[2:-2, 2:-2, 2:-2]
    coarse1_all = coarse0_all - alpha0 * coarse_img_all
    z1 = precondition(rhs_box1, residual1, coarse1_all)
    near1 = faces(z1)
    image_z1 = stencil(free_face * near1, cond_face, z1, storage, free)
    local = [
        jnp.sum(residual1 * z1),
        jnp.sum(z1 * image_z1),
        jnp.sum(z1 * image0),
        jnp.sum(z0 * image_z1),
    ]
    _, (rz1, zz, cross_a, cross_b) = unpack(gather_rows(pack(jnp.zeros((0,), jnp.float32), local)), 0, 4)
    beta = rz1 / rz0
    direction1 = z1 + beta * z0
    image1 = image_z1 + beta * image0
    curve1 = zz + beta * (cross_a + cross_b) + beta * beta * curve0
    alpha1 = rz1 / curve1
    solution2 = solution1 + alpha1 * direction1
    residual2 = residual1 - alpha1 * image1
    return (solution2, residual2)


def solution(mesh):
    placed = (
        P("gx", "gy", "gz"),
        P(None, "gx", "gy", "gz"),
        P("gx", "gy", "gz"),
        P("gx", "gy", "gz"),
        P(None, "gx", "gy", "gz"),
        P(("gx", "gy", "gz"), None),
    )
    return jax.shard_map(
        shards,
        mesh=mesh,
        in_specs=placed,
        out_specs=(P("gx", "gy", "gz"), P("gx", "gy", "gz")),
        check_vma=False,
    )
```

```python
import functools

import jax
import jax.numpy as jnp
from jax import lax
from jax.experimental import pallas as pl
from jax.experimental.pallas import tpu as pltpu
from jax.sharding import PartitionSpec as P

MESH_ID = pl.DeviceIdType.MESH

SWEEPS = 4
ITERS = 2


RELAX = 2.0 / 3.0


def padded(value, sides, width):
    for axis, dim in sides:
        count, length = (lax.axis_size(axis), value.shape[dim])
        up = [(i, (i + 1) % count) for i in range(count - 1)]
        down = [(j, i) for i, j in up]
        last = lax.slice_in_dim(value, length - width, length, axis=dim)
        leading = lax.slice_in_dim(value, 0, width, axis=dim)
        before = lax.ppermute(last, axis, up)
        after = lax.ppermute(leading, axis, down)
        value = jnp.concatenate([before, value, after], axis=dim)
    return value


def pad_cond(cond):
    return jnp.pad(cond, ((0, 0), (1, 1), (1, 1), (1, 1)))


def stencil(padded_free, padded_cond, field, storage, free):
    middle = padded_free[1:-1, 1:-1, 1:-1]
    total = storage * middle
    total = (
        total
        + padded_cond[0, 1:-1, 1:-1, 1:-1] * (middle - padded_free[2:, 1:-1, 1:-1])
        + padded_cond[0, :-2, 1:-1, 1:-1] * (middle - padded_free[:-2, 1:-1, 1:-1])
    )
    total = (
        total
        + padded_cond[1, 1:-1, 1:-1, 1:-1] * (middle - padded_free[1:-1, 2:, 1:-1])
        + padded_cond[1, 1:-1, :-2, 1:-1] * (middle - padded_free[1:-1, :-2, 1:-1])
    )
    total = (
        total
        + padded_cond[2, 1:-1, 1:-1, 1:-1] * (middle - padded_free[1:-1, 1:-1, 2:])
        + padded_cond[2, 1:-1, 1:-1, :-2] * (middle - padded_free[1:-1, 1:-1, :-2])
    )
    return free * total + (1.0 - free) * field


def diagonal_of(padded_cond, storage, free):
    total = storage + padded_cond[0, 1:-1, 1:-1, 1:-1] + padded_cond[0, :-2, 1:-1, 1:-1]
    total = total + padded_cond[1, 1:-1, 1:-1, 1:-1] + padded_cond[1, 1:-1, :-2, 1:-1]
    total = total + padded_cond[2, 1:-1, 1:-1, 1:-1] + padded_cond[2, 1:-1, 1:-1, :-2]
    return free * total + (1.0 - free)


def jacobi(rhs_box, padded_cond, diagonal, storage_box, free_box):
    def sweep(step, guess):
        image = stencil(jnp.pad(free_box * guess, 1), padded_cond, guess, storage_box, free_box)
        return guess + RELAX * (rhs_box - image) / diagonal

    return lax.fori_loop(0, SWEEPS, sweep, jnp.zeros_like(rhs_box))


def project(basis, field):
    return jnp.sum(basis * field[None], axis=(1, 2, 3))


def expand(basis, weights, field):
    return jnp.sum(weights[:, None, None, None] * basis, axis=0)


LANES = 128


def faces(field):
    pieces = []
    for dim, axis in enumerate(("gx", "gy", "gz")):
        count, length = (lax.axis_size(axis), field.shape[dim])
        up = [(i, i + 1) for i in range(count - 1)]
        down = [(j, i) for i, j in up]
        before = lax.ppermute(lax.slice_in_dim(field, length - 1, length, axis=dim), axis, up)
        after = lax.ppermute(lax.slice_in_dim(field, 0, 1, axis=dim), axis, down)
        pieces.append((before, after))
    result = field
    for dim in range(3):
        before, after = pieces[dim]
        widths = [(1, 1) if d < dim else (0, 0) for d in range(3)]
        result = jnp.concatenate([jnp.pad(before, widths), result, jnp.pad(after, widths)], axis=dim)
    return result


def residual_rim(field):
    return padded(field, (("gx", 0), ("gy", 1), ("gz", 2)), 2)


def gather_kernel(sizes, row_ref, out_ref, held, local_sem, send1, recv1, send2, recv2):
    nx, ny, nz = sizes
    plane = ny * nz
    a = lax.axis_index("gx")
    b = lax.axis_index("gy")
    c = lax.axis_index("gz")
    me = (a * ny + b) * nz + c

    def in_plane(k):
        return (a, lax.rem(b + k // nz, ny), lax.rem(c + k % nz, nz))

    def along_x(k):
        return (lax.rem(a + k, nx), b, c)

    peers = [in_plane(k) for k in range(1, plane)] + [along_x(k) for k in range(1, nx)]
    barrier = pltpu.get_barrier_semaphore()
    for peer in peers:
        pl.semaphore_signal(barrier, inc=1, device_id=peer, device_id_type=MESH_ID)
    pl.semaphore_wait(barrier, len(peers))

    own = pltpu.make_async_copy(row_ref, held.at[pl.ds(me, 1)], local_sem.at[0])
    own.start()
    sent = []

    def stage(src_of, first_of, count, size, toward, send, recv):
        for k in range(1, size):
            copy = pltpu.make_async_remote_copy(
                src_ref=src_of(0),
                dst_ref=held.at[pl.ds(first_of(0), count)],
                send_sem=send.at[k],
                recv_sem=recv.at[k],
                device_id=toward(k),
                device_id_type=MESH_ID,
            )
            copy.start()
            sent.append(copy)
        for k in range(1, size):
            pltpu.make_async_remote_copy(
                src_ref=src_of(k),
                dst_ref=held.at[pl.ds(first_of(k), count)],
                send_sem=send.at[k],
                recv_sem=recv.at[k],
                device_id=toward(size - k),
                device_id_type=MESH_ID,
            ).wait_recv()

    def p_first(k):
        return (a * ny + lax.rem(b + ny - k // nz, ny)) * nz + lax.rem(c + nz - k % nz, nz)

    stage(lambda k: row_ref, p_first, 1, plane, in_plane, send1, recv1)
    own.wait()
    x_first = lambda k: lax.rem(a + nx - k, nx) * plane
    stage(lambda k: held.at[pl.ds(x_first(k), plane)], x_first, plane, nx, along_x, send2, recv2)
    for copy in sent:
        copy.wait_send()
    final = pltpu.make_async_copy(held, out_ref, local_sem.at[1])
    final.start()
    final.wait()


def gather_rows(row):
    sizes = (lax.axis_size("gx"), lax.axis_size("gy"), lax.axis_size("gz"))
    count = sizes[0] * sizes[1] * sizes[2]
    tile = row[:, None, :]
    rows = pl.pallas_call(
        functools.partial(gather_kernel, sizes),
        out_shape=jax.ShapeDtypeStruct((count, 1, LANES), jnp.float32),
        in_specs=[pl.BlockSpec(memory_space=pltpu.VMEM)],
        out_specs=pl.BlockSpec(memory_space=pltpu.VMEM),
        scratch_shapes=[
            pltpu.VMEM((count, 1, LANES), jnp.float32),
            pltpu.SemaphoreType.DMA((2,)),
            pltpu.SemaphoreType.DMA((sizes[1] * sizes[2],)),
            pltpu.SemaphoreType.DMA((sizes[1] * sizes[2],)),
            pltpu.SemaphoreType.DMA((sizes[0],)),
            pltpu.SemaphoreType.DMA((sizes[0],)),
        ],
        compiler_params=pltpu.CompilerParams(collective_id=0, has_side_effects=True),
    )(tile)
    return rows[:, 0, :]


def pack(coarse, scalars):
    vecs = coarse.shape[0]
    row = jnp.zeros((LANES,), jnp.float32)
    row = row.at[:vecs].set(coarse)
    if scalars:
        row = row.at[vecs:vecs + len(scalars)].set(jnp.stack(scalars))
    return row[None]


def unpack(rows, vecs, count):
    coarse = rows[:, :vecs].reshape(-1)
    sums = jnp.sum(rows[:, vecs:vecs + count], axis=0)
    return coarse, [sums[i] for i in range(count)]


def shards(right_side, conductance, storage, dirichlet, basis, coarse_inverse):
    vecs = basis.shape[0]
    sides = (("gx", 0), ("gy", 1), ("gz", 2))
    free = 1.0 - dirichlet.astype(jnp.float32)
    stacked = jnp.concatenate([conductance, storage[None], free[None], right_side[None]], axis=0)
    wide = padded(stacked, (("gz", 3), ("gx", 1), ("gy", 2)), 3)
    cond_wide = wide[:3]
    free_wide = wide[4]
    storage_wide = wide[3]
    cond_box = wide[:3, 1:-1, 1:-1, 1:-1]
    storage_box = wide[3, 1:-1, 1:-1, 1:-1]
    free_box = wide[4, 1:-1, 1:-1, 1:-1]
    rhs_box0 = wide[5, 1:-1, 1:-1, 1:-1]
    box_cond = pad_cond(cond_box)
    box_diag = diagonal_of(box_cond, storage_box, free_box)
    cond_face = wide[:3, 2:-2, 2:-2, 2:-2]
    free_face = wide[4, 2:-2, 2:-2, 2:-2]

    def schwarz(rhs_box):
        return jacobi(rhs_box, box_cond, box_diag, storage_box, free_box)[2:-2, 2:-2, 2:-2]

    def precondition(rhs_box, residual, coarse_all):
        weights = jnp.dot(coarse_inverse, coarse_all, precision=lax.Precision.HIGHEST)
        return schwarz(rhs_box) + expand(basis, weights, residual)

    residual0 = right_side
    coarse0 = project(basis, residual0)
    coarse0_all, _ = unpack(gather_rows(pack(coarse0, [])), vecs, 0)
    z0 = precondition(rhs_box0, residual0, coarse0_all)
    near0 = padded(z0, (("gz", 2), ("gx", 0), ("gy", 1)), 3)
    inner = (slice(1, -1),) * 3
    image0_box = stencil(free_wide * near0, cond_wide, near0[inner], storage_wide[inner], free_wide[inner])
    image0 = image0_box[2:-2, 2:-2, 2:-2]
    coarse_img = project(basis, image0)
    rows = gather_rows(pack(coarse_img, [jnp.sum(residual0 * z0), jnp.sum(z0 * image0)]))
    coarse_img_all, (rz0, curve0) = unpack(rows, vecs, 2)
    alpha0 = rz0 / curve0
    solution1 = alpha0 * z0
    rhs_box1 = rhs_box0 - alpha0 * image0_box
    residual1 = rhs_box1[2:-2, 2:-2, 2:-2]
    coarse1_all = coarse0_all - alpha0 * coarse_img_all
    z1 = precondition(rhs_box1, residual1, coarse1_all)
    near1 = faces(z1)
    image_z1 = stencil(free_face * near1, cond_face, z1, storage, free)
    local = [
        jnp.sum(residual1 * z1),
        jnp.sum(z1 * image_z1),
        jnp.sum(z1 * image0),
        jnp.sum(z0 * image_z1),
    ]
    _, (rz1, zz, cross_a, cross_b) = unpack(gather_rows(pack(jnp.zeros((0,), jnp.float32), local)), 0, 4)
    beta = rz1 / rz0
    direction1 = z1 + beta * z0
    image1 = image_z1 + beta * image0
    curve1 = zz + beta * (cross_a + cross_b) + beta * beta * curve0
    alpha1 = rz1 / curve1
    solution2 = solution1 + alpha1 * direction1
    residual2 = residual1 - alpha1 * image1
    return (solution2, residual2)


def solution(mesh):
    placed = (
        P("gx", "gy", "gz"),
        P(None, "gx", "gy", "gz"),
        P("gx", "gy", "gz"),
        P("gx", "gy", "gz"),
        P(None, "gx", "gy", "gz"),
        P(("gx", "gy", "gz"), None),
    )
    return jax.shard_map(
        shards,
        mesh=mesh,
        in_specs=placed,
        out_specs=(P("gx", "gy", "gz"), P("gx", "gy", "gz")),
        check_vma=False,
    )
```

```python
import functools

import jax
import jax.numpy as jnp
from jax import lax
from jax.experimental import pallas as pl
from jax.experimental.pallas import tpu as pltpu
from jax.sharding import PartitionSpec as P

MESH_ID = pl.DeviceIdType.MESH

SWEEPS = 4
ITERS = 2


RELAX = 2.0 / 3.0


def padded(value, sides, width):
    for axis, dim in sides:
        count, length = (lax.axis_size(axis), value.shape[dim])
        up = [(i, (i + 1) % count) for i in range(count - 1)]
        down = [(j, i) for i, j in up]
        last = lax.slice_in_dim(value, length - width, length, axis=dim)
        leading = lax.slice_in_dim(value, 0, width, axis=dim)
        before = lax.ppermute(last, axis, up)
        after = lax.ppermute(leading, axis, down)
        value = jnp.concatenate([before, value, after], axis=dim)
    return value


def pad_cond(cond):
    return jnp.pad(cond, ((0, 0), (1, 1), (1, 1), (1, 1)))


def stencil(padded_free, padded_cond, field, storage, free):
    middle = padded_free[1:-1, 1:-1, 1:-1]
    total = storage * middle
    total = (
        total
        + padded_cond[0, 1:-1, 1:-1, 1:-1] * (middle - padded_free[2:, 1:-1, 1:-1])
        + padded_cond[0, :-2, 1:-1, 1:-1] * (middle - padded_free[:-2, 1:-1, 1:-1])
    )
    total = (
        total
        + padded_cond[1, 1:-1, 1:-1, 1:-1] * (middle - padded_free[1:-1, 2:, 1:-1])
        + padded_cond[1, 1:-1, :-2, 1:-1] * (middle - padded_free[1:-1, :-2, 1:-1])
    )
    total = (
        total
        + padded_cond[2, 1:-1, 1:-1, 1:-1] * (middle - padded_free[1:-1, 1:-1, 2:])
        + padded_cond[2, 1:-1, 1:-1, :-2] * (middle - padded_free[1:-1, 1:-1, :-2])
    )
    return free * total + (1.0 - free) * field


def diagonal_of(padded_cond, storage, free):
    total = storage + padded_cond[0, 1:-1, 1:-1, 1:-1] + padded_cond[0, :-2, 1:-1, 1:-1]
    total = total + padded_cond[1, 1:-1, 1:-1, 1:-1] + padded_cond[1, 1:-1, :-2, 1:-1]
    total = total + padded_cond[2, 1:-1, 1:-1, 1:-1] + padded_cond[2, 1:-1, 1:-1, :-2]
    return free * total + (1.0 - free)


def jacobi(rhs_box, padded_cond, diagonal, storage_box, free_box):
    guess = jnp.zeros_like(rhs_box)
    for sweep in range(SWEEPS):
        image = stencil(jnp.pad(free_box * guess, 1), padded_cond, guess, storage_box, free_box)
        guess = guess + RELAX * (rhs_box - image) / diagonal
    return guess


def project(basis, field):
    return jnp.sum(basis * field[None], axis=(1, 2, 3))


def expand(basis, weights, field):
    return jnp.sum(weights[:, None, None, None] * basis, axis=0)


LANES = 128


def faces(field):
    pieces = []
    for dim, axis in enumerate(("gx", "gy", "gz")):
        count, length = (lax.axis_size(axis), field.shape[dim])
        up = [(i, i + 1) for i in range(count - 1)]
        down = [(j, i) for i, j in up]
        before = lax.ppermute(lax.slice_in_dim(field, length - 1, length, axis=dim), axis, up)
        after = lax.ppermute(lax.slice_in_dim(field, 0, 1, axis=dim), axis, down)
        pieces.append((before, after))
    result = field
    for dim in range(3):
        before, after = pieces[dim]
        widths = [(1, 1) if d < dim else (0, 0) for d in range(3)]
        result = jnp.concatenate([jnp.pad(before, widths), result, jnp.pad(after, widths)], axis=dim)
    return result


def residual_rim(field):
    return padded(field, (("gx", 0), ("gy", 1), ("gz", 2)), 2)


def gather_kernel(sizes, row_ref, out_ref, held, local_sem, send1, recv1, send2, recv2):
    nx, ny, nz = sizes
    plane = ny * nz
    a = lax.axis_index("gx")
    b = lax.axis_index("gy")
    c = lax.axis_index("gz")
    me = (a * ny + b) * nz + c

    def in_plane(k):
        return (a, lax.rem(b + k // nz, ny), lax.rem(c + k % nz, nz))

    def along_x(k):
        return (lax.rem(a + k, nx), b, c)

    peers = [in_plane(k) for k in range(1, plane)] + [along_x(k) for k in range(1, nx)]
    barrier = pltpu.get_barrier_semaphore()
    for peer in peers:
        pl.semaphore_signal(barrier, inc=1, device_id=peer, device_id_type=MESH_ID)
    pl.semaphore_wait(barrier, len(peers))

    own = pltpu.make_async_copy(row_ref, held.at[pl.ds(me, 1)], local_sem.at[0])
    own.start()
    sent = []

    def stage(src_of, first_of, count, size, toward, send, recv):
        for k in range(1, size):
            copy = pltpu.make_async_remote_copy(
                src_ref=src_of(0),
                dst_ref=held.at[pl.ds(first_of(0), count)],
                send_sem=send.at[k],
                recv_sem=recv.at[k],
                device_id=toward(k),
                device_id_type=MESH_ID,
            )
            copy.start()
            sent.append(copy)
        for k in range(1, size):
            pltpu.make_async_remote_copy(
                src_ref=src_of(k),
                dst_ref=held.at[pl.ds(first_of(k), count)],
                send_sem=send.at[k],
                recv_sem=recv.at[k],
                device_id=toward(size - k),
                device_id_type=MESH_ID,
            ).wait_recv()

    def p_first(k):
        return (a * ny + lax.rem(b + ny - k // nz, ny)) * nz + lax.rem(c + nz - k % nz, nz)

    stage(lambda k: row_ref, p_first, 1, plane, in_plane, send1, recv1)
    own.wait()
    x_first = lambda k: lax.rem(a + nx - k, nx) * plane
    stage(lambda k: held.at[pl.ds(x_first(k), plane)], x_first, plane, nx, along_x, send2, recv2)
    for copy in sent:
        copy.wait_send()
    final = pltpu.make_async_copy(held, out_ref, local_sem.at[1])
    final.start()
    final.wait()


def gather_rows(row):
    sizes = (lax.axis_size("gx"), lax.axis_size("gy"), lax.axis_size("gz"))
    count = sizes[0] * sizes[1] * sizes[2]
    tile = row[:, None, :]
    rows = pl.pallas_call(
        functools.partial(gather_kernel, sizes),
        out_shape=jax.ShapeDtypeStruct((count, 1, LANES), jnp.float32),
        in_specs=[pl.BlockSpec(memory_space=pltpu.VMEM)],
        out_specs=pl.BlockSpec(memory_space=pltpu.VMEM),
        scratch_shapes=[
            pltpu.VMEM((count, 1, LANES), jnp.float32),
            pltpu.SemaphoreType.DMA((2,)),
            pltpu.SemaphoreType.DMA((sizes[1] * sizes[2],)),
            pltpu.SemaphoreType.DMA((sizes[1] * sizes[2],)),
            pltpu.SemaphoreType.DMA((sizes[0],)),
            pltpu.SemaphoreType.DMA((sizes[0],)),
        ],
        compiler_params=pltpu.CompilerParams(collective_id=0, has_side_effects=True),
    )(tile)
    return rows[:, 0, :]


def pack(coarse, scalars):
    vecs = coarse.shape[0]
    row = jnp.zeros((LANES,), jnp.float32)
    row = row.at[:vecs].set(coarse)
    if scalars:
        row = row.at[vecs:vecs + len(scalars)].set(jnp.stack(scalars))
    return row[None]


def unpack(rows, vecs, count):
    coarse = rows[:, :vecs].reshape(-1)
    sums = jnp.sum(rows[:, vecs:vecs + count], axis=0)
    return coarse, [sums[i] for i in range(count)]


def shards(right_side, conductance, storage, dirichlet, basis, coarse_inverse):
    vecs = basis.shape[0]
    sides = (("gx", 0), ("gy", 1), ("gz", 2))
    free = 1.0 - dirichlet.astype(jnp.float32)
    stacked = jnp.concatenate([conductance, storage[None], free[None], right_side[None]], axis=0)
    wide = padded(stacked, (("gz", 3), ("gx", 1), ("gy", 2)), 3)
    cond_wide = wide[:3]
    free_wide = wide[4]
    storage_wide = wide[3]
    cond_box = wide[:3, 1:-1, 1:-1, 1:-1]
    storage_box = wide[3, 1:-1, 1:-1, 1:-1]
    free_box = wide[4, 1:-1, 1:-1, 1:-1]
    rhs_box0 = wide[5, 1:-1, 1:-1, 1:-1]
    box_cond = pad_cond(cond_box)
    box_diag = diagonal_of(box_cond, storage_box, free_box)
    cond_face = wide[:3, 2:-2, 2:-2, 2:-2]
    free_face = wide[4, 2:-2, 2:-2, 2:-2]

    def schwarz(rhs_box):
        return jacobi(rhs_box, box_cond, box_diag, storage_box, free_box)[2:-2, 2:-2, 2:-2]

    def precondition(rhs_box, residual, coarse_all):
        weights = jnp.dot(coarse_inverse, coarse_all, precision=lax.Precision.HIGHEST)
        return schwarz(rhs_box) + expand(basis, weights, residual)

    residual0 = right_side
    coarse0 = project(basis, residual0)
    coarse0_all, _ = unpack(gather_rows(pack(coarse0, [])), vecs, 0)
    z0 = precondition(rhs_box0, residual0, coarse0_all)
    near0 = padded(z0, (("gz", 2), ("gx", 0), ("gy", 1)), 3)
    inner = (slice(1, -1),) * 3
    image0_box = stencil(free_wide * near0, cond_wide, near0[inner], storage_wide[inner], free_wide[inner])
    image0 = image0_box[2:-2, 2:-2, 2:-2]
    coarse_img = project(basis, image0)
    rows = gather_rows(pack(coarse_img, [jnp.sum(residual0 * z0), jnp.sum(z0 * image0)]))
    coarse_img_all, (rz0, curve0) = unpack(rows, vecs, 2)
    alpha0 = rz0 / curve0
    solution1 = alpha0 * z0
    rhs_box1 = rhs_box0 - alpha0 * image0_box
    residual1 = rhs_box1[2:-2, 2:-2, 2:-2]
    coarse1_all = coarse0_all - alpha0 * coarse_img_all
    z1 = precondition(rhs_box1, residual1, coarse1_all)
    bare = jnp.pad(z1, 1)
    image_bare = stencil(free_face * bare, cond_face, z1, storage, free)
    near1 = faces(z1)
    halo = free_face * (near1 - bare)
    reach = (
        cond_face[0, 1:-1, 1:-1, 1:-1] * halo[2:, 1:-1, 1:-1]
        + cond_face[0, :-2, 1:-1, 1:-1] * halo[:-2, 1:-1, 1:-1]
        + cond_face[1, 1:-1, 1:-1, 1:-1] * halo[1:-1, 2:, 1:-1]
        + cond_face[1, 1:-1, :-2, 1:-1] * halo[1:-1, :-2, 1:-1]
        + cond_face[2, 1:-1, 1:-1, 1:-1] * halo[1:-1, 1:-1, 2:]
        + cond_face[2, 1:-1, 1:-1, :-2] * halo[1:-1, 1:-1, :-2]
    )
    image_z1 = image_bare - free * reach
    local = [
        jnp.sum(residual1 * z1),
        jnp.sum(z1 * image_z1),
        jnp.sum(z1 * image0),
        jnp.sum(z0 * image_z1),
    ]
    _, (rz1, zz, cross_a, cross_b) = unpack(gather_rows(pack(jnp.zeros((0,), jnp.float32), local)), 0, 4)
    beta = rz1 / rz0
    direction1 = z1 + beta * z0
    image1 = image_z1 + beta * image0
    curve1 = zz + beta * (cross_a + cross_b) + beta * beta * curve0
    alpha1 = rz1 / curve1
    solution2 = solution1 + alpha1 * direction1
    residual2 = residual1 - alpha1 * image1
    return (solution2, residual2)


def solution(mesh):
    placed = (
        P("gx", "gy", "gz"),
        P(None, "gx", "gy", "gz"),
        P("gx", "gy", "gz"),
        P("gx", "gy", "gz"),
        P(None, "gx", "gy", "gz"),
        P(("gx", "gy", "gz"), None),
    )
    return jax.shard_map(
        shards,
        mesh=mesh,
        in_specs=placed,
        out_specs=(P("gx", "gy", "gz"), P("gx", "gy", "gz")),
        check_vma=False,
    )
```

```python
import functools

import jax
import jax.numpy as jnp
from jax import lax
from jax.experimental import pallas as pl
from jax.experimental.pallas import tpu as pltpu
from jax.sharding import PartitionSpec as P

MESH_ID = pl.DeviceIdType.MESH

SWEEPS = 4
ITERS = 2


RELAX = 2.0 / 3.0


def padded(value, sides, width):
    for axis, dim in sides:
        count, length = (lax.axis_size(axis), value.shape[dim])
        up = [(i, (i + 1) % count) for i in range(count - 1)]
        down = [(j, i) for i, j in up]
        last = lax.slice_in_dim(value, length - width, length, axis=dim)
        leading = lax.slice_in_dim(value, 0, width, axis=dim)
        before = lax.ppermute(last, axis, up)
        after = lax.ppermute(leading, axis, down)
        value = jnp.concatenate([before, value, after], axis=dim)
    return value


def pad_cond(cond):
    return jnp.pad(cond, ((0, 0), (1, 1), (1, 1), (1, 1)))


def stencil(padded_free, padded_cond, field, storage, free):
    middle = padded_free[1:-1, 1:-1, 1:-1]
    total = storage * middle
    total = (
        total
        + padded_cond[0, 1:-1, 1:-1, 1:-1] * (middle - padded_free[2:, 1:-1, 1:-1])
        + padded_cond[0, :-2, 1:-1, 1:-1] * (middle - padded_free[:-2, 1:-1, 1:-1])
    )
    total = (
        total
        + padded_cond[1, 1:-1, 1:-1, 1:-1] * (middle - padded_free[1:-1, 2:, 1:-1])
        + padded_cond[1, 1:-1, :-2, 1:-1] * (middle - padded_free[1:-1, :-2, 1:-1])
    )
    total = (
        total
        + padded_cond[2, 1:-1, 1:-1, 1:-1] * (middle - padded_free[1:-1, 1:-1, 2:])
        + padded_cond[2, 1:-1, 1:-1, :-2] * (middle - padded_free[1:-1, 1:-1, :-2])
    )
    return free * total + (1.0 - free) * field


def diagonal_of(padded_cond, storage, free):
    total = storage + padded_cond[0, 1:-1, 1:-1, 1:-1] + padded_cond[0, :-2, 1:-1, 1:-1]
    total = total + padded_cond[1, 1:-1, 1:-1, 1:-1] + padded_cond[1, 1:-1, :-2, 1:-1]
    total = total + padded_cond[2, 1:-1, 1:-1, 1:-1] + padded_cond[2, 1:-1, 1:-1, :-2]
    return free * total + (1.0 - free)


def jacobi(rhs_box, padded_cond, diagonal, storage_box, free_box):
    guess = jnp.zeros_like(rhs_box)
    for sweep in range(SWEEPS):
        image = stencil(jnp.pad(free_box * guess, 1), padded_cond, guess, storage_box, free_box)
        guess = guess + RELAX * (rhs_box - image) / diagonal
    return guess


def project(basis, field):
    return jnp.sum(basis * field[None], axis=(1, 2, 3))


def expand(basis, weights, field):
    return jnp.sum(weights[:, None, None, None] * basis, axis=0)


LANES = 128


def faces(field):
    pieces = []
    for dim, axis in enumerate(("gx", "gy", "gz")):
        count, length = (lax.axis_size(axis), field.shape[dim])
        up = [(i, i + 1) for i in range(count - 1)]
        down = [(j, i) for i, j in up]
        before = lax.ppermute(lax.slice_in_dim(field, length - 1, length, axis=dim), axis, up)
        after = lax.ppermute(lax.slice_in_dim(field, 0, 1, axis=dim), axis, down)
        pieces.append((before, after))
    result = field
    for dim in range(3):
        before, after = pieces[dim]
        widths = [(1, 1) if d < dim else (0, 0) for d in range(3)]
        result = jnp.concatenate([jnp.pad(before, widths), result, jnp.pad(after, widths)], axis=dim)
    return result


def residual_rim(field):
    return padded(field, (("gx", 0), ("gy", 1), ("gz", 2)), 2)


def gather_kernel(sizes, row_ref, out_ref, held, local_sem, send1, recv1, send2, recv2):
    nx, ny, nz = sizes
    plane = ny * nz
    a = lax.axis_index("gx")
    b = lax.axis_index("gy")
    c = lax.axis_index("gz")
    me = (a * ny + b) * nz + c

    def in_plane(k):
        return (a, lax.rem(b + k // nz, ny), lax.rem(c + k % nz, nz))

    def along_x(k):
        return (lax.rem(a + k, nx), b, c)

    peers = [in_plane(k) for k in range(1, plane)] + [along_x(k) for k in range(1, nx)]
    barrier = pltpu.get_barrier_semaphore()
    for peer in peers:
        pl.semaphore_signal(barrier, inc=1, device_id=peer, device_id_type=MESH_ID)
    pl.semaphore_wait(barrier, len(peers))

    own = pltpu.make_async_copy(row_ref, held.at[pl.ds(me, 1)], local_sem.at[0])
    own.start()
    sent = []

    def stage(src_of, first_of, count, size, toward, send, recv):
        for k in range(1, size):
            copy = pltpu.make_async_remote_copy(
                src_ref=src_of(0),
                dst_ref=held.at[pl.ds(first_of(0), count)],
                send_sem=send.at[k],
                recv_sem=recv.at[k],
                device_id=toward(k),
                device_id_type=MESH_ID,
            )
            copy.start()
            sent.append(copy)
        for k in range(1, size):
            pltpu.make_async_remote_copy(
                src_ref=src_of(k),
                dst_ref=held.at[pl.ds(first_of(k), count)],
                send_sem=send.at[k],
                recv_sem=recv.at[k],
                device_id=toward(size - k),
                device_id_type=MESH_ID,
            ).wait_recv()

    def p_first(k):
        return (a * ny + lax.rem(b + ny - k // nz, ny)) * nz + lax.rem(c + nz - k % nz, nz)

    stage(lambda k: row_ref, p_first, 1, plane, in_plane, send1, recv1)
    own.wait()
    x_first = lambda k: lax.rem(a + nx - k, nx) * plane
    stage(lambda k: held.at[pl.ds(x_first(k), plane)], x_first, plane, nx, along_x, send2, recv2)
    for copy in sent:
        copy.wait_send()
    final = pltpu.make_async_copy(held, out_ref, local_sem.at[1])
    final.start()
    final.wait()


def gather_rows(row):
    sizes = (lax.axis_size("gx"), lax.axis_size("gy"), lax.axis_size("gz"))
    count = sizes[0] * sizes[1] * sizes[2]
    tile = row[:, None, :]
    rows = pl.pallas_call(
        functools.partial(gather_kernel, sizes),
        out_shape=jax.ShapeDtypeStruct((count, 1, LANES), jnp.float32),
        in_specs=[pl.BlockSpec(memory_space=pltpu.VMEM)],
        out_specs=pl.BlockSpec(memory_space=pltpu.VMEM),
        scratch_shapes=[
            pltpu.VMEM((count, 1, LANES), jnp.float32),
            pltpu.SemaphoreType.DMA((2,)),
            pltpu.SemaphoreType.DMA((sizes[1] * sizes[2],)),
            pltpu.SemaphoreType.DMA((sizes[1] * sizes[2],)),
            pltpu.SemaphoreType.DMA((sizes[0],)),
            pltpu.SemaphoreType.DMA((sizes[0],)),
        ],
        compiler_params=pltpu.CompilerParams(collective_id=0, has_side_effects=True),
    )(tile)
    return rows[:, 0, :]


def pack(coarse, scalars):
    vecs = coarse.shape[0]
    row = jnp.zeros((LANES,), jnp.float32)
    row = row.at[:vecs].set(coarse)
    if scalars:
        row = row.at[vecs:vecs + len(scalars)].set(jnp.stack(scalars))
    return row[None]


def unpack(rows, vecs, count):
    coarse = rows[:, :vecs].reshape(-1)
    sums = jnp.sum(rows[:, vecs:vecs + count], axis=0)
    return coarse, [sums[i] for i in range(count)]


def shards(right_side, conductance, storage, dirichlet, basis, coarse_inverse):
    vecs = basis.shape[0]
    sides = (("gx", 0), ("gy", 1), ("gz", 2))
    free = 1.0 - dirichlet.astype(jnp.float32)
    stacked = jnp.concatenate([conductance, storage[None], free[None], right_side[None]], axis=0)
    wide = padded(stacked, (("gz", 3), ("gx", 1), ("gy", 2)), 3)
    cond_wide = wide[:3]
    free_wide = wide[4]
    storage_wide = wide[3]
    cond_box = wide[:3, 1:-1, 1:-1, 1:-1]
    storage_box = wide[3, 1:-1, 1:-1, 1:-1]
    free_box = wide[4, 1:-1, 1:-1, 1:-1]
    rhs_box0 = wide[5, 1:-1, 1:-1, 1:-1]
    box_cond = pad_cond(cond_box)
    box_diag = diagonal_of(box_cond, storage_box, free_box)
    cond_face = wide[:3, 2:-2, 2:-2, 2:-2]
    free_face = wide[4, 2:-2, 2:-2, 2:-2]

    def schwarz(rhs_box):
        return jacobi(rhs_box, box_cond, box_diag, storage_box, free_box)[2:-2, 2:-2, 2:-2]

    def precondition(rhs_box, residual, coarse_all):
        weights = jnp.dot(coarse_inverse, coarse_all, precision=lax.Precision.HIGHEST)
        return schwarz(rhs_box) + expand(basis, weights, residual)

    residual0 = right_side
    coarse0 = project(basis, residual0)
    smooth0, row0 = lax.optimization_barrier((schwarz(rhs_box0), pack(coarse0, [])))
    coarse0_all, _ = unpack(gather_rows(row0), vecs, 0)
    weights0 = jnp.dot(coarse_inverse, coarse0_all, precision=lax.Precision.HIGHEST)
    z0 = smooth0 + expand(basis, weights0, residual0)
    near0 = padded(z0, (("gz", 2), ("gx", 0), ("gy", 1)), 3)
    inner = (slice(1, -1),) * 3
    image0_box = stencil(free_wide * near0, cond_wide, near0[inner], storage_wide[inner], free_wide[inner])
    image0 = image0_box[2:-2, 2:-2, 2:-2]
    coarse_img = project(basis, image0)
    rows = gather_rows(pack(coarse_img, [jnp.sum(residual0 * z0), jnp.sum(z0 * image0)]))
    coarse_img_all, (rz0, curve0) = unpack(rows, vecs, 2)
    alpha0 = rz0 / curve0
    solution1 = alpha0 * z0
    rhs_box1 = rhs_box0 - alpha0 * image0_box
    residual1 = rhs_box1[2:-2, 2:-2, 2:-2]
    coarse1_all = coarse0_all - alpha0 * coarse_img_all
    z1 = precondition(rhs_box1, residual1, coarse1_all)
    near1 = faces(z1)
    image_z1 = stencil(free_face * near1, cond_face, z1, storage, free)
    local = [
        jnp.sum(residual1 * z1),
        jnp.sum(z1 * image_z1),
        jnp.sum(z1 * image0),
        jnp.sum(z0 * image_z1),
    ]
    _, (rz1, zz, cross_a, cross_b) = unpack(gather_rows(pack(jnp.zeros((0,), jnp.float32), local)), 0, 4)
    beta = rz1 / rz0
    direction1 = z1 + beta * z0
    image1 = image_z1 + beta * image0
    curve1 = zz + beta * (cross_a + cross_b) + beta * beta * curve0
    alpha1 = rz1 / curve1
    solution2 = solution1 + alpha1 * direction1
    residual2 = residual1 - alpha1 * image1
    return (solution2, residual2)


def solution(mesh):
    placed = (
        P("gx", "gy", "gz"),
        P(None, "gx", "gy", "gz"),
        P("gx", "gy", "gz"),
        P("gx", "gy", "gz"),
        P(None, "gx", "gy", "gz"),
        P(("gx", "gy", "gz"), None),
    )
    return jax.shard_map(
        shards,
        mesh=mesh,
        in_specs=placed,
        out_specs=(P("gx", "gy", "gz"), P("gx", "gy", "gz")),
        check_vma=False,
    )
```

```python
import functools

import jax
import jax.numpy as jnp
from jax import lax
from jax.experimental import pallas as pl
from jax.experimental.pallas import tpu as pltpu
from jax.sharding import PartitionSpec as P

MESH_ID = pl.DeviceIdType.MESH

SWEEPS = 4
ITERS = 2


RELAX = 2.0 / 3.0


def padded(value, sides, width):
    for axis, dim in sides:
        count, length = (lax.axis_size(axis), value.shape[dim])
        up = [(i, (i + 1) % count) for i in range(count - 1)]
        down = [(j, i) for i, j in up]
        last = lax.slice_in_dim(value, length - width, length, axis=dim)
        leading = lax.slice_in_dim(value, 0, width, axis=dim)
        before = lax.ppermute(last, axis, up)
        after = lax.ppermute(leading, axis, down)
        value = jnp.concatenate([before, value, after], axis=dim)
    return value


def pad_cond(cond):
    return jnp.pad(cond, ((0, 0), (1, 1), (1, 1), (1, 1)))


def stencil(padded_free, padded_cond, field, storage, free):
    middle = padded_free[1:-1, 1:-1, 1:-1]
    total = storage * middle
    total = (
        total
        + padded_cond[0, 1:-1, 1:-1, 1:-1] * (middle - padded_free[2:, 1:-1, 1:-1])
        + padded_cond[0, :-2, 1:-1, 1:-1] * (middle - padded_free[:-2, 1:-1, 1:-1])
    )
    total = (
        total
        + padded_cond[1, 1:-1, 1:-1, 1:-1] * (middle - padded_free[1:-1, 2:, 1:-1])
        + padded_cond[1, 1:-1, :-2, 1:-1] * (middle - padded_free[1:-1, :-2, 1:-1])
    )
    total = (
        total
        + padded_cond[2, 1:-1, 1:-1, 1:-1] * (middle - padded_free[1:-1, 1:-1, 2:])
        + padded_cond[2, 1:-1, 1:-1, :-2] * (middle - padded_free[1:-1, 1:-1, :-2])
    )
    return free * total + (1.0 - free) * field


def diagonal_of(padded_cond, storage, free):
    total = storage + padded_cond[0, 1:-1, 1:-1, 1:-1] + padded_cond[0, :-2, 1:-1, 1:-1]
    total = total + padded_cond[1, 1:-1, 1:-1, 1:-1] + padded_cond[1, 1:-1, :-2, 1:-1]
    total = total + padded_cond[2, 1:-1, 1:-1, 1:-1] + padded_cond[2, 1:-1, 1:-1, :-2]
    return free * total + (1.0 - free)


def jacobi(rhs_box, padded_cond, diagonal, storage_box, free_box):
    guess = jnp.zeros_like(rhs_box)
    for sweep in range(SWEEPS):
        image = stencil(jnp.pad(free_box * guess, 1), padded_cond, guess, storage_box, free_box)
        guess = guess + RELAX * (rhs_box - image) / diagonal
    return guess


def project(basis, field):
    return jnp.sum(basis * field[None], axis=(1, 2, 3))


def expand(basis, weights, field):
    return jnp.sum(weights[:, None, None, None] * basis, axis=0)


LANES = 128


def faces(field):
    pieces = []
    for dim, axis in enumerate(("gx", "gy", "gz")):
        count, length = (lax.axis_size(axis), field.shape[dim])
        up = [(i, i + 1) for i in range(count - 1)]
        down = [(j, i) for i, j in up]
        before = lax.ppermute(lax.slice_in_dim(field, length - 1, length, axis=dim), axis, up)
        after = lax.ppermute(lax.slice_in_dim(field, 0, 1, axis=dim), axis, down)
        pieces.append((before, after))
    result = field
    for dim in range(3):
        before, after = pieces[dim]
        widths = [(1, 1) if d < dim else (0, 0) for d in range(3)]
        result = jnp.concatenate([jnp.pad(before, widths), result, jnp.pad(after, widths)], axis=dim)
    return result


def residual_rim(field):
    return padded(field, (("gx", 0), ("gy", 1), ("gz", 2)), 2)


def gather_kernel(sizes, row_ref, out_ref, held, local_sem, send1, recv1, send2, recv2):
    nx, ny, nz = sizes
    plane = ny * nz
    a = lax.axis_index("gx")
    b = lax.axis_index("gy")
    c = lax.axis_index("gz")
    me = (a * ny + b) * nz + c

    def in_plane(k):
        return (a, lax.rem(b + k // nz, ny), lax.rem(c + k % nz, nz))

    def along_x(k):
        return (lax.rem(a + k, nx), b, c)

    own = pltpu.make_async_copy(row_ref, held.at[pl.ds(me, 1)], local_sem.at[0])
    own.start()
    sent = []

    def stage(src_of, first_of, count, size, toward, send, recv):
        for k in range(1, size):
            copy = pltpu.make_async_remote_copy(
                src_ref=src_of(0),
                dst_ref=held.at[pl.ds(first_of(0), count)],
                send_sem=send.at[k],
                recv_sem=recv.at[k],
                device_id=toward(k),
                device_id_type=MESH_ID,
            )
            copy.start()
            sent.append(copy)
        for k in range(1, size):
            pltpu.make_async_remote_copy(
                src_ref=src_of(k),
                dst_ref=held.at[pl.ds(first_of(k), count)],
                send_sem=send.at[k],
                recv_sem=recv.at[k],
                device_id=toward(size - k),
                device_id_type=MESH_ID,
            ).wait_recv()

    def p_first(k):
        return (a * ny + lax.rem(b + ny - k // nz, ny)) * nz + lax.rem(c + nz - k % nz, nz)

    stage(lambda k: row_ref, p_first, 1, plane, in_plane, send1, recv1)
    own.wait()
    x_first = lambda k: lax.rem(a + nx - k, nx) * plane
    stage(lambda k: held.at[pl.ds(x_first(k), plane)], x_first, plane, nx, along_x, send2, recv2)
    for copy in sent:
        copy.wait_send()
    final = pltpu.make_async_copy(held, out_ref, local_sem.at[1])
    final.start()
    final.wait()


def gather_rows(row):
    sizes = (lax.axis_size("gx"), lax.axis_size("gy"), lax.axis_size("gz"))
    count = sizes[0] * sizes[1] * sizes[2]
    tile = row[:, None, :]
    rows = pl.pallas_call(
        functools.partial(gather_kernel, sizes),
        out_shape=jax.ShapeDtypeStruct((count, 1, LANES), jnp.float32),
        in_specs=[pl.BlockSpec(memory_space=pltpu.VMEM)],
        out_specs=pl.BlockSpec(memory_space=pltpu.VMEM),
        scratch_shapes=[
            pltpu.VMEM((count, 1, LANES), jnp.float32),
            pltpu.SemaphoreType.DMA((2,)),
            pltpu.SemaphoreType.DMA((sizes[1] * sizes[2],)),
            pltpu.SemaphoreType.DMA((sizes[1] * sizes[2],)),
            pltpu.SemaphoreType.DMA((sizes[0],)),
            pltpu.SemaphoreType.DMA((sizes[0],)),
        ],
        compiler_params=pltpu.CompilerParams(has_side_effects=True),
    )(tile)
    return rows[:, 0, :]


def pack(coarse, scalars):
    vecs = coarse.shape[0]
    row = jnp.zeros((LANES,), jnp.float32)
    row = row.at[:vecs].set(coarse)
    if scalars:
        row = row.at[vecs:vecs + len(scalars)].set(jnp.stack(scalars))
    return row[None]


def unpack(rows, vecs, count):
    coarse = rows[:, :vecs].reshape(-1)
    sums = jnp.sum(rows[:, vecs:vecs + count], axis=0)
    return coarse, [sums[i] for i in range(count)]


def shards(right_side, conductance, storage, dirichlet, basis, coarse_inverse):
    vecs = basis.shape[0]
    sides = (("gx", 0), ("gy", 1), ("gz", 2))
    free = 1.0 - dirichlet.astype(jnp.float32)
    stacked = jnp.concatenate([conductance, storage[None], free[None], right_side[None]], axis=0)
    wide = padded(stacked, (("gz", 3), ("gx", 1), ("gy", 2)), 3)
    cond_wide = wide[:3]
    free_wide = wide[4]
    storage_wide = wide[3]
    cond_box = wide[:3, 1:-1, 1:-1, 1:-1]
    storage_box = wide[3, 1:-1, 1:-1, 1:-1]
    free_box = wide[4, 1:-1, 1:-1, 1:-1]
    rhs_box0 = wide[5, 1:-1, 1:-1, 1:-1]
    box_cond = pad_cond(cond_box)
    box_diag = diagonal_of(box_cond, storage_box, free_box)
    cond_face = wide[:3, 2:-2, 2:-2, 2:-2]
    free_face = wide[4, 2:-2, 2:-2, 2:-2]

    def schwarz(rhs_box):
        return jacobi(rhs_box, box_cond, box_diag, storage_box, free_box)[2:-2, 2:-2, 2:-2]

    def precondition(rhs_box, residual, coarse_all):
        weights = jnp.dot(coarse_inverse, coarse_all, precision=lax.Precision.HIGHEST)
        return schwarz(rhs_box) + expand(basis, weights, residual)

    residual0 = right_side
    coarse0 = project(basis, residual0)
    coarse0_all, _ = unpack(gather_rows(pack(coarse0, [])), vecs, 0)
    z0 = precondition(rhs_box0, residual0, coarse0_all)
    near0 = padded(z0, (("gz", 2), ("gx", 0), ("gy", 1)), 3)
    inner = (slice(1, -1),) * 3
    image0_box = stencil(free_wide * near0, cond_wide, near0[inner], storage_wide[inner], free_wide[inner])
    image0 = image0_box[2:-2, 2:-2, 2:-2]
    coarse_img = project(basis, image0)
    rows = gather_rows(pack(coarse_img, [jnp.sum(residual0 * z0), jnp.sum(z0 * image0)]))
    coarse_img_all, (rz0, curve0) = unpack(rows, vecs, 2)
    alpha0 = rz0 / curve0
    solution1 = alpha0 * z0
    rhs_box1 = rhs_box0 - alpha0 * image0_box
    residual1 = rhs_box1[2:-2, 2:-2, 2:-2]
    coarse1_all = coarse0_all - alpha0 * coarse_img_all
    z1 = precondition(rhs_box1, residual1, coarse1_all)
    near1 = faces(z1)
    image_z1 = stencil(free_face * near1, cond_face, z1, storage, free)
    local = [
        jnp.sum(residual1 * z1),
        jnp.sum(z1 * image_z1),
        jnp.sum(z1 * image0),
        jnp.sum(z0 * image_z1),
    ]
    _, (rz1, zz, cross_a, cross_b) = unpack(gather_rows(pack(jnp.zeros((0,), jnp.float32), local)), 0, 4)
    beta = rz1 / rz0
    direction1 = z1 + beta * z0
    image1 = image_z1 + beta * image0
    curve1 = zz + beta * (cross_a + cross_b) + beta * beta * curve0
    alpha1 = rz1 / curve1
    solution2 = solution1 + alpha1 * direction1
    residual2 = residual1 - alpha1 * image1
    return (solution2, residual2)


def solution(mesh):
    placed = (
        P("gx", "gy", "gz"),
        P(None, "gx", "gy", "gz"),
        P("gx", "gy", "gz"),
        P("gx", "gy", "gz"),
        P(None, "gx", "gy", "gz"),
        P(("gx", "gy", "gz"), None),
    )
    return jax.shard_map(
        shards,
        mesh=mesh,
        in_specs=placed,
        out_specs=(P("gx", "gy", "gz"), P("gx", "gy", "gz")),
        check_vma=False,
    )
```

```python
import functools

import jax
import jax.numpy as jnp
from jax import lax
from jax.experimental import pallas as pl
from jax.experimental.pallas import tpu as pltpu
from jax.sharding import PartitionSpec as P

MESH_ID = pl.DeviceIdType.MESH

SWEEPS = 4
ITERS = 2


RELAX = 2.0 / 3.0


def padded(value, sides, width):
    for axis, dim in sides:
        count, length = (lax.axis_size(axis), value.shape[dim])
        up = [(i, (i + 1) % count) for i in range(count - 1)]
        down = [(j, i) for i, j in up]
        last = lax.slice_in_dim(value, length - width, length, axis=dim)
        leading = lax.slice_in_dim(value, 0, width, axis=dim)
        before = lax.ppermute(last, axis, up)
        after = lax.ppermute(leading, axis, down)
        value = jnp.concatenate([before, value, after], axis=dim)
    return value


def pad_cond(cond):
    return jnp.pad(cond, ((0, 0), (1, 1), (1, 1), (1, 1)))


def stencil(padded_free, padded_cond, field, storage, free):
    middle = padded_free[1:-1, 1:-1, 1:-1]
    total = storage * middle
    total = (
        total
        + padded_cond[0, 1:-1, 1:-1, 1:-1] * (middle - padded_free[2:, 1:-1, 1:-1])
        + padded_cond[0, :-2, 1:-1, 1:-1] * (middle - padded_free[:-2, 1:-1, 1:-1])
    )
    total = (
        total
        + padded_cond[1, 1:-1, 1:-1, 1:-1] * (middle - padded_free[1:-1, 2:, 1:-1])
        + padded_cond[1, 1:-1, :-2, 1:-1] * (middle - padded_free[1:-1, :-2, 1:-1])
    )
    total = (
        total
        + padded_cond[2, 1:-1, 1:-1, 1:-1] * (middle - padded_free[1:-1, 1:-1, 2:])
        + padded_cond[2, 1:-1, 1:-1, :-2] * (middle - padded_free[1:-1, 1:-1, :-2])
    )
    return free * total + (1.0 - free) * field


def diagonal_of(padded_cond, storage, free):
    total = storage + padded_cond[0, 1:-1, 1:-1, 1:-1] + padded_cond[0, :-2, 1:-1, 1:-1]
    total = total + padded_cond[1, 1:-1, 1:-1, 1:-1] + padded_cond[1, 1:-1, :-2, 1:-1]
    total = total + padded_cond[2, 1:-1, 1:-1, 1:-1] + padded_cond[2, 1:-1, 1:-1, :-2]
    return free * total + (1.0 - free)


def jacobi(rhs_box, padded_cond, diagonal, storage_box, free_box):
    guess = jnp.zeros_like(rhs_box)
    for sweep in range(SWEEPS):
        image = stencil(jnp.pad(free_box * guess, 1), padded_cond, guess, storage_box, free_box)
        guess = guess + RELAX * (rhs_box - image) / diagonal
    return guess


def project(basis, field):
    return jnp.sum(basis * field[None], axis=(1, 2, 3))


def expand(basis, weights, field):
    return jnp.sum(weights[:, None, None, None] * basis, axis=0)


LANES = 128


def faces(field):
    pieces = []
    for dim, axis in enumerate(("gx", "gy", "gz")):
        count, length = (lax.axis_size(axis), field.shape[dim])
        up = [(i, i + 1) for i in range(count - 1)]
        down = [(j, i) for i, j in up]
        before = lax.ppermute(lax.slice_in_dim(field, length - 1, length, axis=dim), axis, up)
        after = lax.ppermute(lax.slice_in_dim(field, 0, 1, axis=dim), axis, down)
        pieces.append((before, after))
    result = field
    for dim in range(3):
        before, after = pieces[dim]
        widths = [(1, 1) if d < dim else (0, 0) for d in range(3)]
        result = jnp.concatenate([jnp.pad(before, widths), result, jnp.pad(after, widths)], axis=dim)
    return result


def residual_rim(field):
    return padded(field, (("gx", 0), ("gy", 1), ("gz", 2)), 2)


def gather_kernel(sizes, row_ref, held, local_sem, send1, recv1, send2, recv2):
    nx, ny, nz = sizes
    plane = ny * nz
    a = lax.axis_index("gx")
    b = lax.axis_index("gy")
    c = lax.axis_index("gz")
    me = (a * ny + b) * nz + c

    def in_plane(k):
        return (a, lax.rem(b + k // nz, ny), lax.rem(c + k % nz, nz))

    def along_x(k):
        return (lax.rem(a + k, nx), b, c)

    peers = [in_plane(k) for k in range(1, plane)] + [along_x(k) for k in range(1, nx)]
    barrier = pltpu.get_barrier_semaphore()
    for peer in peers:
        pl.semaphore_signal(barrier, inc=1, device_id=peer, device_id_type=MESH_ID)
    pl.semaphore_wait(barrier, len(peers))

    own = pltpu.make_async_copy(row_ref, held.at[pl.ds(me, 1)], local_sem.at[0])
    own.start()
    sent = []

    def stage(src_of, first_of, count, size, toward, send, recv):
        for k in range(1, size):
            copy = pltpu.make_async_remote_copy(
                src_ref=src_of(0),
                dst_ref=held.at[pl.ds(first_of(0), count)],
                send_sem=send.at[k],
                recv_sem=recv.at[k],
                device_id=toward(k),
                device_id_type=MESH_ID,
            )
            copy.start()
            sent.append(copy)
        for k in range(1, size):
            pltpu.make_async_remote_copy(
                src_ref=src_of(k),
                dst_ref=held.at[pl.ds(first_of(k), count)],
                send_sem=send.at[k],
                recv_sem=recv.at[k],
                device_id=toward(size - k),
                device_id_type=MESH_ID,
            ).wait_recv()

    def p_first(k):
        return (a * ny + lax.rem(b + ny - k // nz, ny)) * nz + lax.rem(c + nz - k % nz, nz)

    stage(lambda k: row_ref, p_first, 1, plane, in_plane, send1, recv1)
    own.wait()
    x_first = lambda k: lax.rem(a + nx - k, nx) * plane
    stage(lambda k: held.at[pl.ds(x_first(k), plane)], x_first, plane, nx, along_x, send2, recv2)
    for copy in sent:
        copy.wait_send()


def gather_rows(row):
    sizes = (lax.axis_size("gx"), lax.axis_size("gy"), lax.axis_size("gz"))
    count = sizes[0] * sizes[1] * sizes[2]
    tile = row[:, None, :]
    rows = pl.pallas_call(
        functools.partial(gather_kernel, sizes),
        out_shape=jax.ShapeDtypeStruct((count, 1, LANES), jnp.float32),
        in_specs=[pl.BlockSpec(memory_space=pltpu.VMEM)],
        out_specs=pl.BlockSpec(memory_space=pltpu.VMEM),
        scratch_shapes=[
            pltpu.SemaphoreType.DMA((1,)),
            pltpu.SemaphoreType.DMA((sizes[1] * sizes[2],)),
            pltpu.SemaphoreType.DMA((sizes[1] * sizes[2],)),
            pltpu.SemaphoreType.DMA((sizes[0],)),
            pltpu.SemaphoreType.DMA((sizes[0],)),
        ],
        compiler_params=pltpu.CompilerParams(collective_id=0, has_side_effects=True),
    )(tile)
    return rows[:, 0, :]


def pack(coarse, scalars):
    vecs = coarse.shape[0]
    row = jnp.zeros((LANES,), jnp.float32)
    row = row.at[:vecs].set(coarse)
    if scalars:
        row = row.at[vecs:vecs + len(scalars)].set(jnp.stack(scalars))
    return row[None]


def unpack(rows, vecs, count):
    coarse = rows[:, :vecs].reshape(-1)
    sums = jnp.sum(rows[:, vecs:vecs + count], axis=0)
    return coarse, [sums[i] for i in range(count)]


def shards(right_side, conductance, storage, dirichlet, basis, coarse_inverse):
    vecs = basis.shape[0]
    sides = (("gx", 0), ("gy", 1), ("gz", 2))
    free = 1.0 - dirichlet.astype(jnp.float32)
    stacked = jnp.concatenate([conductance, storage[None], free[None], right_side[None]], axis=0)
    wide = padded(stacked, (("gz", 3), ("gx", 1), ("gy", 2)), 3)
    cond_wide = wide[:3]
    free_wide = wide[4]
    storage_wide = wide[3]
    cond_box = wide[:3, 1:-1, 1:-1, 1:-1]
    storage_box = wide[3, 1:-1, 1:-1, 1:-1]
    free_box = wide[4, 1:-1, 1:-1, 1:-1]
    rhs_box0 = wide[5, 1:-1, 1:-1, 1:-1]
    box_cond = pad_cond(cond_box)
    box_diag = diagonal_of(box_cond, storage_box, free_box)
    cond_face = wide[:3, 2:-2, 2:-2, 2:-2]
    free_face = wide[4, 2:-2, 2:-2, 2:-2]

    def schwarz(rhs_box):
        return jacobi(rhs_box, box_cond, box_diag, storage_box, free_box)[2:-2, 2:-2, 2:-2]

    def precondition(rhs_box, residual, coarse_all):
        weights = jnp.dot(coarse_inverse, coarse_all, precision=lax.Precision.HIGHEST)
        return schwarz(rhs_box) + expand(basis, weights, residual)

    residual0 = right_side
    coarse0 = project(basis, residual0)
    coarse0_all, _ = unpack(gather_rows(pack(coarse0, [])), vecs, 0)
    z0 = precondition(rhs_box0, residual0, coarse0_all)
    near0 = padded(z0, (("gz", 2), ("gx", 0), ("gy", 1)), 3)
    inner = (slice(1, -1),) * 3
    image0_box = stencil(free_wide * near0, cond_wide, near0[inner], storage_wide[inner], free_wide[inner])
    image0 = image0_box[2:-2, 2:-2, 2:-2]
    coarse_img = project(basis, image0)
    rows = gather_rows(pack(coarse_img, [jnp.sum(residual0 * z0), jnp.sum(z0 * image0)]))
    coarse_img_all, (rz0, curve0) = unpack(rows, vecs, 2)
    alpha0 = rz0 / curve0
    solution1 = alpha0 * z0
    rhs_box1 = rhs_box0 - alpha0 * image0_box
    residual1 = rhs_box1[2:-2, 2:-2, 2:-2]
    coarse1_all = coarse0_all - alpha0 * coarse_img_all
    z1 = precondition(rhs_box1, residual1, coarse1_all)
    near1 = faces(z1)
    image_z1 = stencil(free_face * near1, cond_face, z1, storage, free)
    local = [
        jnp.sum(residual1 * z1),
        jnp.sum(z1 * image_z1),
        jnp.sum(z1 * image0),
        jnp.sum(z0 * image_z1),
    ]
    _, (rz1, zz, cross_a, cross_b) = unpack(gather_rows(pack(jnp.zeros((0,), jnp.float32), local)), 0, 4)
    beta = rz1 / rz0
    direction1 = z1 + beta * z0
    image1 = image_z1 + beta * image0
    curve1 = zz + beta * (cross_a + cross_b) + beta * beta * curve0
    alpha1 = rz1 / curve1
    solution2 = solution1 + alpha1 * direction1
    residual2 = residual1 - alpha1 * image1
    return (solution2, residual2)


def solution(mesh):
    placed = (
        P("gx", "gy", "gz"),
        P(None, "gx", "gy", "gz"),
        P("gx", "gy", "gz"),
        P("gx", "gy", "gz"),
        P(None, "gx", "gy", "gz"),
        P(("gx", "gy", "gz"), None),
    )
    return jax.shard_map(
        shards,
        mesh=mesh,
        in_specs=placed,
        out_specs=(P("gx", "gy", "gz"), P("gx", "gy", "gz")),
        check_vma=False,
    )
```

```python
import functools

import jax
import jax.numpy as jnp
from jax import lax
from jax.experimental import pallas as pl
from jax.experimental.pallas import tpu as pltpu
from jax.sharding import PartitionSpec as P

MESH_ID = pl.DeviceIdType.MESH

SWEEPS = 4
ITERS = 2


RELAX = 2.0 / 3.0


def padded(value, sides, width):
    for axis, dim in sides:
        count, length = (lax.axis_size(axis), value.shape[dim])
        up = [(i, (i + 1) % count) for i in range(count - 1)]
        down = [(j, i) for i, j in up]
        last = lax.slice_in_dim(value, length - width, length, axis=dim)
        leading = lax.slice_in_dim(value, 0, width, axis=dim)
        before = lax.ppermute(last, axis, up)
        after = lax.ppermute(leading, axis, down)
        value = jnp.concatenate([before, value, after], axis=dim)
    return value


def pad_cond(cond):
    return jnp.pad(cond, ((0, 0), (1, 1), (1, 1), (1, 1)))


def stencil(padded_free, padded_cond, field, storage, free):
    middle = padded_free[1:-1, 1:-1, 1:-1]
    total = storage * middle
    total = (
        total
        + padded_cond[0, 1:-1, 1:-1, 1:-1] * (middle - padded_free[2:, 1:-1, 1:-1])
        + padded_cond[0, :-2, 1:-1, 1:-1] * (middle - padded_free[:-2, 1:-1, 1:-1])
    )
    total = (
        total
        + padded_cond[1, 1:-1, 1:-1, 1:-1] * (middle - padded_free[1:-1, 2:, 1:-1])
        + padded_cond[1, 1:-1, :-2, 1:-1] * (middle - padded_free[1:-1, :-2, 1:-1])
    )
    total = (
        total
        + padded_cond[2, 1:-1, 1:-1, 1:-1] * (middle - padded_free[1:-1, 1:-1, 2:])
        + padded_cond[2, 1:-1, 1:-1, :-2] * (middle - padded_free[1:-1, 1:-1, :-2])
    )
    return free * total + (1.0 - free) * field


def diagonal_of(padded_cond, storage, free):
    total = storage + padded_cond[0, 1:-1, 1:-1, 1:-1] + padded_cond[0, :-2, 1:-1, 1:-1]
    total = total + padded_cond[1, 1:-1, 1:-1, 1:-1] + padded_cond[1, 1:-1, :-2, 1:-1]
    total = total + padded_cond[2, 1:-1, 1:-1, 1:-1] + padded_cond[2, 1:-1, 1:-1, :-2]
    return free * total + (1.0 - free)


def jacobi(rhs_box, padded_cond, diagonal, storage_box, free_box):
    guess = jnp.zeros_like(rhs_box)
    for sweep in range(SWEEPS):
        image = stencil(jnp.pad(free_box * guess, 1), padded_cond, guess, storage_box, free_box)
        guess = guess + RELAX * (rhs_box - image) / diagonal
    return guess


def project(basis, field):
    return jnp.sum(basis * field[None], axis=(1, 2, 3))


def expand(basis, weights, field):
    return jnp.sum(weights[:, None, None, None] * basis, axis=0)


LANES = 128


def faces(field):
    pieces = []
    for dim, axis in enumerate(("gx", "gy", "gz")):
        count, length = (lax.axis_size(axis), field.shape[dim])
        up = [(i, i + 1) for i in range(count - 1)]
        down = [(j, i) for i, j in up]
        before = lax.ppermute(lax.slice_in_dim(field, length - 1, length, axis=dim), axis, up)
        after = lax.ppermute(lax.slice_in_dim(field, 0, 1, axis=dim), axis, down)
        pieces.append((before, after))
    result = field
    for dim in range(3):
        before, after = pieces[dim]
        widths = [(1, 1) if d < dim else (0, 0) for d in range(3)]
        result = jnp.concatenate([jnp.pad(before, widths), result, jnp.pad(after, widths)], axis=dim)
    return result


def residual_rim(field):
    return padded(field, (("gx", 0), ("gy", 1), ("gz", 2)), 2)


def gather_kernel(sizes, row_ref, held, local_sem, send1, recv1, send2, recv2):
    nx, ny, nz = sizes
    plane = ny * nz
    a = lax.axis_index("gx")
    b = lax.axis_index("gy")
    c = lax.axis_index("gz")
    me = (a * ny + b) * nz + c

    def in_plane(k):
        return (a, lax.rem(b + k // nz, ny), lax.rem(c + k % nz, nz))

    def along_x(k):
        return (lax.rem(a + k, nx), b, c)

    peers = [in_plane(k) for k in range(1, plane)] + [along_x(k) for k in range(1, nx)]
    barrier = pltpu.get_barrier_semaphore()
    for peer in peers:
        pl.semaphore_signal(barrier, inc=1, device_id=peer, device_id_type=MESH_ID)
    pl.semaphore_wait(barrier, len(peers))

    own = pltpu.make_async_copy(row_ref, held.at[pl.ds(me, 1)], local_sem.at[0])
    own.start()
    sent = []

    def stage(src_of, first_of, count, size, toward, send, recv):
        for k in range(1, size):
            copy = pltpu.make_async_remote_copy(
                src_ref=src_of(0),
                dst_ref=held.at[pl.ds(first_of(0), count)],
                send_sem=send.at[k],
                recv_sem=recv.at[k],
                device_id=toward(k),
                device_id_type=MESH_ID,
            )
            copy.start()
            sent.append(copy)
        for k in range(1, size):
            pltpu.make_async_remote_copy(
                src_ref=src_of(k),
                dst_ref=held.at[pl.ds(first_of(k), count)],
                send_sem=send.at[k],
                recv_sem=recv.at[k],
                device_id=toward(size - k),
                device_id_type=MESH_ID,
            ).wait_recv()

    def p_first(k):
        return (a * ny + lax.rem(b + ny - k // nz, ny)) * nz + lax.rem(c + nz - k % nz, nz)

    stage(lambda k: row_ref, p_first, 1, plane, in_plane, send1, recv1)
    own.wait()
    x_first = lambda k: lax.rem(a + nx - k, nx) * plane
    stage(lambda k: held.at[pl.ds(x_first(k), plane)], x_first, plane, nx, along_x, send2, recv2)
    for copy in sent:
        copy.wait_send()


def gather_rows(row):
    sizes = (lax.axis_size("gx"), lax.axis_size("gy"), lax.axis_size("gz"))
    count = sizes[0] * sizes[1] * sizes[2]
    tile = row[:, None, :]
    rows = pl.pallas_call(
        functools.partial(gather_kernel, sizes),
        out_shape=jax.ShapeDtypeStruct((count, 1, LANES), jnp.float32),
        in_specs=[pl.BlockSpec(memory_space=pltpu.VMEM)],
        out_specs=pl.BlockSpec(memory_space=pltpu.VMEM),
        scratch_shapes=[
            pltpu.SemaphoreType.DMA((1,)),
            pltpu.SemaphoreType.DMA((sizes[1] * sizes[2],)),
            pltpu.SemaphoreType.DMA((sizes[1] * sizes[2],)),
            pltpu.SemaphoreType.DMA((sizes[0],)),
            pltpu.SemaphoreType.DMA((sizes[0],)),
        ],
        compiler_params=pltpu.CompilerParams(collective_id=0, has_side_effects=True),
    )(tile)
    return rows[:, 0, :]


def pack(coarse, scalars):
    vecs = coarse.shape[0]
    row = jnp.zeros((LANES,), jnp.float32)
    row = row.at[:vecs].set(coarse)
    if scalars:
        row = row.at[vecs:vecs + len(scalars)].set(jnp.stack(scalars))
    return row[None]


def unpack(rows, vecs, count):
    coarse = rows[:, :vecs].reshape(-1)
    sums = jnp.sum(rows[:, vecs:vecs + count], axis=0)
    return coarse, [sums[i] for i in range(count)]


def shards(right_side, conductance, storage, dirichlet, basis, coarse_inverse):
    vecs = basis.shape[0]
    sides = (("gx", 0), ("gy", 1), ("gz", 2))
    free = 1.0 - dirichlet.astype(jnp.float32)
    stacked = jnp.concatenate([conductance, storage[None], free[None], right_side[None]], axis=0)
    wide = padded(stacked, (("gz", 3), ("gx", 1), ("gy", 2)), 3)
    cond_wide = wide[:3]
    free_wide = wide[4]
    storage_wide = wide[3]
    cond_box = wide[:3, 1:-1, 1:-1, 1:-1]
    storage_box = wide[3, 1:-1, 1:-1, 1:-1]
    free_box = wide[4, 1:-1, 1:-1, 1:-1]
    rhs_box0 = wide[5, 1:-1, 1:-1, 1:-1]
    box_cond = pad_cond(cond_box)
    box_diag = diagonal_of(box_cond, storage_box, free_box)
    cond_face = wide[:3, 2:-2, 2:-2, 2:-2]
    free_face = wide[4, 2:-2, 2:-2, 2:-2]

    def schwarz(rhs_box):
        return jacobi(rhs_box, box_cond, box_diag, storage_box, free_box)[2:-2, 2:-2, 2:-2]

    def precondition(rhs_box, residual, coarse_all):
        weights = jnp.sum(coarse_inverse * coarse_all[None], axis=1)
        return schwarz(rhs_box) + expand(basis, weights, residual)

    residual0 = right_side
    coarse0 = project(basis, residual0)
    coarse0_all, _ = unpack(gather_rows(pack(coarse0, [])), vecs, 0)
    z0 = precondition(rhs_box0, residual0, coarse0_all)
    near0 = padded(z0, (("gz", 2), ("gx", 0), ("gy", 1)), 3)
    inner = (slice(1, -1),) * 3
    image0_box = stencil(free_wide * near0, cond_wide, near0[inner], storage_wide[inner], free_wide[inner])
    image0 = image0_box[2:-2, 2:-2, 2:-2]
    coarse_img = project(basis, image0)
    rows = gather_rows(pack(coarse_img, [jnp.sum(residual0 * z0), jnp.sum(z0 * image0)]))
    coarse_img_all, (rz0, curve0) = unpack(rows, vecs, 2)
    alpha0 = rz0 / curve0
    solution1 = alpha0 * z0
    rhs_box1 = rhs_box0 - alpha0 * image0_box
    residual1 = rhs_box1[2:-2, 2:-2, 2:-2]
    coarse1_all = coarse0_all - alpha0 * coarse_img_all
    z1 = precondition(rhs_box1, residual1, coarse1_all)
    near1 = faces(z1)
    image_z1 = stencil(free_face * near1, cond_face, z1, storage, free)
    local = [
        jnp.sum(residual1 * z1),
        jnp.sum(z1 * image_z1),
        jnp.sum(z1 * image0),
        jnp.sum(z0 * image_z1),
    ]
    _, (rz1, zz, cross_a, cross_b) = unpack(gather_rows(pack(jnp.zeros((0,), jnp.float32), local)), 0, 4)
    beta = rz1 / rz0
    direction1 = z1 + beta * z0
    image1 = image_z1 + beta * image0
    curve1 = zz + beta * (cross_a + cross_b) + beta * beta * curve0
    alpha1 = rz1 / curve1
    solution2 = solution1 + alpha1 * direction1
    residual2 = residual1 - alpha1 * image1
    return (solution2, residual2)


def solution(mesh):
    placed = (
        P("gx", "gy", "gz"),
        P(None, "gx", "gy", "gz"),
        P("gx", "gy", "gz"),
        P("gx", "gy", "gz"),
        P(None, "gx", "gy", "gz"),
        P(("gx", "gy", "gz"), None),
    )
    return jax.shard_map(
        shards,
        mesh=mesh,
        in_specs=placed,
        out_specs=(P("gx", "gy", "gz"), P("gx", "gy", "gz")),
        check_vma=False,
    )
```

```python
import functools

import jax
import jax.numpy as jnp
from jax import lax
from jax.experimental import pallas as pl
from jax.experimental.pallas import tpu as pltpu
from jax.sharding import PartitionSpec as P

MESH_ID = pl.DeviceIdType.MESH

SWEEPS = 4
ITERS = 2


RELAX = 2.0 / 3.0


def padded(value, sides, width):
    for axis, dim in sides:
        count, length = (lax.axis_size(axis), value.shape[dim])
        up = [(i, (i + 1) % count) for i in range(count - 1)]
        down = [(j, i) for i, j in up]
        last = lax.slice_in_dim(value, length - width, length, axis=dim)
        leading = lax.slice_in_dim(value, 0, width, axis=dim)
        before = lax.ppermute(last, axis, up)
        after = lax.ppermute(leading, axis, down)
        value = jnp.concatenate([before, value, after], axis=dim)
    return value


def pad_cond(cond):
    return jnp.pad(cond, ((0, 0), (1, 1), (1, 1), (1, 1)))


def stencil(padded_free, padded_cond, field, storage, free):
    middle = padded_free[1:-1, 1:-1, 1:-1]
    total = storage * middle
    total = (
        total
        + padded_cond[0, 1:-1, 1:-1, 1:-1] * (middle - padded_free[2:, 1:-1, 1:-1])
        + padded_cond[0, :-2, 1:-1, 1:-1] * (middle - padded_free[:-2, 1:-1, 1:-1])
    )
    total = (
        total
        + padded_cond[1, 1:-1, 1:-1, 1:-1] * (middle - padded_free[1:-1, 2:, 1:-1])
        + padded_cond[1, 1:-1, :-2, 1:-1] * (middle - padded_free[1:-1, :-2, 1:-1])
    )
    total = (
        total
        + padded_cond[2, 1:-1, 1:-1, 1:-1] * (middle - padded_free[1:-1, 1:-1, 2:])
        + padded_cond[2, 1:-1, 1:-1, :-2] * (middle - padded_free[1:-1, 1:-1, :-2])
    )
    return free * total + (1.0 - free) * field


def diagonal_of(padded_cond, storage, free):
    total = storage + padded_cond[0, 1:-1, 1:-1, 1:-1] + padded_cond[0, :-2, 1:-1, 1:-1]
    total = total + padded_cond[1, 1:-1, 1:-1, 1:-1] + padded_cond[1, 1:-1, :-2, 1:-1]
    total = total + padded_cond[2, 1:-1, 1:-1, 1:-1] + padded_cond[2, 1:-1, 1:-1, :-2]
    return free * total + (1.0 - free)


def jacobi(rhs_box, padded_cond, diagonal, storage_box, free_box):
    guess = RELAX * rhs_box / diagonal
    for sweep in range(1, SWEEPS):
        image = stencil(jnp.pad(free_box * guess, 1), padded_cond, guess, storage_box, free_box)
        guess = guess + RELAX * (rhs_box - image) / diagonal
    return guess


def project(basis, field):
    return jnp.sum(basis * field[None], axis=(1, 2, 3))


def expand(basis, weights, field):
    return jnp.sum(weights[:, None, None, None] * basis, axis=0)


LANES = 128


def faces(field):
    pieces = []
    for dim, axis in enumerate(("gx", "gy", "gz")):
        count, length = (lax.axis_size(axis), field.shape[dim])
        up = [(i, i + 1) for i in range(count - 1)]
        down = [(j, i) for i, j in up]
        before = lax.ppermute(lax.slice_in_dim(field, length - 1, length, axis=dim), axis, up)
        after = lax.ppermute(lax.slice_in_dim(field, 0, 1, axis=dim), axis, down)
        pieces.append((before, after))
    result = field
    for dim in range(3):
        before, after = pieces[dim]
        widths = [(1, 1) if d < dim else (0, 0) for d in range(3)]
        result = jnp.concatenate([jnp.pad(before, widths), result, jnp.pad(after, widths)], axis=dim)
    return result


def residual_rim(field):
    return padded(field, (("gx", 0), ("gy", 1), ("gz", 2)), 2)


def gather_kernel(sizes, row_ref, held, local_sem, send1, recv1, send2, recv2):
    nx, ny, nz = sizes
    plane = ny * nz
    a = lax.axis_index("gx")
    b = lax.axis_index("gy")
    c = lax.axis_index("gz")
    me = (a * ny + b) * nz + c

    def in_plane(k):
        return (a, lax.rem(b + k // nz, ny), lax.rem(c + k % nz, nz))

    def along_x(k):
        return (lax.rem(a + k, nx), b, c)

    peers = [in_plane(k) for k in range(1, plane)] + [along_x(k) for k in range(1, nx)]
    barrier = pltpu.get_barrier_semaphore()
    for peer in peers:
        pl.semaphore_signal(barrier, inc=1, device_id=peer, device_id_type=MESH_ID)
    pl.semaphore_wait(barrier, len(peers))

    own = pltpu.make_async_copy(row_ref, held.at[pl.ds(me, 1)], local_sem.at[0])
    own.start()
    sent = []

    def stage(src_of, first_of, count, size, toward, send, recv):
        for k in range(1, size):
            copy = pltpu.make_async_remote_copy(
                src_ref=src_of(0),
                dst_ref=held.at[pl.ds(first_of(0), count)],
                send_sem=send.at[k],
                recv_sem=recv.at[k],
                device_id=toward(k),
                device_id_type=MESH_ID,
            )
            copy.start()
            sent.append(copy)
        for k in range(1, size):
            pltpu.make_async_remote_copy(
                src_ref=src_of(k),
                dst_ref=held.at[pl.ds(first_of(k), count)],
                send_sem=send.at[k],
                recv_sem=recv.at[k],
                device_id=toward(size - k),
                device_id_type=MESH_ID,
            ).wait_recv()

    def p_first(k):
        return (a * ny + lax.rem(b + ny - k // nz, ny)) * nz + lax.rem(c + nz - k % nz, nz)

    stage(lambda k: row_ref, p_first, 1, plane, in_plane, send1, recv1)
    own.wait()
    x_first = lambda k: lax.rem(a + nx - k, nx) * plane
    stage(lambda k: held.at[pl.ds(x_first(k), plane)], x_first, plane, nx, along_x, send2, recv2)
    for copy in sent:
        copy.wait_send()


def gather_rows(row):
    sizes = (lax.axis_size("gx"), lax.axis_size("gy"), lax.axis_size("gz"))
    count = sizes[0] * sizes[1] * sizes[2]
    tile = row[:, None, :]
    rows = pl.pallas_call(
        functools.partial(gather_kernel, sizes),
        out_shape=jax.ShapeDtypeStruct((count, 1, LANES), jnp.float32),
        in_specs=[pl.BlockSpec(memory_space=pltpu.VMEM)],
        out_specs=pl.BlockSpec(memory_space=pltpu.VMEM),
        scratch_shapes=[
            pltpu.SemaphoreType.DMA((1,)),
            pltpu.SemaphoreType.DMA((sizes[1] * sizes[2],)),
            pltpu.SemaphoreType.DMA((sizes[1] * sizes[2],)),
            pltpu.SemaphoreType.DMA((sizes[0],)),
            pltpu.SemaphoreType.DMA((sizes[0],)),
        ],
        compiler_params=pltpu.CompilerParams(collective_id=0, has_side_effects=True),
    )(tile)
    return rows[:, 0, :]


def pack(coarse, scalars):
    vecs = coarse.shape[0]
    row = jnp.zeros((LANES,), jnp.float32)
    row = row.at[:vecs].set(coarse)
    if scalars:
        row = row.at[vecs:vecs + len(scalars)].set(jnp.stack(scalars))
    return row[None]


def unpack(rows, vecs, count):
    coarse = rows[:, :vecs].reshape(-1)
    sums = jnp.sum(rows[:, vecs:vecs + count], axis=0)
    return coarse, [sums[i] for i in range(count)]


def shards(right_side, conductance, storage, dirichlet, basis, coarse_inverse):
    vecs = basis.shape[0]
    sides = (("gx", 0), ("gy", 1), ("gz", 2))
    free = 1.0 - dirichlet.astype(jnp.float32)
    stacked = jnp.concatenate([conductance, storage[None], free[None], right_side[None]], axis=0)
    wide = padded(stacked, (("gz", 3), ("gx", 1), ("gy", 2)), 3)
    cond_wide = wide[:3]
    free_wide = wide[4]
    storage_wide = wide[3]
    cond_box = wide[:3, 1:-1, 1:-1, 1:-1]
    storage_box = wide[3, 1:-1, 1:-1, 1:-1]
    free_box = wide[4, 1:-1, 1:-1, 1:-1]
    rhs_box0 = wide[5, 1:-1, 1:-1, 1:-1]
    box_cond = pad_cond(cond_box)
    box_diag = diagonal_of(box_cond, storage_box, free_box)
    cond_face = wide[:3, 2:-2, 2:-2, 2:-2]
    free_face = wide[4, 2:-2, 2:-2, 2:-2]

    def schwarz(rhs_box):
        return jacobi(rhs_box, box_cond, box_diag, storage_box, free_box)[2:-2, 2:-2, 2:-2]

    def precondition(rhs_box, residual, coarse_all):
        weights = jnp.dot(coarse_inverse, coarse_all, precision=lax.Precision.HIGHEST)
        return schwarz(rhs_box) + expand(basis, weights, residual)

    residual0 = right_side
    coarse0 = project(basis, residual0)
    coarse0_all, _ = unpack(gather_rows(pack(coarse0, [])), vecs, 0)
    z0 = precondition(rhs_box0, residual0, coarse0_all)
    near0 = padded(z0, (("gz", 2), ("gx", 0), ("gy", 1)), 3)
    inner = (slice(1, -1),) * 3
    image0_box = stencil(free_wide * near0, cond_wide, near0[inner], storage_wide[inner], free_wide[inner])
    image0 = image0_box[2:-2, 2:-2, 2:-2]
    coarse_img = project(basis, image0)
    rows = gather_rows(pack(coarse_img, [jnp.sum(residual0 * z0), jnp.sum(z0 * image0)]))
    coarse_img_all, (rz0, curve0) = unpack(rows, vecs, 2)
    alpha0 = rz0 / curve0
    solution1 = alpha0 * z0
    rhs_box1 = rhs_box0 - alpha0 * image0_box
    residual1 = rhs_box1[2:-2, 2:-2, 2:-2]
    coarse1_all = coarse0_all - alpha0 * coarse_img_all
    z1 = precondition(rhs_box1, residual1, coarse1_all)
    near1 = faces(z1)
    image_z1 = stencil(free_face * near1, cond_face, z1, storage, free)
    local = [
        jnp.sum(residual1 * z1),
        jnp.sum(z1 * image_z1),
        jnp.sum(z1 * image0),
        jnp.sum(z0 * image_z1),
    ]
    _, (rz1, zz, cross_a, cross_b) = unpack(gather_rows(pack(jnp.zeros((0,), jnp.float32), local)), 0, 4)
    beta = rz1 / rz0
    direction1 = z1 + beta * z0
    image1 = image_z1 + beta * image0
    curve1 = zz + beta * (cross_a + cross_b) + beta * beta * curve0
    alpha1 = rz1 / curve1
    solution2 = solution1 + alpha1 * direction1
    residual2 = residual1 - alpha1 * image1
    return (solution2, residual2)


def solution(mesh):
    placed = (
        P("gx", "gy", "gz"),
        P(None, "gx", "gy", "gz"),
        P("gx", "gy", "gz"),
        P("gx", "gy", "gz"),
        P(None, "gx", "gy", "gz"),
        P(("gx", "gy", "gz"), None),
    )
    return jax.shard_map(
        shards,
        mesh=mesh,
        in_specs=placed,
        out_specs=(P("gx", "gy", "gz"), P("gx", "gy", "gz")),
        check_vma=False,
    )
```

```python
import functools

import jax
import jax.numpy as jnp
from jax import lax
from jax.experimental import pallas as pl
from jax.experimental.pallas import tpu as pltpu
from jax.sharding import PartitionSpec as P

MESH_ID = pl.DeviceIdType.MESH

SWEEPS = 4
ITERS = 2


RELAX = 2.0 / 3.0


def padded(value, sides, width):
    for axis, dim in sides:
        count, length = (lax.axis_size(axis), value.shape[dim])
        up = [(i, (i + 1) % count) for i in range(count - 1)]
        down = [(j, i) for i, j in up]
        last = lax.slice_in_dim(value, length - width, length, axis=dim)
        leading = lax.slice_in_dim(value, 0, width, axis=dim)
        before = lax.ppermute(last, axis, up)
        after = lax.ppermute(leading, axis, down)
        value = jnp.concatenate([before, value, after], axis=dim)
    return value


def pad_cond(cond):
    return jnp.pad(cond, ((0, 0), (1, 1), (1, 1), (1, 1)))


def stencil(padded_free, padded_cond, field, storage, free):
    middle = padded_free[1:-1, 1:-1, 1:-1]
    total = storage * middle
    total = (
        total
        + padded_cond[0, 1:-1, 1:-1, 1:-1] * (middle - padded_free[2:, 1:-1, 1:-1])
        + padded_cond[0, :-2, 1:-1, 1:-1] * (middle - padded_free[:-2, 1:-1, 1:-1])
    )
    total = (
        total
        + padded_cond[1, 1:-1, 1:-1, 1:-1] * (middle - padded_free[1:-1, 2:, 1:-1])
        + padded_cond[1, 1:-1, :-2, 1:-1] * (middle - padded_free[1:-1, :-2, 1:-1])
    )
    total = (
        total
        + padded_cond[2, 1:-1, 1:-1, 1:-1] * (middle - padded_free[1:-1, 1:-1, 2:])
        + padded_cond[2, 1:-1, 1:-1, :-2] * (middle - padded_free[1:-1, 1:-1, :-2])
    )
    return free * total + (1.0 - free) * field


def diagonal_of(padded_cond, storage, free):
    total = storage + padded_cond[0, 1:-1, 1:-1, 1:-1] + padded_cond[0, :-2, 1:-1, 1:-1]
    total = total + padded_cond[1, 1:-1, 1:-1, 1:-1] + padded_cond[1, 1:-1, :-2, 1:-1]
    total = total + padded_cond[2, 1:-1, 1:-1, 1:-1] + padded_cond[2, 1:-1, 1:-1, :-2]
    return free * total + (1.0 - free)


def jacobi(rhs_box, padded_cond, diagonal, storage_box, free_box):
    guess = jnp.zeros_like(rhs_box)
    for sweep in range(SWEEPS):
        image = stencil(jnp.pad(free_box * guess, 1), padded_cond, guess, storage_box, free_box)
        guess = guess + RELAX * (rhs_box - image) / diagonal
    return guess


def project(basis, field):
    return jnp.sum(basis * field[None], axis=(1, 2, 3))


def expand(basis, weights, field):
    return jnp.sum(weights[:, None, None, None] * basis, axis=0)


LANES = 128


def faces(field):
    pieces = []
    for dim, axis in enumerate(("gx", "gy", "gz")):
        count, length = (lax.axis_size(axis), field.shape[dim])
        up = [(i, i + 1) for i in range(count - 1)]
        down = [(j, i) for i, j in up]
        before = lax.ppermute(lax.slice_in_dim(field, length - 1, length, axis=dim), axis, up)
        after = lax.ppermute(lax.slice_in_dim(field, 0, 1, axis=dim), axis, down)
        pieces.append((before, after))
    result = field
    for dim in range(3):
        before, after = pieces[dim]
        widths = [(1, 1) if d < dim else (0, 0) for d in range(3)]
        result = jnp.concatenate([jnp.pad(before, widths), result, jnp.pad(after, widths)], axis=dim)
    return result


def residual_rim(field):
    return padded(field, (("gx", 0), ("gy", 1), ("gz", 2)), 2)


def gather_kernel(sizes, row_ref, held, local_sem, send1, recv1, send2, recv2):
    nx, ny, nz = sizes
    plane = ny * nz
    a = lax.axis_index("gx")
    b = lax.axis_index("gy")
    c = lax.axis_index("gz")
    me = (a * ny + b) * nz + c

    def in_plane(k):
        return (a, lax.rem(b + k // nz, ny), lax.rem(c + k % nz, nz))

    def along_x(k):
        return (lax.rem(a + k, nx), b, c)

    peers = [in_plane(k) for k in range(1, plane)] + [along_x(k) for k in range(1, nx)]
    barrier = pltpu.get_barrier_semaphore()
    for peer in peers:
        pl.semaphore_signal(barrier, inc=1, device_id=peer, device_id_type=MESH_ID)
    pl.semaphore_wait(barrier, len(peers))

    own = pltpu.make_async_copy(row_ref, held.at[pl.ds(me, 1)], local_sem.at[0])
    own.start()
    sent = []

    def stage(src_of, first_of, count, size, toward, send, recv):
        for k in range(1, size):
            copy = pltpu.make_async_remote_copy(
                src_ref=src_of(0),
                dst_ref=held.at[pl.ds(first_of(0), count)],
                send_sem=send.at[k],
                recv_sem=recv.at[k],
                device_id=toward(k),
                device_id_type=MESH_ID,
            )
            copy.start()
            sent.append(copy)
        for k in range(1, size):
            pltpu.make_async_remote_copy(
                src_ref=src_of(k),
                dst_ref=held.at[pl.ds(first_of(k), count)],
                send_sem=send.at[k],
                recv_sem=recv.at[k],
                device_id=toward(size - k),
                device_id_type=MESH_ID,
            ).wait_recv()

    def p_first(k):
        return (a * ny + lax.rem(b + ny - k // nz, ny)) * nz + lax.rem(c + nz - k % nz, nz)

    stage(lambda k: row_ref, p_first, 1, plane, in_plane, send1, recv1)
    own.wait()
    x_first = lambda k: lax.rem(a + nx - k, nx) * plane
    stage(lambda k: held.at[pl.ds(x_first(k), plane)], x_first, plane, nx, along_x, send2, recv2)
    for copy in sent:
        copy.wait_send()


def gather_rows(row):
    sizes = (lax.axis_size("gx"), lax.axis_size("gy"), lax.axis_size("gz"))
    count = sizes[0] * sizes[1] * sizes[2]
    tile = row[:, None, :]
    rows = pl.pallas_call(
        functools.partial(gather_kernel, sizes),
        out_shape=jax.ShapeDtypeStruct((count, 1, LANES), jnp.float32),
        in_specs=[pl.BlockSpec(memory_space=pltpu.VMEM)],
        out_specs=pl.BlockSpec(memory_space=pltpu.VMEM),
        scratch_shapes=[
            pltpu.SemaphoreType.DMA((1,)),
            pltpu.SemaphoreType.DMA((sizes[1] * sizes[2],)),
            pltpu.SemaphoreType.DMA((sizes[1] * sizes[2],)),
            pltpu.SemaphoreType.DMA((sizes[0],)),
            pltpu.SemaphoreType.DMA((sizes[0],)),
        ],
        compiler_params=pltpu.CompilerParams(collective_id=0, has_side_effects=True),
    )(tile)
    return rows[:, 0, :]


def pack(coarse, scalars):
    vecs = coarse.shape[0]
    row = jnp.zeros((LANES,), jnp.float32)
    row = row.at[:vecs].set(coarse)
    if scalars:
        row = row.at[vecs:vecs + len(scalars)].set(jnp.stack(scalars))
    return row[None]


def unpack(rows, vecs, count):
    coarse = rows[:, :vecs].reshape(-1)
    sums = jnp.sum(rows[:, vecs:vecs + count], axis=0)
    return coarse, [sums[i] for i in range(count)]


def shards(right_side, conductance, storage, dirichlet, basis, coarse_inverse):
    vecs = basis.shape[0]
    sides = (("gx", 0), ("gy", 1), ("gz", 2))
    free = 1.0 - dirichlet.astype(jnp.float32)
    signed = jnp.where(dirichlet == 0, storage, -storage)
    stacked = jnp.concatenate([conductance, signed[None], right_side[None]], axis=0)
    wide = padded(stacked, (("gz", 3), ("gx", 1), ("gy", 2)), 3)
    cond_wide = wide[:3]
    free_wide = (wide[3] > 0).astype(jnp.float32)
    storage_wide = jnp.abs(wide[3])
    cond_box = wide[:3, 1:-1, 1:-1, 1:-1]
    storage_box = storage_wide[1:-1, 1:-1, 1:-1]
    free_box = free_wide[1:-1, 1:-1, 1:-1]
    rhs_box0 = wide[4, 1:-1, 1:-1, 1:-1]
    box_cond = pad_cond(cond_box)
    box_diag = diagonal_of(box_cond, storage_box, free_box)
    cond_face = wide[:3, 2:-2, 2:-2, 2:-2]
    free_face = free_wide[2:-2, 2:-2, 2:-2]

    def schwarz(rhs_box):
        return jacobi(rhs_box, box_cond, box_diag, storage_box, free_box)[2:-2, 2:-2, 2:-2]

    def precondition(rhs_box, residual, coarse_all):
        weights = jnp.dot(coarse_inverse, coarse_all, precision=lax.Precision.HIGHEST)
        return schwarz(rhs_box) + expand(basis, weights, residual)

    residual0 = right_side
    coarse0 = project(basis, residual0)
    coarse0_all, _ = unpack(gather_rows(pack(coarse0, [])), vecs, 0)
    z0 = precondition(rhs_box0, residual0, coarse0_all)
    near0 = padded(z0, (("gz", 2), ("gx", 0), ("gy", 1)), 3)
    inner = (slice(1, -1),) * 3
    image0_box = stencil(free_wide * near0, cond_wide, near0[inner], storage_wide[inner], free_wide[inner])
    image0 = image0_box[2:-2, 2:-2, 2:-2]
    coarse_img = project(basis, image0)
    rows = gather_rows(pack(coarse_img, [jnp.sum(residual0 * z0), jnp.sum(z0 * image0)]))
    coarse_img_all, (rz0, curve0) = unpack(rows, vecs, 2)
    alpha0 = rz0 / curve0
    solution1 = alpha0 * z0
    rhs_box1 = rhs_box0 - alpha0 * image0_box
    residual1 = rhs_box1[2:-2, 2:-2, 2:-2]
    coarse1_all = coarse0_all - alpha0 * coarse_img_all
    z1 = precondition(rhs_box1, residual1, coarse1_all)
    near1 = faces(z1)
    image_z1 = stencil(free_face * near1, cond_face, z1, storage, free)
    local = [
        jnp.sum(residual1 * z1),
        jnp.sum(z1 * image_z1),
        jnp.sum(z1 * image0),
        jnp.sum(z0 * image_z1),
    ]
    _, (rz1, zz, cross_a, cross_b) = unpack(gather_rows(pack(jnp.zeros((0,), jnp.float32), local)), 0, 4)
    beta = rz1 / rz0
    direction1 = z1 + beta * z0
    image1 = image_z1 + beta * image0
    curve1 = zz + beta * (cross_a + cross_b) + beta * beta * curve0
    alpha1 = rz1 / curve1
    solution2 = solution1 + alpha1 * direction1
    residual2 = residual1 - alpha1 * image1
    return (solution2, residual2)


def solution(mesh):
    placed = (
        P("gx", "gy", "gz"),
        P(None, "gx", "gy", "gz"),
        P("gx", "gy", "gz"),
        P("gx", "gy", "gz"),
        P(None, "gx", "gy", "gz"),
        P(("gx", "gy", "gz"), None),
    )
    return jax.shard_map(
        shards,
        mesh=mesh,
        in_specs=placed,
        out_specs=(P("gx", "gy", "gz"), P("gx", "gy", "gz")),
        check_vma=False,
    )
```
